128 devices in a mesh: visit: 4 (over z), sky: 32 (over y, x, core).
Axes of the slice: x: 4, y: 4, z: 4, core: 2. Of those that a mesh axis runs over, the one named last changes fastest.
Arguments:
- cutouts: float32 [256, 512, 512], P(('visit', 'sky')), may hold values from -6 to 6
- vert_taps: float32 [256, 16, 21], P(('visit', 'sky')), may hold values from -1.25 to 1.25
- horiz_taps: float32 [256, 16, 21], P(('visit', 'sky')), may hold values from -1.25 to 1.25
- field_coeffs: float32 [256, 4, 16], P(('visit', 'sky')), may hold values from -1.5 to 1.5
- exposure_weight: float32 [256], P(('visit', 'sky')), may hold values from 0.2 to 2
- dest_owner: int32 [256, 16, 1], P(('visit', 'sky')), may hold values from 0 to 127; in each aligned block of 32 rows (0 to 31, 32 to 63, ..., all dimensions but the last counted through in order) at most 2 rows name the same one
- dest_column: int32 [256, 16], P(('visit', 'sky')), may hold values from 0 to 3
- shift_index: int32 [256, 16], P(('visit', 'sky')), may hold values from 0 to 15
- threshold_level: int32 [128, 4], replicated, may hold values from 1 to 4
Outputs:
- sky_template: float32 [16384, 512], P(('visit', 'sky'))
- difference: float32 [256, 512, 512], P(('visit', 'sky'))
The draws below stay inside these ranges and needn't reach their ends.
Inputs may be any that keep to these rules, and one draw needn't show every extreme that they name: `dest_owner`: among the blocks of the cutouts of one device no owner is named more than 2 times, a bound that some block reaches.
All inputs are finite; a program needn't handle non-finite values.
Results may differ from the reference program's by a relative error of at most 0.0084.
Values may be sent and summed in bfloat16 or wider, within the bound.
No kernel may reach another device: no remote copies, remote signals or barrier semaphores. Data moves between devices by JAX's collectives and lax.ppermute only.
A program may use at most 64 MiB of HBM per device.

```python
import math
import jax
import jax.numpy as jnp
import numpy as np
from jax import lax

CUT = 512
BLOCK = 128
KERNELS = 16
TAPS = 21
PW = 4
SHIFTS = 16
SWEEPS = 2
EXP_DEV = 2
BLOCKS = 16
EXPOSURES = 256
OWNERS = 128
CAP = 2
SKY_ROWS = 16384
SKY_COLS = 512
DEVICES = 128


def set_ends(array, key, smallest, largest):
    extent = array.shape
    place = [jax.random.randint(jax.random.fold_in(key, axis), (), 0, extent[axis]) for axis in range(len(extent))]
    array = array.at[tuple(place)].set(smallest)
    longest = extent.index(max(extent))
    place[longest] = (place[longest] + 1) % extent[longest]
    return array.at[tuple(place)].set(largest)


def level_of(key, shape, split, smallest, high):
    def one(dim, shards_of):
        draws = jax.random.uniform(jax.random.fold_in(jax.random.fold_in(key, 6), dim), (shards_of,), jnp.float32, smallest / len(split), high / len(split))
        return jnp.repeat(jnp.exp(draws), shape[dim] // shards_of).reshape((-1,) + (1,) * (len(shape) - dim - 1))

    gain = one(*split[0])
    for cut in split[1:]:
        gain = gain * one(*cut)
    return gain


def deal_out(own_key, own, number, rows, count, top, most, lean):
    sequence = jax.random.permutation(own_key, count)
    heavy_load, common = portions_of(count, rows * top, most, lean, True), portions_of(count, rows * top, most, lean, False)
    places = jnp.arange(count)

    def named(sizes, rotation):
        used = int((sizes > 0).sum())
        fixed = max(1, used // 4)
        moved = fixed + (places - fixed + rotation * (used - fixed)) % max(1, count - fixed)
        return jnp.zeros((count,), jnp.int32).at[sequence[jnp.where(places < fixed, places, moved)]].set(jnp.asarray(sizes, jnp.int32))

    sizes = jnp.where(number % 4 == 0, named(heavy_load, number // 4), named(common, number - number // 4 - 1))
    mixed = jax.random.permutation(jax.random.fold_in(own, 3), count)
    source_of, receiver = mixed[0:count // 2 * 2:2], mixed[1:count // 2 * 2:2]
    slack = jnp.minimum(sizes[source_of] - 1, most - sizes[receiver]) // 2
    slack = jnp.where((source_of == sequence[0]) | (receiver == sequence[0]) | (sizes[receiver] == 0), 0, jnp.maximum(slack, 0))
    moved = jax.random.randint(jax.random.fold_in(own, 4), (count // 2,), 0, 1 << 20) % (slack + 1)
    sizes = sizes.at[source_of].add(-moved).at[receiver].add(moved)
    items = jnp.searchsorted(jnp.cumsum(sizes), jnp.arange(rows * top), side="right").astype(jnp.int32)
    listing = items.reshape(top, rows).T
    listing = listing[jax.random.permutation(jax.random.fold_in(own, 1), rows)]
    rotation = jax.random.randint(jax.random.fold_in(own, 2), (rows, 1), 0, top)
    return jnp.take_along_axis(listing, (jnp.arange(top)[None, :] + rotation) % top, axis=1)


def portions_of(count, total, bound, slope, full):
    weights = [(1 << 20) // math.isqrt(standing ** slope) + 1 for standing in range(1, count + 1)]
    largest = bound if full else min(bound, max(-(-total // count), total * weights[0] // sum(weights)))
    least = 1 if total - largest >= count - 1 else 0
    given, spare = [largest] + [least] * (count - 1), total - largest - least * (count - 1)
    while spare > 0:
        free = [i for i in range(1, count) if given[i] < largest] or [i for i in range(1, count) if given[i] < bound]
        pool, left = sum([weights[i] for i in free]), spare
        for i in free:
            more = min(bound - given[i], max(1, left * weights[i] // pool), spare)
            given[i] = given[i] + more
            spare = spare - more
    return np.array(given)


def centred(rng, shape, width, reach, pieces=(), held_as=jnp.bfloat16):
    gain = level_of(rng, shape, pieces, -0.22, 0.18) if pieces else 1.0
    drawn = jax.random.normal(rng, shape, jnp.float32) * width * gain
    return jnp.minimum(jnp.maximum(drawn, -reach), reach).astype(held_as)


def setup_inputs(seed: int = 0) -> dict:
    key_of = jax.random.split(jax.random.key(seed), 10)
    cutouts = centred(key_of[0], (EXPOSURES, CUT, CUT), 1.0, 6.0, ((0, 128),), jnp.float32)
    vert_taps = centred(key_of[1], (EXPOSURES, KERNELS, TAPS), TAPS ** -0.5, 1.25, ((0, 128),), jnp.float32)
    horiz_taps = centred(key_of[2], (EXPOSURES, KERNELS, TAPS), TAPS ** -0.5, 1.25, ((0, 128),), jnp.float32)
    field_coeffs = centred(key_of[3], (EXPOSURES, 4, KERNELS), KERNELS ** -0.5, 1.5, ((0, 128),), jnp.float32)
    exposure_weight = jnp.clip(jnp.exp(math.log(2.0) - 2.3025851 * jax.random.uniform(key_of[4], (EXPOSURES,), jnp.float32) ** level_of(key_of[4], (EXPOSURES,), ((0, 128),), -0.2, 0.2)), 0.2, 2.0)
    dest_owner_keys = jax.random.split(jax.random.fold_in(key_of[5], 1), EXPOSURES * BLOCKS // (EXP_DEV * BLOCKS))
    dest_owner_turns = jax.random.permutation(jax.random.fold_in(key_of[5], 3), EXPOSURES * BLOCKS // (EXP_DEV * BLOCKS))
    dest_owner = jax.vmap(lambda own, number: deal_out(jax.random.fold_in(key_of[5], 2), own, number, EXP_DEV * BLOCKS, DEVICES, 1, CAP, 2))(dest_owner_keys, dest_owner_turns).reshape((EXPOSURES, BLOCKS, 1))
    dest_column = set_ends(jax.random.randint(key_of[6], (EXPOSURES, BLOCKS), 0, PW), jax.random.fold_in(key_of[6], 1), 0, PW - 1).astype(jnp.int32)
    shift_index = set_ends(jax.random.randint(key_of[7], (EXPOSURES, BLOCKS), 0, SHIFTS), jax.random.fold_in(key_of[7], 1), 0, SHIFTS - 1).astype(jnp.int32)
    threshold_level = set_ends(jax.random.randint(key_of[8], (OWNERS, PW), 1, 5), jax.random.fold_in(key_of[8], 1), 1, 4).astype(jnp.int32)
    return {"cutouts": cutouts, "vert_taps": vert_taps, "horiz_taps": horiz_taps, "field_coeffs": field_coeffs, "exposure_weight": exposure_weight, "dest_owner": dest_owner, "dest_column": dest_column, "shift_index": shift_index, "threshold_level": threshold_level}


highest = lax.Precision.HIGHEST
spline_taps = (0.0625, 0.25, 0.375, 0.25, 0.0625)
fine_tau = 0.04
coarse_tau = 0.02


def to_bf(values):
    return lax.optimization_barrier(values.astype(jnp.bfloat16)).astype(jnp.float32)


def band_matrix(kernel_taps, tile_width):
    margin = (kernel_taps.shape[1] - 1) // 2
    lag_table = jnp.arange(tile_width + 2 * margin)[:, None] - jnp.arange(tile_width)[None, :]
    one_hot = (lag_table[:, :, None] == jnp.arange(kernel_taps.shape[1])[None, None, :]).astype(jnp.float32)
    return jnp.einsum("kt,mnt->kmn", kernel_taps, one_hot, precision=highest)


def convolve_shift(cutout, vertical, horizontal, coeffs, shifts):
    margin = (vertical.shape[1] - 1) // 2
    tile_count = CUT // BLOCK
    window_rows = BLOCK + 2 * margin
    padded = jnp.pad(to_bf(cutout), margin)
    across = band_matrix(to_bf(horizontal), BLOCK)
    downward = band_matrix(to_bf(vertical), BLOCK).transpose(0, 2, 1)
    windows = jnp.stack([padded[:, column_tile * BLOCK:column_tile * BLOCK + window_rows] for column_tile in range(tile_count)])
    col_pos = (jnp.arange(CUT).astype(jnp.float32) + 0.5) / CUT - 0.5

    def row_tile(tile_number):
        window = lax.dynamic_slice_in_dim(windows, tile_number * BLOCK, window_rows, 1)
        smeared = jnp.einsum("tmj,kjn->kmtn", window, across, precision=highest)
        smeared = to_bf(smeared).reshape(KERNELS, window_rows, CUT)
        stacked = jnp.einsum("knm,kmc->knc", downward, smeared, precision=highest)
        basis_parts = jnp.einsum("jk,knc->jnc", coeffs, stacked, precision=highest)
        row_pos = ((tile_number * BLOCK + jnp.arange(BLOCK)).astype(jnp.float32) + 0.5) / CUT - 0.5
        row_pos = row_pos[:, None]
        return basis_parts[0] + row_pos * basis_parts[1] + col_pos[None, :] * basis_parts[2] + (row_pos * col_pos[None, :]) * basis_parts[3]

    convolved = lax.map(row_tile, jnp.arange(tile_count)).reshape(CUT, CUT)
    padded_conv = jnp.pad(convolved, ((0, 1), (0, 1)))
    col_frac = (((shifts % 4).astype(jnp.float32) + 0.5) / 4.0).reshape(tile_count, 1, tile_count, 1)
    row_frac = (((shifts // 4).astype(jnp.float32) + 0.5) / 4.0).reshape(tile_count, 1, tile_count, 1)

    def on_grid(raster):
        return raster.reshape(tile_count, BLOCK, tile_count, BLOCK)

    result = (1.0 - row_frac) * (1.0 - col_frac) * on_grid(convolved)
    result = result + (1.0 - row_frac) * col_frac * on_grid(padded_conv[:-1, 1:])
    result = result + row_frac * (1.0 - col_frac) * on_grid(padded_conv[1:, :-1])
    result = result + row_frac * col_frac * on_grid(padded_conv[1:, 1:])
    return result.transpose(0, 2, 1, 3).reshape(tile_count * tile_count, BLOCK, BLOCK)


def smooth_rows(raster, dilation):
    kept_rows = raster.shape[0] - 4 * dilation
    summed = spline_taps[0] * raster[0:kept_rows]
    for offset in range(1, 5):
        summed = summed + spline_taps[offset] * raster[offset * dilation:offset * dilation + kept_rows]
    return summed


def smooth_cols(raster, dilation):
    col_count = raster.shape[1]
    padded = jnp.pad(raster, ((0, 0), (2 * dilation, 2 * dilation)))
    summed = spline_taps[0] * padded[:, 0:col_count]
    for offset in range(1, 5):
        summed = summed + spline_taps[offset] * padded[:, offset * dilation:offset * dilation + col_count]
    return summed


def shrink(detail, limit):
    return detail - jnp.clip(detail, -limit, limit)


def sweep(raster, limits):
    coarse_one = smooth_cols(smooth_rows(jnp.pad(raster, ((2, 2), (0, 0))), 1), 1)
    coarse_two = smooth_cols(smooth_rows(jnp.pad(coarse_one, ((4, 4), (0, 0))), 2), 2)
    detail_fine = raster - coarse_one
    detail_coarse = coarse_one - coarse_two
    return coarse_two + shrink(detail_fine, fine_tau * limits) + shrink(detail_coarse, coarse_tau * limits)


def reference(cutouts, vert_taps, horiz_taps, field_coeffs, exposure_weight, dest_owner, dest_column, shift_index, threshold_level):
    targets = (dest_owner[:, :, 0] * PW + dest_column).astype(jnp.int32)

    def one_exposure(carry, bundle):
        coadd_sum, weight_total = carry
        cutout, vertical, horizontal, coeffs, weight, target_row, shifts = bundle
        blocks = convolve_shift(cutout, vertical, horizontal, coeffs, shifts)
        weight_bf = to_bf(weight)
        coadd_sum = coadd_sum.at[target_row].add(weight_bf * to_bf(blocks))
        weight_total = weight_total.at[target_row].add(weight_bf * jnp.ones(target_row.shape, jnp.float32))
        return (coadd_sum, weight_total), blocks

    start = (jnp.zeros((OWNERS * PW, BLOCK, BLOCK), jnp.float32), jnp.zeros((OWNERS * PW,), jnp.float32))
    (coadd_sum, weight_total), shifted = lax.scan(one_exposure, start, (cutouts, vert_taps, horiz_taps, field_coeffs, exposure_weight, targets, shift_index))
    coadd = coadd_sum / (1.0 + weight_total)[:, None, None]
    coadd = coadd.reshape(OWNERS, PW, BLOCK, BLOCK).transpose(0, 2, 1, 3).reshape(SKY_ROWS, SKY_COLS)
    levels = threshold_level.astype(jnp.float32)
    limits = jnp.repeat(jnp.repeat(levels, BLOCK, axis=0), BLOCK, axis=1)
    denoised = coadd
    for sweep_number in range(SWEEPS):
        denoised = sweep(denoised, limits)
    template_blocks = to_bf(denoised).reshape(OWNERS, BLOCK, PW, BLOCK).transpose(0, 2, 1, 3).reshape(OWNERS * PW, BLOCK, BLOCK)
    tile_count = CUT // BLOCK

    def difference_of(bundle):
        blocks, target_row = bundle
        raster = blocks - template_blocks[target_row]
        return raster.reshape(tile_count, tile_count, BLOCK, BLOCK).transpose(0, 2, 1, 3).reshape(CUT, CUT)

    difference = lax.map(difference_of, (shifted, targets))
    return denoised, difference
```

```python
import jax
import jax.numpy as jnp
from jax import lax
from jax.experimental import pallas as pl
from jax.experimental.pallas import tpu as pltpu
from jax.sharding import PartitionSpec as P

BLOCK = 128
PW = 4
SWEEPS = 2
SIDE = 512
TILES = 4
KERNELS = 16
TAPS = 21
MARGIN = 10
TOP = 16
HALO = 16
TAIL = 32
MAIN_K = KERNELS * BLOCK
TAIL_K = KERNELS * TAIL
PAD_ROWS = SIDE + 2 * TOP
PAD_COLS = SIDE + BLOCK
WIN_ROWS = BLOCK + TAIL
SLOTS = 2
SLOT_ROWS = SLOTS * BLOCK
META = 8
MIB = 1 << 20
AXES = ("visit", "sky")

fine_tau = 0.04
coarse_tau = 0.02
f32 = jnp.float32
bf16 = jnp.bfloat16


def conv_kernel(
    owner_ref, rank_ref, fx_ref, fy_ref,
    cut_ref, gh_ref, gv_ref, cmain_ref, ctail_ref, meta_ref,
    shifted_ref, send_ref,
    padded, win, band, base_main, base_tail, ab_main, ab_tail, sm_main, sm_tail,
    carry, staged, sems,
):
    e = pl.program_id(0)
    step = pl.program_id(1)
    p = TILES - 1 - step
    first = (e == 0) & (step == 0)
    meta_copy = pltpu.make_async_copy(
        meta_ref, send_ref.at[:, pl.ds(SLOT_ROWS, META), :], sems.at[32]
    )

    @pl.when(first)
    def _():
        meta_copy.start()
        padded[pl.ds(0, TOP), :] = jnp.zeros((TOP, PAD_COLS), bf16)
        padded[pl.ds(TOP + SIDE, TOP), :] = jnp.zeros((TOP, PAD_COLS), bf16)
        band[pl.ds(WIN_ROWS, 256 - WIN_ROWS), :] = jnp.zeros((256 - WIN_ROWS, MAIN_K), bf16)

    @pl.when(step == 0)
    def _():
        image = cut_ref[0]
        wide = jnp.concatenate([image, jnp.zeros((SIDE, BLOCK), f32)], axis=1)
        padded[pl.ds(TOP, SIDE), :] = pltpu.roll(wide, MARGIN, 1).astype(bf16)
        lanes = lax.broadcasted_iota(jnp.int32, (BLOCK, BLOCK), 1)
        for k in range(KERNELS):
            row = jnp.broadcast_to(gh_ref[0, pl.ds(k, 1), :], (WIN_ROWS, 256))
            rolled = pltpu.roll(row, 0, 1, stride=1, stride_axis=0)
            band[pl.ds(0, WIN_ROWS), k * BLOCK : (k + 1) * BLOCK] = rolled[:, :BLOCK].astype(bf16)
        for group in range(KERNELS // 4):
            tail = jnp.zeros((BLOCK, BLOCK), f32)
            for inner in range(4):
                k = group * 4 + inner
                row = jnp.broadcast_to(gv_ref[0, pl.ds(k, 1), :], (BLOCK, 256))
                rolled = pltpu.roll(row, 0, 1, stride=1, stride_axis=0)
                base_main[:, k * BLOCK : (k + 1) * BLOCK] = rolled[:, :BLOCK]
                moved = pltpu.roll(rolled, (128 + TAIL * inner) % 256, 1)[:, :BLOCK]
                here = (lanes >= TAIL * inner) & (lanes < TAIL * (inner + 1))
                tail = jnp.where(here, moved, tail)
            base_tail[:, group * BLOCK : (group + 1) * BLOCK] = tail
        carry[...] = jnp.zeros_like(carry)

    start = pl.multiple_of(p * BLOCK, BLOCK)
    for q in range(TILES):
        win[pl.ds(q * WIN_ROWS, WIN_ROWS), :] = padded[
            pl.ds(start, WIN_ROWS), q * BLOCK : q * BLOCK + 256
        ]
    for pair in range(KERNELS // 2):
        part = jnp.dot(
            win[...], band[:, pair * 256 : (pair + 1) * 256], preferred_element_type=f32
        ).astype(bf16)
        for q in range(TILES):
            for inner in range(2):
                k = pair * 2 + inner
                piece = part[
                    q * WIN_ROWS : (q + 1) * WIN_ROWS, inner * BLOCK : (inner + 1) * BLOCK
                ]
                cols = slice(q * BLOCK, (q + 1) * BLOCK)
                sm_main[pl.ds(k * BLOCK, BLOCK), cols] = piece[:BLOCK]
                sm_tail[pl.ds(k * TAIL, TAIL), cols] = piece[BLOCK:]

    rows = lax.broadcasted_iota(jnp.int32, (BLOCK, 1), 0) + p * BLOCK
    u = (rows.astype(f32) + 0.5) / SIDE - 0.5
    for out, base, coeff in ((ab_main, base_main, cmain_ref), (ab_tail, base_tail, ctail_ref)):
        c0, c1 = coeff[0, pl.ds(0, 1), :], coeff[0, pl.ds(1, 1), :]
        c2, c3 = coeff[0, pl.ds(2, 1), :], coeff[0, pl.ds(3, 1), :]
        out[pl.ds(0, BLOCK), :] = (base[...] * (c0 + u * c1)).astype(bf16)
        out[pl.ds(BLOCK, BLOCK), :] = (base[...] * (c2 + u * c3)).astype(bf16)
    both = jnp.dot(ab_main[...], sm_main[...], preferred_element_type=f32)
    both = both + jnp.dot(ab_tail[...], sm_tail[...], preferred_element_type=f32)
    cols = lax.broadcasted_iota(jnp.int32, (1, SIDE), 1)
    v = (cols.astype(f32) + 0.5) / SIDE - 0.5
    image = both[:BLOCK] + v * both[BLOCK:]

    first_block = e * 16 + p * TILES
    tile_of = cols // BLOCK
    fx = jnp.zeros((1, SIDE), f32)
    fy = jnp.zeros((1, SIDE), f32)
    for q in range(TILES):
        fx = jnp.where(tile_of == q, fx_ref[first_block + q], fx)
        fy = jnp.where(tile_of == q, fy_ref[first_block + q], fy)
    inside = cols < SIDE - 1

    def along(x):
        return (1.0 - fx) * x + fx * jnp.where(inside, pltpu.roll(x, SIDE - 1, 1), 0.0)

    mixed = along(image)
    below_row = along(carry[...])[:1]
    last = lax.broadcasted_iota(jnp.int32, (BLOCK, 1), 0) == BLOCK - 1
    below = jnp.where(last, below_row, pltpu.roll(mixed, BLOCK - 1, 0))
    result = (1.0 - fy) * mixed + fy * below
    carry[...] = image[:8]
    shifted_ref[0] = result
    order = (e * TILES + step) * TILES
    rounded = result.astype(bf16)
    for q in range(TILES):
        staged[order + q] = rounded[:, q * BLOCK : (q + 1) * BLOCK]
        block = first_block + q
        row0 = pl.multiple_of(rank_ref[block] * BLOCK, BLOCK)
        pltpu.make_async_copy(
            staged.at[order + q],
            send_ref.at[owner_ref[block], pl.ds(row0, BLOCK), :],
            sems.at[order + q],
        ).start()

    @pl.when((e == pl.num_programs(0) - 1) & (step == TILES - 1))
    def _():
        meta_copy.wait()
        for i in range(32):
            pltpu.make_async_copy(
                staged.at[i], send_ref.at[0, pl.ds(0, BLOCK), :], sems.at[i]
            ).wait()


def conv_send(owners, ranks, fx, fy, cutouts, gh, gv, cmain, ctail, meta):
    def by_exposure(shape):
        return pl.BlockSpec((1,) + shape, lambda e, s, *_: (e,) + (0,) * len(shape))

    return pl.pallas_call(
        conv_kernel,
        out_shape=(
            jax.ShapeDtypeStruct((2, SIDE, SIDE), f32),
            jax.ShapeDtypeStruct((128, SLOT_ROWS + META, BLOCK), bf16),
        ),
        grid_spec=pltpu.PrefetchScalarGridSpec(
            num_scalar_prefetch=4,
            grid=(2, TILES),
            in_specs=[
                by_exposure((SIDE, SIDE)),
                by_exposure((KERNELS, 256)),
                by_exposure((KERNELS, 256)),
                by_exposure((4, MAIN_K)),
                by_exposure((4, TAIL_K)),
                pl.BlockSpec((128, META, BLOCK), lambda e, s, *_: (0, 0, 0)),
            ],
            out_specs=[
                pl.BlockSpec((1, BLOCK, SIDE), lambda e, s, *_: (e, TILES - 1 - s, 0)),
                pl.BlockSpec(memory_space=pl.ANY),
            ],
            scratch_shapes=[
                pltpu.VMEM((PAD_ROWS, PAD_COLS), bf16),
                pltpu.VMEM((TILES * WIN_ROWS, 256), bf16),
                pltpu.VMEM((256, MAIN_K), bf16),
                pltpu.VMEM((BLOCK, MAIN_K), f32),
                pltpu.VMEM((BLOCK, TAIL_K), f32),
                pltpu.VMEM((2 * BLOCK, MAIN_K), bf16),
                pltpu.VMEM((2 * BLOCK, TAIL_K), bf16),
                pltpu.VMEM((MAIN_K, SIDE), bf16),
                pltpu.VMEM((TAIL_K, SIDE), bf16),
                pltpu.VMEM((8, SIDE), f32),
                pltpu.VMEM((32, BLOCK, BLOCK), bf16),
                pltpu.SemaphoreType.DMA((33,)),
            ],
        ),
        compiler_params=pltpu.CompilerParams(vmem_limit_bytes=48 * MIB),
        name="conv_send",
    )(owners, ranks, fx, fy, cutouts, gh, gv, cmain, ctail, meta)


GROUP = 8


def coadd_kernel(col_ref, w_ref, got_ref, strip_ref, head_ref, foot_ref, acc, total):
    step = pl.program_id(0)

    @pl.when(step == 0)
    def _():
        acc[...] = jnp.zeros_like(acc)
        for j in range(PW):
            total[j] = 0.0

    for i in range(GROUP):
        for slot in range(SLOTS):
            index = (step * GROUP + i) * SLOTS + slot

            @pl.when(col_ref[index] >= 0)
            def _():
                col, w = col_ref[index], w_ref[index]
                block = got_ref[i, slot * BLOCK : (slot + 1) * BLOCK, :].astype(f32)
                acc[col] = acc[col] + w * block
                total[col] = total[col] + w

    @pl.when(step == pl.num_programs(0) - 1)
    def _():
        for j in range(PW):
            mean = acc[j] / jnp.full((BLOCK, BLOCK), 1.0 + total[j], f32)
            cols = slice(j * BLOCK, (j + 1) * BLOCK)
            strip_ref[:, cols] = mean
            head_ref[:, cols] = mean[:HALO]
            foot_ref[:, cols] = mean[BLOCK - HALO :]


def coadd(cols, weights, got):
    def whole(rows):
        return pl.BlockSpec((rows, SIDE), lambda i, *_: (0, 0))

    return pl.pallas_call(
        coadd_kernel,
        out_shape=tuple(jax.ShapeDtypeStruct((r, SIDE), f32) for r in (BLOCK, HALO, HALO)),
        grid_spec=pltpu.PrefetchScalarGridSpec(
            num_scalar_prefetch=2,
            grid=(128 // GROUP,),
            in_specs=[
                pl.BlockSpec((GROUP, SLOT_ROWS + META, BLOCK), lambda i, *_: (i, 0, 0))
            ],
            out_specs=[whole(BLOCK), whole(HALO), whole(HALO)],
            scratch_shapes=[
                pltpu.VMEM((PW, BLOCK, BLOCK), f32),
                pltpu.SMEM((PW,), f32),
            ],
        ),
        compiler_params=pltpu.CompilerParams(vmem_limit_bytes=16 * MIB),
        name="coadd",
    )(cols, weights, got)


WIDE = BLOCK + 2 * HALO


def starlet_kernel(
    col_ref, level_ref, edge_ref, strip_ref, before_ref, after_ref,
    sky_ref, answer_ref, wide, template, sems,
):
    wide[pl.ds(0, HALO), :] = before_ref[...]
    wide[pl.ds(HALO, BLOCK), :] = strip_ref[...]
    wide[pl.ds(HALO + BLOCK, HALO), :] = after_ref[...]
    rows = lax.broadcasted_iota(jnp.int32, (WIDE, 1), 0)
    cols = lax.broadcasted_iota(jnp.int32, (1, SIDE), 1)
    above = (rows < HALO).astype(f32)
    under = (rows >= HALO + BLOCK).astype(f32)
    inside = 1.0 - above * edge_ref[0] - under * edge_ref[1]
    tile_of = cols // BLOCK
    lims = []
    for r in range(3):
        lim = jnp.zeros((1, SIDE), f32)
        for j in range(PW):
            lim = jnp.where(tile_of == j, level_ref[r * PW + j], lim)
        lims.append(lim)
    middle = (1.0 - above) - under
    lim = above * lims[0] + middle * lims[1] + under * lims[2]
    fine, coarse = fine_tau * lim, coarse_tau * lim

    def smooth(x, d):
        def up(y, n):
            return pltpu.roll(y, n % WIDE, 0)

        x = 0.375 * x + 0.25 * (up(x, d) + up(x, -d)) + 0.0625 * (up(x, 2 * d) + up(x, -2 * d))

        def side(y, n):
            keep = cols >= n if n > 0 else cols < SIDE + n
            return jnp.where(keep, pltpu.roll(y, n % SIDE, 1), 0.0)

        return (
            0.375 * x
            + 0.25 * (side(x, d) + side(x, -d))
            + 0.0625 * (side(x, 2 * d) + side(x, -2 * d))
        )

    def shrink(detail, limit):
        return detail - jnp.clip(detail, -limit, limit)

    x = wide[...]
    for _ in range(SWEEPS):
        x = x * inside
        one = smooth(x, 1) * inside
        two = smooth(one, 2)
        x = two + shrink(x - one, fine) + shrink(one - two, coarse)
    sky = x[HALO : HALO + BLOCK]
    sky_ref[...] = sky
    rounded = sky.astype(bf16)
    for j in range(PW):
        template[j] = rounded[:, j * BLOCK : (j + 1) * BLOCK]

    def copy(index):
        return pltpu.make_async_copy(
            template.at[col_ref[index]], answer_ref.at[index], sems.at[index]
        )

    @pl.loop(0, 256)
    def _(index):
        @pl.when(col_ref[index] >= 0)
        def _():
            copy(index).start()

    @pl.loop(0, 256)
    def _(index):
        @pl.when(col_ref[index] >= 0)
        def _():
            copy(index).wait()


def starlet(cols, levels, edges, strip, before, after):
    def whole(rows):
        return pl.BlockSpec((rows, SIDE), lambda i, *_: (0, 0))

    return pl.pallas_call(
        starlet_kernel,
        out_shape=(
            jax.ShapeDtypeStruct((BLOCK, SIDE), f32),
            jax.ShapeDtypeStruct((256, BLOCK, BLOCK), bf16),
        ),
        grid_spec=pltpu.PrefetchScalarGridSpec(
            num_scalar_prefetch=3,
            grid=(1,),
            in_specs=[whole(BLOCK), whole(HALO), whole(HALO)],
            out_specs=[whole(BLOCK), pl.BlockSpec(memory_space=pl.ANY)],
            scratch_shapes=[
                pltpu.VMEM((WIDE, SIDE), f32),
                pltpu.VMEM((PW, BLOCK, BLOCK), bf16),
                pltpu.SemaphoreType.DMA((256,)),
            ],
        ),
        compiler_params=pltpu.CompilerParams(vmem_limit_bytes=16 * MIB),
        name="starlet",
    )(cols, levels, edges, strip, before, after)


def difference_kernel(slot_ref, shifted_ref, b0, b1, b2, b3, out_ref):
    for q, block in enumerate((b0, b1, b2, b3)):
        cols = slice(q * BLOCK, (q + 1) * BLOCK)
        out_ref[0, :, cols] = shifted_ref[0, :, cols] - block[0].astype(f32)


def difference(slots, shifted, returned):
    def block_of(q):
        return pl.BlockSpec(
            (1, BLOCK, BLOCK), lambda e, p, slot: (slot[e * 16 + p * TILES + q], 0, 0)
        )

    rows = pl.BlockSpec((1, BLOCK, SIDE), lambda e, p, slot: (e, p, 0))
    return pl.pallas_call(
        difference_kernel,
        out_shape=jax.ShapeDtypeStruct((2, SIDE, SIDE), f32),
        grid_spec=pltpu.PrefetchScalarGridSpec(
            num_scalar_prefetch=1,
            grid=(2, TILES),
            in_specs=[rows] + [block_of(q) for q in range(TILES)],
            out_specs=rows,
        ),
        compiler_params=pltpu.CompilerParams(vmem_limit_bytes=16 * MIB),
        name="difference",
    )(slots, shifted, returned, returned, returned, returned)


def taps_to_rows(vert_taps, horiz_taps):
    h = horiz_taps.astype(bf16).astype(f32)
    v = vert_taps.astype(bf16).astype(f32)
    zeros = jnp.zeros(h.shape[:2] + (256 - TAPS,), f32)
    gh = jnp.concatenate([h[:, :, :1], zeros, h[:, :, :0:-1]], axis=2)
    gv = jnp.pad(v, ((0, 0), (0, 0), (TOP - MARGIN, 256 - TAPS - TOP + MARGIN)))
    return gh, gv


def shards(
    cutouts, vert_taps, horiz_taps, field_coeffs, exposure_weight,
    dest_owner, dest_column, shift_index, threshold_level,
):
    owners = dest_owner.reshape(32)
    columns = dest_column.reshape(32)
    earlier = jnp.arange(32)[None, :] < jnp.arange(32)[:, None]
    ranks = jnp.sum(((owners[:, None] == owners[None, :]) & earlier).astype(jnp.int32), axis=1)
    slots = owners * SLOTS + ranks
    shifts = shift_index.reshape(32)
    fx = ((shifts % 4).astype(f32) + 0.5) / 4.0
    fy = ((shifts // 4).astype(f32) + 0.5) / 4.0
    weight = jnp.repeat(exposure_weight.astype(bf16).astype(f32), 16)
    hit = (jnp.arange(256)[:, None] == slots[None, :]).astype(f32)
    meta_col = jnp.sum(hit * (columns[None, :] + 1).astype(f32), axis=1) - 1.0
    meta_w = jnp.sum(hit * weight[None, :], axis=1)
    lane = jnp.arange(BLOCK)
    meta = jnp.where(lane == 0, meta_col[:, None], jnp.where(lane == 1, meta_w[:, None], 0.0))
    meta = jnp.pad(meta.reshape(128, SLOTS, BLOCK), ((0, 0), (0, META - SLOTS), (0, 0)))
    gh, gv = taps_to_rows(vert_taps, horiz_taps)
    cmain = jnp.repeat(field_coeffs, BLOCK, axis=2)
    ctail = jnp.repeat(field_coeffs, TAIL, axis=2)
    shifted, send = conv_send(
        owners, ranks, fx, fy, cutouts, gh, gv, cmain, ctail, meta.astype(bf16)
    )
    got = lax.all_to_all(send, AXES, split_axis=0, concat_axis=0, tiled=True)
    notes = got[:, SLOT_ROWS : SLOT_ROWS + SLOTS, :2].astype(f32)
    cols = notes[:, :, 0].astype(jnp.int32).reshape(256)
    weights = notes[:, :, 1].reshape(256)
    strip, head, foot = coadd(cols, weights, got)
    count = lax.axis_size(AXES)
    down = [(i, i + 1) for i in range(count - 1)]
    up = [(i + 1, i) for i in range(count - 1)]
    before = lax.ppermute(foot, AXES, down)
    after = lax.ppermute(head, AXES, up)
    here = lax.axis_index(AXES)
    levels = threshold_level.astype(f32)
    level_rows = jnp.pad(levels, ((1, 1), (0, 0)))
    near = lax.dynamic_slice(level_rows, (here, 0), (3, PW)).reshape(3 * PW)
    edges = jnp.stack([here == 0, here == count - 1]).astype(f32)
    sky, answers = starlet(cols, near, edges, strip, before, after)
    returned = lax.all_to_all(answers, AXES, split_axis=0, concat_axis=0, tiled=True)
    return sky, difference(slots, shifted, returned)


def solution(mesh):
    placed = (
        P(AXES, None, None),
        P(AXES, None, None),
        P(AXES, None, None),
        P(AXES, None, None),
        P(AXES),
        P(AXES, None, None),
        P(AXES, None),
        P(AXES, None),
        P(),
    )
    return jax.shard_map(
        shards,
        mesh=mesh,
        in_specs=placed,
        out_specs=(P(AXES, None), P(AXES, None, None)),
        check_vma=False,
    )
```

```python
import jax
import jax.numpy as jnp
from jax import lax
from jax.experimental import pallas as pl
from jax.experimental.pallas import tpu as pltpu
from jax.sharding import PartitionSpec as P

BLOCK = 128
PW = 4
SWEEPS = 2
SIDE = 512
TILES = 4
KERNELS = 16
TAPS = 21
MARGIN = 10
TOP = 16
HALO = 16
TAIL = 32
MAIN_K = KERNELS * BLOCK
TAIL_K = KERNELS * TAIL
PAD_ROWS = SIDE + 2 * TOP
PAD_COLS = SIDE + BLOCK
WIN_ROWS = BLOCK + TAIL
GROUP = 16
SLICE = BLOCK // GROUP
UNROLL = 8
MIB = 1 << 20
AXES = ("z", "y", "x", "c")
NEAR = ("y", "x")

fine_tau = 0.04
coarse_tau = 0.02
f32 = jnp.float32
bf16 = jnp.bfloat16


def conv_kernel(
    fx_ref, fy_ref,
    cut_ref, gh_ref, gv_ref, cmain_ref, ctail_ref, note_ref,
    shifted_ref, send_ref,
    padded, win, band, base_main, base_tail, ab_main, ab_tail, sm_main, sm_tail,
    carry,
):
    e = pl.program_id(0)
    step = pl.program_id(1)
    p = TILES - 1 - step
    first = (e == 0) & (step == 0)
    @pl.when(first)
    def _():
        for g in range(GROUP):
            send_ref[g, 32] = note_ref[...]
        padded[pl.ds(0, TOP), :] = jnp.zeros((TOP, PAD_COLS), bf16)
        padded[pl.ds(TOP + SIDE, TOP), :] = jnp.zeros((TOP, PAD_COLS), bf16)
        band[pl.ds(WIN_ROWS, 256 - WIN_ROWS), :] = jnp.zeros((256 - WIN_ROWS, MAIN_K), bf16)

    @pl.when(step == 0)
    def _():
        image = cut_ref[0]
        wide = jnp.concatenate([image, jnp.zeros((SIDE, BLOCK), f32)], axis=1)
        padded[pl.ds(TOP, SIDE), :] = pltpu.roll(wide, MARGIN, 1).astype(bf16)
        lanes = lax.broadcasted_iota(jnp.int32, (BLOCK, BLOCK), 1)
        for k in range(KERNELS):
            row = jnp.broadcast_to(gh_ref[0, pl.ds(k, 1), :], (WIN_ROWS, 256))
            rolled = pltpu.roll(row, 0, 1, stride=1, stride_axis=0)
            band[pl.ds(0, WIN_ROWS), k * BLOCK : (k + 1) * BLOCK] = rolled[:, :BLOCK].astype(bf16)
        for group in range(KERNELS // 4):
            tail = jnp.zeros((BLOCK, BLOCK), f32)
            for inner in range(4):
                k = group * 4 + inner
                row = jnp.broadcast_to(gv_ref[0, pl.ds(k, 1), :], (BLOCK, 256))
                rolled = pltpu.roll(row, 0, 1, stride=1, stride_axis=0)
                base_main[:, k * BLOCK : (k + 1) * BLOCK] = rolled[:, :BLOCK]
                moved = pltpu.roll(rolled, (128 + TAIL * inner) % 256, 1)[:, :BLOCK]
                here = (lanes >= TAIL * inner) & (lanes < TAIL * (inner + 1))
                tail = jnp.where(here, moved, tail)
            base_tail[:, group * BLOCK : (group + 1) * BLOCK] = tail
        carry[...] = jnp.zeros_like(carry)

    start = pl.multiple_of(p * BLOCK, BLOCK)
    for q in range(TILES):
        win[pl.ds(q * WIN_ROWS, WIN_ROWS), :] = padded[
            pl.ds(start, WIN_ROWS), q * BLOCK : q * BLOCK + 256
        ]
    for pair in range(KERNELS // 2):
        part = jnp.dot(
            win[...], band[:, pair * 256 : (pair + 1) * 256], preferred_element_type=f32
        ).astype(bf16)
        for q in range(TILES):
            for inner in range(2):
                k = pair * 2 + inner
                piece = part[
                    q * WIN_ROWS : (q + 1) * WIN_ROWS, inner * BLOCK : (inner + 1) * BLOCK
                ]
                cols = slice(q * BLOCK, (q + 1) * BLOCK)
                sm_main[pl.ds(k * BLOCK, BLOCK), cols] = piece[:BLOCK]
                sm_tail[pl.ds(k * TAIL, TAIL), cols] = piece[BLOCK:]

    rows = lax.broadcasted_iota(jnp.int32, (BLOCK, 1), 0) + p * BLOCK
    u = (rows.astype(f32) + 0.5) / SIDE - 0.5
    for out, base, coeff in ((ab_main, base_main, cmain_ref), (ab_tail, base_tail, ctail_ref)):
        c0, c1 = coeff[0, pl.ds(0, 1), :], coeff[0, pl.ds(1, 1), :]
        c2, c3 = coeff[0, pl.ds(2, 1), :], coeff[0, pl.ds(3, 1), :]
        out[pl.ds(0, BLOCK), :] = (base[...] * (c0 + u * c1)).astype(bf16)
        out[pl.ds(BLOCK, BLOCK), :] = (base[...] * (c2 + u * c3)).astype(bf16)
    both = jnp.dot(ab_main[...], sm_main[...], preferred_element_type=f32)
    both = both + jnp.dot(ab_tail[...], sm_tail[...], preferred_element_type=f32)
    cols = lax.broadcasted_iota(jnp.int32, (1, SIDE), 1)
    v = (cols.astype(f32) + 0.5) / SIDE - 0.5
    image = both[:BLOCK] + v * both[BLOCK:]

    first_block = e * 16 + p * TILES
    tile_of = cols // BLOCK
    fx = jnp.zeros((1, SIDE), f32)
    fy = jnp.zeros((1, SIDE), f32)
    for q in range(TILES):
        fx = jnp.where(tile_of == q, fx_ref[first_block + q], fx)
        fy = jnp.where(tile_of == q, fy_ref[first_block + q], fy)
    inside = cols < SIDE - 1

    def along(x):
        return (1.0 - fx) * x + fx * jnp.where(inside, pltpu.roll(x, SIDE - 1, 1), 0.0)

    mixed = along(image)
    below_row = along(carry[...])[:1]
    last = lax.broadcasted_iota(jnp.int32, (BLOCK, 1), 0) == BLOCK - 1
    below = jnp.where(last, below_row, pltpu.roll(mixed, BLOCK - 1, 0))
    result = (1.0 - fy) * mixed + fy * below
    carry[...] = image[:8]
    shifted_ref[0] = result
    rounded = result.astype(bf16)
    for q in range(TILES):
        for g in range(GROUP):
            send_ref[g, first_block + q] = rounded[
                g * SLICE : (g + 1) * SLICE, q * BLOCK : (q + 1) * BLOCK
            ]


def conv_send(fx, fy, cutouts, gh, gv, cmain, ctail, note):
    def by_exposure(shape):
        return pl.BlockSpec((1,) + shape, lambda e, s, *_: (e,) + (0,) * len(shape))

    return pl.pallas_call(
        conv_kernel,
        out_shape=(
            jax.ShapeDtypeStruct((2, SIDE, SIDE), f32),
            jax.ShapeDtypeStruct((GROUP, 33, SLICE, BLOCK), bf16),
        ),
        grid_spec=pltpu.PrefetchScalarGridSpec(
            num_scalar_prefetch=2,
            grid=(2, TILES),
            in_specs=[
                by_exposure((SIDE, SIDE)),
                by_exposure((KERNELS, 256)),
                by_exposure((KERNELS, 256)),
                by_exposure((4, MAIN_K)),
                by_exposure((4, TAIL_K)),
                pl.BlockSpec((SLICE, BLOCK), lambda e, s, *_: (0, 0)),
            ],
            out_specs=[
                pl.BlockSpec((1, BLOCK, SIDE), lambda e, s, *_: (e, TILES - 1 - s, 0)),
                pl.BlockSpec((GROUP, 33, SLICE, BLOCK), lambda e, s, *_: (0, 0, 0, 0)),
            ],
            scratch_shapes=[
                pltpu.VMEM((PAD_ROWS, PAD_COLS), bf16),
                pltpu.VMEM((TILES * WIN_ROWS, 256), bf16),
                pltpu.VMEM((256, MAIN_K), bf16),
                pltpu.VMEM((BLOCK, MAIN_K), f32),
                pltpu.VMEM((BLOCK, TAIL_K), f32),
                pltpu.VMEM((2 * BLOCK, MAIN_K), bf16),
                pltpu.VMEM((2 * BLOCK, TAIL_K), bf16),
                pltpu.VMEM((MAIN_K, SIDE), bf16),
                pltpu.VMEM((TAIL_K, SIDE), bf16),
                pltpu.VMEM((8, SIDE), f32),
            ],
        ),
        compiler_params=pltpu.CompilerParams(vmem_limit_bytes=48 * MIB),
        name="conv_send",
    )(fx, fy, cutouts, gh, gv, cmain, ctail, note)


def whole(*shape):
    return pl.BlockSpec(shape, lambda i, *_: (0,) * len(shape))


def combine_kernel(target_ref, w_ref, got_ref, out_ref, acc):
    acc[...] = jnp.zeros_like(acc)
    rows = lax.broadcasted_iota(jnp.int32, (SLICE, BLOCK), 0)

    @pl.loop(0, GROUP * 32 // UNROLL)
    def _(turn):
        for i in range(UNROLL):
            index = turn * UNROLL + i
            source, block = index >> 5, index & 31
            target, w = target_ref[index], w_ref[index]
            owner, col = target >> 2, target & 3
            acc[owner, col] = acc[owner, col] + w * got_ref[source, block].astype(f32)
            acc[owner, PW] = acc[owner, PW] + jnp.where(rows == col, w, 0.0)

    @pl.loop(0, 128)
    def _(owner):
        for j in range(PW):
            out_ref[owner, j] = acc[owner, j].astype(bf16)
        total = acc[owner, PW]
        high = total.astype(bf16).astype(f32)
        out_ref[owner, PW] = (high + pltpu.roll(total - high, PW, 0)).astype(bf16)


def combine(targets, weights, got):
    return pl.pallas_call(
        combine_kernel,
        out_shape=jax.ShapeDtypeStruct((128, PW + 1, SLICE, BLOCK), bf16),
        grid_spec=pltpu.PrefetchScalarGridSpec(
            num_scalar_prefetch=2,
            grid=(1,),
            in_specs=[whole(GROUP, 33, SLICE, BLOCK)],
            out_specs=whole(128, PW + 1, SLICE, BLOCK),
            scratch_shapes=[pltpu.VMEM((128, PW + 1, SLICE, BLOCK), f32)],
        ),
        compiler_params=pltpu.CompilerParams(vmem_limit_bytes=24 * MIB),
        name="combine",
    )(targets, weights, got)


def coadd_kernel(got_ref, strip_ref, head_ref, foot_ref):
    def gathered(g, j):
        total = jnp.zeros((SLICE, BLOCK), f32)
        for z in range(4):
            for c in range(2):
                total = total + got_ref[z * 32 + g * 2 + c, j].astype(f32)
        return total

    parts = gathered(0, PW)
    weight = 1.0 + (parts + pltpu.roll(parts, PW, 0))
    for j in range(PW):
        inverse = 1.0 / weight[j : j + 1]
        cols = slice(j * BLOCK, (j + 1) * BLOCK)
        for g in range(GROUP):
            strip_ref[g * SLICE : (g + 1) * SLICE, cols] = gathered(g, j) * inverse
    head_ref[...] = strip_ref[:HALO]
    foot_ref[...] = strip_ref[BLOCK - HALO :]


def coadd(got):
    return pl.pallas_call(
        coadd_kernel,
        out_shape=tuple(jax.ShapeDtypeStruct((r, SIDE), f32) for r in (BLOCK, HALO, HALO)),
        grid=(1,),
        in_specs=[whole(128, PW + 1, SLICE, BLOCK)],
        out_specs=[whole(BLOCK, SIDE), whole(HALO, SIDE), whole(HALO, SIDE)],
        compiler_params=pltpu.CompilerParams(vmem_limit_bytes=16 * MIB),
        name="coadd",
    )(got)


WIDE = BLOCK + 2 * HALO


def starlet_kernel(
    level_ref, edge_ref, strip_ref, before_ref, after_ref,
    sky_ref, answer_ref, wide,
):
    wide[pl.ds(0, HALO), :] = before_ref[...]
    wide[pl.ds(HALO, BLOCK), :] = strip_ref[...]
    wide[pl.ds(HALO + BLOCK, HALO), :] = after_ref[...]
    rows = lax.broadcasted_iota(jnp.int32, (WIDE, 1), 0)
    cols = lax.broadcasted_iota(jnp.int32, (1, SIDE), 1)
    above = (rows < HALO).astype(f32)
    under = (rows >= HALO + BLOCK).astype(f32)
    inside = 1.0 - above * edge_ref[0] - under * edge_ref[1]
    tile_of = cols // BLOCK
    lims = []
    for r in range(3):
        lim = jnp.zeros((1, SIDE), f32)
        for j in range(PW):
            lim = jnp.where(tile_of == j, level_ref[r * PW + j], lim)
        lims.append(lim)
    middle = (1.0 - above) - under
    lim = above * lims[0] + middle * lims[1] + under * lims[2]
    fine, coarse = fine_tau * lim, coarse_tau * lim

    def smooth(x, d):
        def up(y, n):
            return pltpu.roll(y, n % WIDE, 0)

        x = 0.375 * x + 0.25 * (up(x, d) + up(x, -d)) + 0.0625 * (up(x, 2 * d) + up(x, -2 * d))

        def side(y, n):
            keep = cols >= n if n > 0 else cols < SIDE + n
            return jnp.where(keep, pltpu.roll(y, n % SIDE, 1), 0.0)

        return (
            0.375 * x
            + 0.25 * (side(x, d) + side(x, -d))
            + 0.0625 * (side(x, 2 * d) + side(x, -2 * d))
        )

    def shrink(detail, limit):
        return detail - jnp.clip(detail, -limit, limit)

    x = wide[...]
    for _ in range(SWEEPS):
        x = x * inside
        one = smooth(x, 1) * inside
        two = smooth(one, 2)
        x = two + shrink(x - one, fine) + shrink(one - two, coarse)
    sky = x[HALO : HALO + BLOCK]
    sky_ref[...] = sky
    rounded = sky.astype(bf16)
    for g in range(GROUP):
        for j in range(PW):
            part = rounded[g * SLICE : (g + 1) * SLICE, j * BLOCK : (j + 1) * BLOCK]
            for z in range(4):
                for c in range(2):
                    answer_ref[z * 32 + g * 2 + c, j] = part


def starlet(levels, edges, strip, before, after):
    return pl.pallas_call(
        starlet_kernel,
        out_shape=(
            jax.ShapeDtypeStruct((BLOCK, SIDE), f32),
            jax.ShapeDtypeStruct((128, PW, SLICE, BLOCK), bf16),
        ),
        grid_spec=pltpu.PrefetchScalarGridSpec(
            num_scalar_prefetch=2,
            grid=(1,),
            in_specs=[whole(BLOCK, SIDE), whole(HALO, SIDE), whole(HALO, SIDE)],
            out_specs=[whole(BLOCK, SIDE), whole(128, PW, SLICE, BLOCK)],
            scratch_shapes=[pltpu.VMEM((WIDE, SIDE), f32)],
        ),
        compiler_params=pltpu.CompilerParams(vmem_limit_bytes=16 * MIB),
        name="starlet",
    )(levels, edges, strip, before, after)


def pick_kernel(target_ref, all_ref, out_ref):
    @pl.loop(0, GROUP * 32 // UNROLL)
    def _(turn):
        for i in range(UNROLL):
            index = turn * UNROLL + i
            target = target_ref[index]
            out_ref[index >> 5, index & 31] = all_ref[target >> 2, target & 3]


def pick(targets, templates):
    return pl.pallas_call(
        pick_kernel,
        out_shape=jax.ShapeDtypeStruct((GROUP, 32, SLICE, BLOCK), bf16),
        grid_spec=pltpu.PrefetchScalarGridSpec(
            num_scalar_prefetch=1,
            grid=(1,),
            in_specs=[whole(128, PW, SLICE, BLOCK)],
            out_specs=whole(GROUP, 32, SLICE, BLOCK),
        ),
        compiler_params=pltpu.CompilerParams(vmem_limit_bytes=16 * MIB),
        name="pick",
    )(targets, templates)


def difference_kernel(shifted_ref, template_ref, out_ref):
    for q in range(TILES):
        for g in range(GROUP):
            rows, cols = slice(g * SLICE, (g + 1) * SLICE), slice(q * BLOCK, (q + 1) * BLOCK)
            out_ref[0, rows, cols] = shifted_ref[0, rows, cols] - template_ref[g, q].astype(f32)


def difference(shifted, returned):
    rows = pl.BlockSpec((1, BLOCK, SIDE), lambda e, p: (e, p, 0))
    return pl.pallas_call(
        difference_kernel,
        out_shape=jax.ShapeDtypeStruct((2, SIDE, SIDE), f32),
        grid=(2, TILES),
        in_specs=[
            rows,
            pl.BlockSpec((GROUP, TILES, SLICE, BLOCK), lambda e, p: (0, e * TILES + p, 0, 0)),
        ],
        out_specs=rows,
        compiler_params=pltpu.CompilerParams(vmem_limit_bytes=16 * MIB),
        name="difference",
    )(shifted, returned)


def taps_to_rows(vert_taps, horiz_taps):
    h = horiz_taps.astype(bf16).astype(f32)
    v = vert_taps.astype(bf16).astype(f32)
    zeros = jnp.zeros(h.shape[:2] + (256 - TAPS,), f32)
    gh = jnp.concatenate([h[:, :, :1], zeros, h[:, :, :0:-1]], axis=2)
    gv = jnp.pad(v, ((0, 0), (0, 0), (TOP - MARGIN, 256 - TAPS - TOP + MARGIN)))
    return gh, gv


def shards(
    cutouts, vert_taps, horiz_taps, field_coeffs, exposure_weight,
    dest_owner, dest_column, shift_index, threshold_level,
):
    owners = dest_owner.reshape(32)
    columns = dest_column.reshape(32)
    shifts = shift_index.reshape(32)
    fx = ((shifts % 4).astype(f32) + 0.5) / 4.0
    fy = ((shifts // 4).astype(f32) + 0.5) / 4.0
    weight = jnp.repeat(exposure_weight, 16)
    note = jnp.stack([owners.astype(f32), columns.astype(f32), weight]).astype(bf16)
    note = jnp.pad(note, ((0, SLICE - 3), (0, BLOCK - 32)))
    gh, gv = taps_to_rows(vert_taps, horiz_taps)
    cmain = jnp.repeat(field_coeffs, BLOCK, axis=2)
    ctail = jnp.repeat(field_coeffs, TAIL, axis=2)
    shifted, slices = conv_send(fx, fy, cutouts, gh, gv, cmain, ctail, note)
    got = lax.all_to_all(slices, NEAR, split_axis=0, concat_axis=0, tiled=True)
    notes = got[:, 32, :3, :32].astype(f32)
    targets = (notes[:, 0] * PW + notes[:, 1]).astype(jnp.int32).reshape(GROUP * 32)
    weights = notes[:, 2].reshape(GROUP * 32)
    sums = combine(targets, weights, got)
    partial = lax.all_to_all(sums, AXES, split_axis=0, concat_axis=0, tiled=True)
    strip, head, foot = coadd(partial)
    count = lax.axis_size(AXES)
    down = [(i, i + 1) for i in range(count - 1)]
    up = [(i + 1, i) for i in range(count - 1)]
    before = lax.ppermute(foot, AXES, down)
    after = lax.ppermute(head, AXES, up)
    here = lax.axis_index(AXES)
    levels = threshold_level.astype(f32)
    level_rows = jnp.pad(levels, ((1, 1), (0, 0)))
    near = lax.dynamic_slice(level_rows, (here, 0), (3, PW)).reshape(3 * PW)
    edges = jnp.stack([here == 0, here == count - 1]).astype(f32)
    sky, answers = starlet(near, edges, strip, before, after)
    templates = lax.all_to_all(answers, AXES, split_axis=0, concat_axis=0, tiled=True)
    picked = pick(targets, templates)
    returned = lax.all_to_all(picked, NEAR, split_axis=0, concat_axis=0, tiled=True)
    return sky, difference(shifted, returned)


def solution(mesh):
    split = jax.sharding.Mesh(mesh.devices.reshape(4, 4, 4, 2), AXES)
    placed = (
        P(AXES, None, None),
        P(AXES, None, None),
        P(AXES, None, None),
        P(AXES, None, None),
        P(AXES),
        P(AXES, None, None),
        P(AXES, None),
        P(AXES, None),
        P(),
    )
    return jax.shard_map(
        shards,
        mesh=split,
        in_specs=placed,
        out_specs=(P(AXES, None), P(AXES, None, None)),
        check_vma=False,
    )
```

```python
import jax
import jax.numpy as jnp
from jax import lax
from jax.experimental import pallas as pl
from jax.experimental.pallas import tpu as pltpu
from jax.sharding import PartitionSpec as P

BLOCK = 128
PW = 4
SWEEPS = 2
SIDE = 512
TILES = 4
KERNELS = 16
TAPS = 21
MARGIN = 10
TOP = 16
HALO = 16
TAIL = 32
MAIN_K = KERNELS * BLOCK
TAIL_K = KERNELS * TAIL
PAD_ROWS = SIDE + 2 * TOP
PAD_COLS = SIDE + BLOCK
WIN_ROWS = BLOCK + TAIL
GROUP = 16
SLICE = BLOCK // GROUP
MIB = 1 << 20
AXES = ("z", "y", "x", "c")
NEAR = ("y", "x")

fine_tau = 0.04
coarse_tau = 0.02
f32 = jnp.float32
bf16 = jnp.bfloat16


def lane_of(shape):
    return lax.broadcasted_iota(jnp.int32, shape, len(shape) - 1)


def row_of(shape):
    return lax.broadcasted_iota(jnp.int32, shape, 0)


def placed_taps(taps, first, step):
    shape = (TAPS, BLOCK)
    lanes = (first + step * row_of(shape)) & (BLOCK - 1)
    onto = (lane_of(shape) == lanes).astype(bf16)
    return jnp.dot(taps.astype(bf16), onto, preferred_element_type=f32)


def sloped(rows, k):
    row = jnp.broadcast_to(rows[k : k + 1], (8, BLOCK))
    return pltpu.roll(row, 0, 1, stride=1, stride_axis=0)


def conv_kernel(
    owner_ref, column_ref, shift_ref, weight_ref,
    cut_ref, vert_ref, horiz_ref, coeff_ref,
    shifted_ref, send_ref,
    padded, win, band, base_main, base_tail, cmain, ctail, ab_main, ab_tail, smeared,
    carry,
):
    e = pl.program_id(0)
    step = pl.program_id(1)
    p = TILES - 1 - step
    tile = (8, BLOCK)

    @pl.when((e == 0) & (step == 0))
    def _():
        lanes = lane_of((1, BLOCK))
        owners = jnp.zeros((1, BLOCK), f32)
        columns = jnp.zeros((1, BLOCK), f32)
        for b in range(32):
            owners = jnp.where(lanes == b, owner_ref[b // 16, b % 16].astype(f32), owners)
            columns = jnp.where(lanes == b, column_ref[b // 16, b % 16].astype(f32), columns)
        weights = jnp.where(lanes < 16, weight_ref[0], weight_ref[1])
        rows = row_of(tile)
        note = jnp.where(rows == 0, owners, jnp.where(rows == 1, columns, weights))
        note = note.astype(bf16)
        for g in range(GROUP):
            send_ref[g, 32] = note
        padded[pl.ds(0, TOP), :] = jnp.zeros((TOP, PAD_COLS), bf16)
        padded[pl.ds(TOP + SIDE, TOP), :] = jnp.zeros((TOP, PAD_COLS), bf16)
        band[pl.ds(WIN_ROWS, 256 - WIN_ROWS), :] = jnp.zeros((256 - WIN_ROWS, MAIN_K), bf16)
        base_tail[...] = jnp.zeros_like(base_tail)

    @pl.when(step == 0)
    def _():
        image = cut_ref[0]
        wide = jnp.concatenate([image, jnp.zeros((SIDE, BLOCK), f32)], axis=1)
        padded[pl.ds(TOP, SIDE), :] = pltpu.roll(wide, MARGIN, 1).astype(bf16)
        rows_h = placed_taps(horiz_ref[0], BLOCK, -1)
        rows_v = placed_taps(vert_ref[0], TOP - MARGIN, 1)
        lanes, rows = lane_of(tile), row_of(tile)
        for k in range(KERNELS):
            cols = slice(k * BLOCK, (k + 1) * BLOCK)
            slope = sloped(rows_h, k)
            tiles = []
            for i in range(WIN_ROWS // 8):
                part = pltpu.roll(slope, 8 * i % BLOCK, 1) if 8 * i % BLOCK else slope
                if i < 3 or i >= 16:
                    lag = 8 * i + rows - lanes
                    part = jnp.where((lag >= 0) & (lag < TAPS), part, 0.0)
                tiles.append(part)
            band[pl.ds(0, WIN_ROWS), cols] = jnp.concatenate(tiles, axis=0).astype(bf16)
            slope = sloped(rows_v, k)
            for i in range(BLOCK // 8):
                part = pltpu.roll(slope, 8 * i, 1) if i else slope
                if i >= 12:
                    spot = 32 * (k % 4)
                    tail = jnp.where(lanes < TAIL, part, 0.0)
                    tail = pltpu.roll(tail, spot, 1) if spot else tail
                    group = slice(k // 4 * BLOCK, (k // 4 + 1) * BLOCK)
                    here = slice(8 * i, 8 * i + 8)
                    if spot:
                        tail = tail + base_tail[here, group]
                    base_tail[here, group] = tail
                    part = jnp.where(lanes < TAIL, 0.0, part)
                base_main[8 * i : 8 * i + 8, cols] = part
            coeff = jnp.broadcast_to(coeff_ref[0][:, k : k + 1], (4, BLOCK))
            cmain[:, cols] = coeff
            group = slice(k // 4 * BLOCK, (k // 4 + 1) * BLOCK)
            if k % 4:
                keep = lane_of((4, BLOCK)) < TAIL * (k % 4)
                coeff = jnp.where(keep, ctail[:, group], coeff)
            ctail[:, group] = coeff
        for q in range(TILES):
            win[q * PAD_ROWS : (q + 1) * PAD_ROWS, :] = padded[:, q * BLOCK : q * BLOCK + 256]
        for pair in range(KERNELS // 2):
            part = jnp.dot(
                win[...], band[:, pair * 256 : (pair + 1) * 256], preferred_element_type=f32
            ).astype(bf16)
            for q in range(TILES):
                for inner in range(2):
                    smeared[pair * 2 + inner, :, q * BLOCK : (q + 1) * BLOCK] = part[
                        q * PAD_ROWS : (q + 1) * PAD_ROWS, inner * BLOCK : (inner + 1) * BLOCK
                    ]
        carry[...] = jnp.zeros_like(carry)

    start = pl.multiple_of(p * BLOCK, BLOCK)
    u = ((row_of((BLOCK, 1)) + p * BLOCK).astype(f32) + 0.5) / SIDE - 0.5
    for out, base, coeff in ((ab_main, base_main, cmain), (ab_tail, base_tail, ctail)):
        c0, c1 = coeff[pl.ds(0, 1), :], coeff[pl.ds(1, 1), :]
        c2, c3 = coeff[pl.ds(2, 1), :], coeff[pl.ds(3, 1), :]
        out[pl.ds(0, BLOCK), :] = (base[...] * (c0 + u * c1)).astype(bf16)
        out[pl.ds(BLOCK, BLOCK), :] = (base[...] * (c2 + u * c3)).astype(bf16)
    main = smeared[:, pl.ds(start, BLOCK), :].reshape(MAIN_K, SIDE)
    tail = smeared[:, pl.ds(start + BLOCK, TAIL), :].reshape(TAIL_K, SIDE)
    both = jnp.dot(ab_main[...], main, preferred_element_type=f32)
    both = both + jnp.dot(ab_tail[...], tail, preferred_element_type=f32)
    cols = lane_of((1, SIDE))
    v = (cols.astype(f32) + 0.5) / SIDE - 0.5
    image = both[:BLOCK] + v * both[BLOCK:]

    tile_of = cols // BLOCK
    fx = jnp.zeros((1, SIDE), f32)
    fy = jnp.zeros((1, SIDE), f32)
    for q in range(TILES):
        shift = shift_ref[e, p * TILES + q]
        fx = jnp.where(tile_of == q, ((shift & 3).astype(f32) + 0.5) * 0.25, fx)
        fy = jnp.where(tile_of == q, ((shift >> 2).astype(f32) + 0.5) * 0.25, fy)
    inside = cols < SIDE - 1

    def along(x):
        return (1.0 - fx) * x + fx * jnp.where(inside, pltpu.roll(x, SIDE - 1, 1), 0.0)

    mixed = along(image)
    below_row = along(carry[...])[:1]
    last = row_of((BLOCK, 1)) == BLOCK - 1
    below = jnp.where(last, below_row, pltpu.roll(mixed, BLOCK - 1, 0))
    result = (1.0 - fy) * mixed + fy * below
    carry[...] = image[:8]
    shifted_ref[0] = result
    rounded = result.astype(bf16)
    first_block = e * 16 + p * TILES
    for q in range(TILES):
        for g in range(GROUP):
            send_ref[g, first_block + q] = rounded[
                g * SLICE : (g + 1) * SLICE, q * BLOCK : (q + 1) * BLOCK
            ]


def conv_send(owners, columns, shifts, weight, cutouts, vert, horiz, coeffs):
    def by_exposure(*shape):
        return pl.BlockSpec((1,) + shape, lambda e, s, *_: (e,) + (0,) * len(shape))

    return pl.pallas_call(
        conv_kernel,
        out_shape=(
            jax.ShapeDtypeStruct((2, SIDE, SIDE), f32),
            jax.ShapeDtypeStruct((GROUP, 33, SLICE, BLOCK), bf16),
        ),
        grid_spec=pltpu.PrefetchScalarGridSpec(
            num_scalar_prefetch=4,
            grid=(2, TILES),
            in_specs=[
                by_exposure(SIDE, SIDE),
                by_exposure(KERNELS, TAPS),
                by_exposure(KERNELS, TAPS),
                by_exposure(4, KERNELS),
            ],
            out_specs=[
                pl.BlockSpec((1, BLOCK, SIDE), lambda e, s, *_: (e, TILES - 1 - s, 0)),
                pl.BlockSpec((GROUP, 33, SLICE, BLOCK), lambda e, s, *_: (0, 0, 0, 0)),
            ],
            scratch_shapes=[
                pltpu.VMEM((PAD_ROWS, PAD_COLS), bf16),
                pltpu.VMEM((TILES * PAD_ROWS, 256), bf16),
                pltpu.VMEM((256, MAIN_K), bf16),
                pltpu.VMEM((BLOCK, MAIN_K), f32),
                pltpu.VMEM((BLOCK, TAIL_K), f32),
                pltpu.VMEM((4, MAIN_K), f32),
                pltpu.VMEM((4, TAIL_K), f32),
                pltpu.VMEM((2 * BLOCK, MAIN_K), bf16),
                pltpu.VMEM((2 * BLOCK, TAIL_K), bf16),
                pltpu.VMEM((KERNELS, PAD_ROWS, SIDE), bf16),
                pltpu.VMEM((8, SIDE), f32),
            ],
        ),
        compiler_params=pltpu.CompilerParams(vmem_limit_bytes=48 * MIB),
        name="conv_send",
    )(owners, columns, shifts, weight, cutouts, vert, horiz, coeffs)


def whole(*shape):
    return pl.BlockSpec(shape, lambda i, *_: (0,) * len(shape))


def combine_kernel(target_ref, w_ref, got_ref, targets_ref, weights_ref, out_ref, even, odd):
    even[...] = jnp.zeros_like(even)
    odd[...] = jnp.zeros_like(odd)

    @pl.loop(0, GROUP)
    def _(source):
        for block in range(32):
            index = source * 32 + block
            acc, target = (even, odd)[block % 2], target_ref[index]
            acc[target] = acc[target] + w_ref[index] * got_ref[source, block].astype(f32)

    shape = (SLICE, GROUP * 32)
    targets = jnp.broadcast_to(targets_ref[...], shape)
    weights = jnp.broadcast_to(weights_ref[...], shape)
    column = row_of(shape) & 3
    high_row = row_of((SLICE, BLOCK)) < PW

    @pl.loop(0, 128 // 8)
    def _(turn):
        for i in range(8):
            owner = turn * 8 + i
            for j in range(PW):
                total = even[owner * PW + j] + odd[owner * PW + j]
                out_ref[owner, j] = total.astype(bf16)
            hit = jnp.where(targets == owner * PW + column, weights, 0.0)
            total = jnp.broadcast_to(jnp.sum(hit, axis=1, keepdims=True), (SLICE, BLOCK))
            high = total.astype(bf16).astype(f32)
            out_ref[owner, PW] = jnp.where(high_row, high, total - high).astype(bf16)


def combine(targets, weights, got):
    return pl.pallas_call(
        combine_kernel,
        out_shape=jax.ShapeDtypeStruct((128, PW + 1, SLICE, BLOCK), bf16),
        grid_spec=pltpu.PrefetchScalarGridSpec(
            num_scalar_prefetch=2,
            grid=(1,),
            in_specs=[
                whole(GROUP, 33, SLICE, BLOCK),
                whole(1, GROUP * 32),
                whole(1, GROUP * 32),
            ],
            out_specs=whole(128, PW + 1, SLICE, BLOCK),
            scratch_shapes=[pltpu.VMEM((128 * PW, SLICE, BLOCK), f32)] * 2,
        ),
        compiler_params=pltpu.CompilerParams(vmem_limit_bytes=24 * MIB),
        name="combine",
    )(targets, weights, got, targets.reshape(1, -1), weights.reshape(1, -1))


def summed(got_ref, g, j):
    total = jnp.zeros((SLICE, BLOCK), f32)
    for z in range(4):
        for c in range(2):
            total = total + got_ref[z * 32 + g * 2 + c, j].astype(f32)
    return total


def inverse_weights(got_ref):
    parts = summed(got_ref, 0, PW)
    return 1.0 / (1.0 + (parts + pltpu.roll(parts, PW, 0)))


def edges_kernel(got_ref, head_ref, foot_ref):
    inverse = inverse_weights(got_ref)
    for j in range(PW):
        cols = slice(j * BLOCK, (j + 1) * BLOCK)
        for i in range(HALO // SLICE):
            rows = slice(i * SLICE, (i + 1) * SLICE)
            head_ref[rows, cols] = summed(got_ref, i, j) * inverse[j : j + 1]
            far = GROUP - HALO // SLICE + i
            foot_ref[rows, cols] = summed(got_ref, far, j) * inverse[j : j + 1]


def edge_rows(got):
    return pl.pallas_call(
        edges_kernel,
        out_shape=(jax.ShapeDtypeStruct((HALO, SIDE), f32),) * 2,
        grid=(1,),
        in_specs=[whole(128, PW + 1, SLICE, BLOCK)],
        out_specs=[whole(HALO, SIDE), whole(HALO, SIDE)],
        compiler_params=pltpu.CompilerParams(vmem_limit_bytes=16 * MIB),
        name="edge_rows",
    )(got)


WIDE = BLOCK + 2 * HALO


def starlet_kernel(
    level_ref, edge_ref, got_ref, before_ref, after_ref,
    sky_ref, answer_ref, wide,
):
    wide[pl.ds(0, HALO), :] = before_ref[...]
    inverse = inverse_weights(got_ref)
    for g in range(GROUP):
        for j in range(PW):
            wide[pl.ds(HALO + g * SLICE, SLICE), j * BLOCK : (j + 1) * BLOCK] = (
                summed(got_ref, g, j) * inverse[j : j + 1]
            )
    wide[pl.ds(HALO + BLOCK, HALO), :] = after_ref[...]
    rows = lax.broadcasted_iota(jnp.int32, (WIDE, 1), 0)
    cols = lax.broadcasted_iota(jnp.int32, (1, SIDE), 1)
    above = (rows < HALO).astype(f32)
    under = (rows >= HALO + BLOCK).astype(f32)
    inside = 1.0 - above * edge_ref[0] - under * edge_ref[1]
    tile_of = cols // BLOCK
    lims = []
    for r in range(3):
        lim = jnp.zeros((1, SIDE), f32)
        for j in range(PW):
            lim = jnp.where(tile_of == j, level_ref[r * PW + j], lim)
        lims.append(lim)
    middle = (1.0 - above) - under
    lim = above * lims[0] + middle * lims[1] + under * lims[2]
    fine, coarse = fine_tau * lim, coarse_tau * lim

    def smooth(x, d):
        def up(y, n):
            return pltpu.roll(y, n % WIDE, 0)

        x = 0.375 * x + 0.25 * (up(x, d) + up(x, -d)) + 0.0625 * (up(x, 2 * d) + up(x, -2 * d))

        def side(y, n):
            keep = cols >= n if n > 0 else cols < SIDE + n
            return jnp.where(keep, pltpu.roll(y, n % SIDE, 1), 0.0)

        return (
            0.375 * x
            + 0.25 * (side(x, d) + side(x, -d))
            + 0.0625 * (side(x, 2 * d) + side(x, -2 * d))
        )

    def shrink(detail, limit):
        return detail - jnp.clip(detail, -limit, limit)

    x = wide[...]
    for _ in range(SWEEPS):
        x = x * inside
        one = smooth(x, 1) * inside
        two = smooth(one, 2)
        x = two + shrink(x - one, fine) + shrink(one - two, coarse)
    sky = x[HALO : HALO + BLOCK]
    sky_ref[...] = sky
    rounded = sky.astype(bf16)
    for g in range(GROUP):
        for j in range(PW):
            part = rounded[g * SLICE : (g + 1) * SLICE, j * BLOCK : (j + 1) * BLOCK]
            for z in range(4):
                for c in range(2):
                    answer_ref[z * 32 + g * 2 + c, j] = part


def starlet(levels, edges, partial, before, after):
    return pl.pallas_call(
        starlet_kernel,
        out_shape=(
            jax.ShapeDtypeStruct((BLOCK, SIDE), f32),
            jax.ShapeDtypeStruct((128, PW, SLICE, BLOCK), bf16),
        ),
        grid_spec=pltpu.PrefetchScalarGridSpec(
            num_scalar_prefetch=2,
            grid=(1,),
            in_specs=[whole(128, PW + 1, SLICE, BLOCK), whole(HALO, SIDE), whole(HALO, SIDE)],
            out_specs=[whole(BLOCK, SIDE), whole(128, PW, SLICE, BLOCK)],
            scratch_shapes=[pltpu.VMEM((WIDE, SIDE), f32)],
        ),
        compiler_params=pltpu.CompilerParams(vmem_limit_bytes=16 * MIB),
        name="starlet",
    )(levels, edges, partial, before, after)


def pick_kernel(target_ref, all_ref, out_ref):
    @pl.loop(0, GROUP)
    def _(source):
        for block in range(32):
            out_ref[source, block] = all_ref[target_ref[source * 32 + block]]


def pick(targets, templates):
    return pl.pallas_call(
        pick_kernel,
        out_shape=jax.ShapeDtypeStruct((GROUP, 32, SLICE, BLOCK), bf16),
        grid_spec=pltpu.PrefetchScalarGridSpec(
            num_scalar_prefetch=1,
            grid=(1,),
            in_specs=[whole(128 * PW, SLICE, BLOCK)],
            out_specs=whole(GROUP, 32, SLICE, BLOCK),
        ),
        compiler_params=pltpu.CompilerParams(vmem_limit_bytes=16 * MIB),
        name="pick",
    )(targets, templates.reshape(128 * PW, SLICE, BLOCK))


def difference_kernel(shifted_ref, template_ref, out_ref):
    for q in range(TILES):
        for g in range(GROUP):
            rows, cols = slice(g * SLICE, (g + 1) * SLICE), slice(q * BLOCK, (q + 1) * BLOCK)
            out_ref[0, rows, cols] = shifted_ref[0, rows, cols] - template_ref[g, q].astype(f32)


def difference(shifted, returned):
    rows = pl.BlockSpec((1, BLOCK, SIDE), lambda e, p: (e, p, 0))
    return pl.pallas_call(
        difference_kernel,
        out_shape=jax.ShapeDtypeStruct((2, SIDE, SIDE), f32),
        grid=(2, TILES),
        in_specs=[
            rows,
            pl.BlockSpec((GROUP, TILES, SLICE, BLOCK), lambda e, p: (0, e * TILES + p, 0, 0)),
        ],
        out_specs=rows,
        compiler_params=pltpu.CompilerParams(vmem_limit_bytes=16 * MIB),
        name="difference",
    )(shifted, returned)


def shards(
    cutouts, vert_taps, horiz_taps, field_coeffs, exposure_weight,
    dest_owner, dest_column, shift_index, threshold_level,
):
    shifted, slices = conv_send(
        dest_owner.reshape(2, 16), dest_column, shift_index, exposure_weight,
        cutouts, vert_taps, horiz_taps, field_coeffs,
    )
    got = lax.all_to_all(slices, NEAR, split_axis=0, concat_axis=0, tiled=True)
    notes = got[:, 32, :3, :32].astype(f32)
    targets = (notes[:, 0] * PW + notes[:, 1]).astype(jnp.int32).reshape(GROUP * 32)
    weights = notes[:, 2].reshape(GROUP * 32)
    sums = combine(targets, weights, got)
    partial = lax.all_to_all(sums, AXES, split_axis=0, concat_axis=0, tiled=True)
    head, foot = edge_rows(partial)
    count = lax.axis_size(AXES)
    down = [(i, i + 1) for i in range(count - 1)]
    up = [(i + 1, i) for i in range(count - 1)]
    before = lax.ppermute(foot, AXES, down)
    after = lax.ppermute(head, AXES, up)
    here = lax.axis_index(AXES)
    levels = threshold_level.astype(f32)
    level_rows = jnp.pad(levels, ((1, 1), (0, 0)))
    near = lax.dynamic_slice(level_rows, (here, 0), (3, PW)).reshape(3 * PW)
    edges = jnp.stack([here == 0, here == count - 1]).astype(f32)
    sky, answers = starlet(near, edges, partial, before, after)
    templates = lax.all_to_all(answers, AXES, split_axis=0, concat_axis=0, tiled=True)
    picked = pick(targets, templates)
    returned = lax.all_to_all(picked, NEAR, split_axis=0, concat_axis=0, tiled=True)
    return sky, difference(shifted, returned)


def solution(mesh):
    split = jax.sharding.Mesh(mesh.devices.reshape(4, 4, 4, 2), AXES)
    placed = (
        P(AXES, None, None),
        P(AXES, None, None),
        P(AXES, None, None),
        P(AXES, None, None),
        P(AXES),
        P(AXES, None, None),
        P(AXES, None),
        P(AXES, None),
        P(),
    )
    return jax.shard_map(
        shards,
        mesh=split,
        in_specs=placed,
        out_specs=(P(AXES, None), P(AXES, None, None)),
        check_vma=False,
    )
```

```python
import jax
import jax.numpy as jnp
from jax import lax
from jax.experimental import pallas as pl
from jax.experimental.pallas import tpu as pltpu
from jax.sharding import PartitionSpec as P

BLOCK = 128
PW = 4
SWEEPS = 2
SIDE = 512
TILES = 4
KERNELS = 16
TAPS = 21
MARGIN = 10
TOP = 16
HALO = 16
TAIL = 32
MAIN_K = KERNELS * BLOCK
TAIL_K = KERNELS * TAIL
PAD_ROWS = SIDE + 2 * TOP
PAD_COLS = SIDE + BLOCK
WIN_ROWS = BLOCK + TAIL
GROUP = 16
SLICE = BLOCK // GROUP
MIB = 1 << 20
AXES = ("z1", "z0", "y1", "y0", "x1", "x0", "c")
NEAR = ("z0", "y0", "x0", "c")
TILES_OUT = PW + 2

fine_tau = 0.04
coarse_tau = 0.02
f32 = jnp.float32
bf16 = jnp.bfloat16


def member(group, g):
    far = (group >> 2 & 1, group >> 1 & 1, group & 1)
    near = (g >> 3 & 1, g >> 2 & 1, g >> 1 & 1, g & 1)
    bits = (far[0], near[0], far[1], near[1], far[2], near[2], near[3])
    return sum(bit << (6 - i) for i, bit in enumerate(bits))


def every(g):
    return pl.ds(g, SLICE, stride=GROUP)


def lane_of(shape):
    return lax.broadcasted_iota(jnp.int32, shape, len(shape) - 1)


def row_of(shape):
    return lax.broadcasted_iota(jnp.int32, shape, 0)


def placed_taps(taps, first, step):
    shape = (TAPS, BLOCK)
    lanes = (first + step * row_of(shape)) & (BLOCK - 1)
    onto = (lane_of(shape) == lanes).astype(bf16)
    return jnp.dot(taps.astype(bf16), onto, preferred_element_type=f32)


def sloped(rows, k):
    row = jnp.broadcast_to(rows[k : k + 1], (8, BLOCK))
    return pltpu.roll(row, 0, 1, stride=1, stride_axis=0)


def conv_kernel(
    owner_ref, column_ref, shift_ref, weight_ref,
    cut_ref, vert_ref, horiz_ref, coeff_ref,
    shifted_ref, send_ref,
    padded, win, band, base_main, base_tail, cmain, ctail, ab_main, ab_tail, smeared,
    carry, cells,
):
    e = pl.program_id(0)
    step = pl.program_id(1)
    p = TILES - 1 - step
    tile = (8, BLOCK)

    @pl.when((e == 0) & (step == 0))
    def _():
        lanes = lane_of((1, BLOCK))
        owners = jnp.zeros((1, BLOCK), f32)
        columns = jnp.zeros((1, BLOCK), f32)
        for b in range(32):
            owners = jnp.where(lanes == b, owner_ref[b // 16, b % 16].astype(f32), owners)
            columns = jnp.where(lanes == b, column_ref[b // 16, b % 16].astype(f32), columns)
        weights = jnp.where(lanes < 16, weight_ref[0], weight_ref[1])
        rows = row_of(tile)
        note = jnp.where(rows == 0, owners, jnp.where(rows == 1, columns, weights))
        note = note.astype(bf16)
        for g in range(GROUP):
            send_ref[g, 32] = note
        padded[pl.ds(0, TOP), :] = jnp.zeros((TOP, PAD_COLS), bf16)
        padded[pl.ds(TOP + SIDE, TOP), :] = jnp.zeros((TOP, PAD_COLS), bf16)
        band[pl.ds(WIN_ROWS, 256 - WIN_ROWS), :] = jnp.zeros((256 - WIN_ROWS, MAIN_K), bf16)
        base_tail[...] = jnp.zeros_like(base_tail)

    @pl.when(step == 0)
    def _():
        image = cut_ref[0]
        wide = jnp.concatenate([image, jnp.zeros((SIDE, BLOCK), f32)], axis=1)
        padded[pl.ds(TOP, SIDE), :] = pltpu.roll(wide, MARGIN, 1).astype(bf16)
        rows_h = placed_taps(horiz_ref[0], BLOCK, -1)
        rows_v = placed_taps(vert_ref[0], TOP - MARGIN, 1)
        lanes, rows = lane_of(tile), row_of(tile)
        for k in range(KERNELS):
            cols = slice(k * BLOCK, (k + 1) * BLOCK)
            slope = sloped(rows_h, k)
            tiles = []
            for i in range(WIN_ROWS // 8):
                part = pltpu.roll(slope, 8 * i % BLOCK, 1) if 8 * i % BLOCK else slope
                if i < 3 or i >= 16:
                    lag = 8 * i + rows - lanes
                    part = jnp.where((lag >= 0) & (lag < TAPS), part, 0.0)
                tiles.append(part)
            band[pl.ds(0, WIN_ROWS), cols] = jnp.concatenate(tiles, axis=0).astype(bf16)
            slope = sloped(rows_v, k)
            for i in range(BLOCK // 8):
                part = pltpu.roll(slope, 8 * i, 1) if i else slope
                if i >= 12:
                    spot = 32 * (k % 4)
                    tail = jnp.where(lanes < TAIL, part, 0.0)
                    tail = pltpu.roll(tail, spot, 1) if spot else tail
                    group = slice(k // 4 * BLOCK, (k // 4 + 1) * BLOCK)
                    here = slice(8 * i, 8 * i + 8)
                    if spot:
                        tail = tail + base_tail[here, group]
                    base_tail[here, group] = tail
                    part = jnp.where(lanes < TAIL, 0.0, part)
                base_main[8 * i : 8 * i + 8, cols] = part
            coeff = jnp.broadcast_to(coeff_ref[0][:, k : k + 1], (4, BLOCK))
            cmain[:, cols] = coeff
            group = slice(k // 4 * BLOCK, (k // 4 + 1) * BLOCK)
            if k % 4:
                keep = lane_of((4, BLOCK)) < TAIL * (k % 4)
                coeff = jnp.where(keep, ctail[:, group], coeff)
            ctail[:, group] = coeff
        for q in range(TILES):
            win[q * PAD_ROWS : (q + 1) * PAD_ROWS, :] = padded[:, q * BLOCK : q * BLOCK + 256]
        for pair in range(KERNELS // 2):
            part = jnp.dot(
                win[...], band[:, pair * 256 : (pair + 1) * 256], preferred_element_type=f32
            ).astype(bf16)
            for q in range(TILES):
                for inner in range(2):
                    smeared[pair * 2 + inner, :, q * BLOCK : (q + 1) * BLOCK] = part[
                        q * PAD_ROWS : (q + 1) * PAD_ROWS, inner * BLOCK : (inner + 1) * BLOCK
                    ]
        carry[...] = jnp.zeros_like(carry)

    start = pl.multiple_of(p * BLOCK, BLOCK)
    u = ((row_of((BLOCK, 1)) + p * BLOCK).astype(f32) + 0.5) / SIDE - 0.5
    for out, base, coeff in ((ab_main, base_main, cmain), (ab_tail, base_tail, ctail)):
        c0, c1 = coeff[pl.ds(0, 1), :], coeff[pl.ds(1, 1), :]
        c2, c3 = coeff[pl.ds(2, 1), :], coeff[pl.ds(3, 1), :]
        out[pl.ds(0, BLOCK), :] = (base[...] * (c0 + u * c1)).astype(bf16)
        out[pl.ds(BLOCK, BLOCK), :] = (base[...] * (c2 + u * c3)).astype(bf16)
    main = smeared[:, pl.ds(start, BLOCK), :].reshape(MAIN_K, SIDE)
    tail = smeared[:, pl.ds(start + BLOCK, TAIL), :].reshape(TAIL_K, SIDE)
    both = jnp.dot(ab_main[...], main, preferred_element_type=f32)
    both = both + jnp.dot(ab_tail[...], tail, preferred_element_type=f32)
    cols = lane_of((1, SIDE))
    v = (cols.astype(f32) + 0.5) / SIDE - 0.5
    image = both[:BLOCK] + v * both[BLOCK:]

    tile_of = cols // BLOCK
    fx = jnp.zeros((1, SIDE), f32)
    fy = jnp.zeros((1, SIDE), f32)
    for q in range(TILES):
        shift = shift_ref[e, p * TILES + q]
        fx = jnp.where(tile_of == q, ((shift & 3).astype(f32) + 0.5) * 0.25, fx)
        fy = jnp.where(tile_of == q, ((shift >> 2).astype(f32) + 0.5) * 0.25, fy)
    inside = cols < SIDE - 1

    def along(x):
        return (1.0 - fx) * x + fx * jnp.where(inside, pltpu.roll(x, SIDE - 1, 1), 0.0)

    mixed = along(image)
    below_row = along(carry[...])[:1]
    last = row_of((BLOCK, 1)) == BLOCK - 1
    below = jnp.where(last, below_row, pltpu.roll(mixed, BLOCK - 1, 0))
    result = (1.0 - fy) * mixed + fy * below
    carry[...] = image[:8]
    shifted_ref[0] = result
    first_block = e * 16 + p * TILES
    for q in range(TILES):
        cells[q] = result[:, q * BLOCK : (q + 1) * BLOCK]
        for g in range(GROUP):
            send_ref[g, first_block + q] = cells[q, every(g), :].astype(bf16)


def conv_send(owners, columns, shifts, weight, cutouts, vert, horiz, coeffs):
    def by_exposure(*shape):
        return pl.BlockSpec((1,) + shape, lambda e, s, *_: (e,) + (0,) * len(shape))

    return pl.pallas_call(
        conv_kernel,
        out_shape=(
            pltpu.HBM((2, SIDE, SIDE), f32),
            jax.ShapeDtypeStruct((GROUP, 33, SLICE, BLOCK), bf16),
        ),
        grid_spec=pltpu.PrefetchScalarGridSpec(
            num_scalar_prefetch=4,
            grid=(2, TILES),
            in_specs=[
                by_exposure(SIDE, SIDE),
                by_exposure(KERNELS, TAPS),
                by_exposure(KERNELS, TAPS),
                by_exposure(4, KERNELS),
            ],
            out_specs=[
                pl.BlockSpec((1, BLOCK, SIDE), lambda e, s, *_: (e, TILES - 1 - s, 0)),
                pl.BlockSpec((GROUP, 33, SLICE, BLOCK), lambda e, s, *_: (0, 0, 0, 0)),
            ],
            scratch_shapes=[
                pltpu.VMEM((PAD_ROWS, PAD_COLS), bf16),
                pltpu.VMEM((TILES * PAD_ROWS, 256), bf16),
                pltpu.VMEM((256, MAIN_K), bf16),
                pltpu.VMEM((BLOCK, MAIN_K), f32),
                pltpu.VMEM((BLOCK, TAIL_K), f32),
                pltpu.VMEM((4, MAIN_K), f32),
                pltpu.VMEM((4, TAIL_K), f32),
                pltpu.VMEM((2 * BLOCK, MAIN_K), bf16),
                pltpu.VMEM((2 * BLOCK, TAIL_K), bf16),
                pltpu.VMEM((KERNELS, PAD_ROWS, SIDE), bf16),
                pltpu.VMEM((8, SIDE), f32),
                pltpu.VMEM((TILES, BLOCK, BLOCK), f32),
            ],
        ),
        compiler_params=pltpu.CompilerParams(vmem_limit_bytes=48 * MIB),
        name="conv_send",
    )(*(
        pltpu.with_memory_space_constraint(x, pltpu.HBM)
        for x in (owners, columns, shifts, weight, cutouts, vert, horiz, coeffs)
    ))


def whole(*shape):
    return pl.BlockSpec(shape, lambda i, *_: (0,) * len(shape))


def combine_kernel(
    target_ref, w_ref, got_ref, targets_ref, weights_ref, out_ref, even, odd, held
):
    even[...] = jnp.zeros_like(even)
    odd[...] = jnp.zeros_like(odd)
    tile = (SLICE, BLOCK)
    held[0] = jnp.zeros(tile, f32)
    held[129] = jnp.zeros(tile, f32)

    @pl.loop(0, GROUP)
    def _(source):
        for block in range(32):
            index = source * 32 + block
            acc = (even, odd)[block % 2]
            rows = pl.ds(pl.multiple_of((target_ref[index] + PW) * SLICE, SLICE), SLICE)
            acc[rows, :] = acc[rows, :] + w_ref[index] * got_ref[source, block].astype(f32)

    shape = (SLICE, GROUP * 32)
    targets = jnp.broadcast_to(targets_ref[...], shape)
    weights = jnp.broadcast_to(weights_ref[...], shape)
    column = row_of(shape) & 3
    upper = row_of(tile) < PW
    lanes = lane_of(tile)

    @pl.loop(0, 128 // 8)
    def _(turn):
        for i in range(8):
            owner = turn * 8 + i
            hit = jnp.where(targets == owner * PW + column, weights, 0.0)
            total = jnp.broadcast_to(jnp.sum(hit, axis=1, keepdims=True), tile)
            high = total.astype(bf16).astype(f32)
            held[owner + 1] = jnp.where(upper, high, total - high)

    @pl.loop(0, 128 // 8)
    def _(turn):
        for i in range(8):
            owner = turn * 8 + i
            base = pl.multiple_of((owner + 1) * PW * SLICE, PW * SLICE)
            for j in range(PW):
                rows = pl.ds(base + j * SLICE, SLICE)
                out_ref[owner, j] = (even[rows, :] + odd[rows, :]).astype(bf16)
            feet = pl.ds(base - PW * SLICE + SLICE - 1, 2 * PW, stride=SLICE)
            heads = pl.ds(base, 2 * PW, stride=SLICE)
            foot = even[feet, :] + odd[feet, :]
            head = even[heads, :] + odd[heads, :]
            out_ref[owner, PW] = jnp.where(upper, foot, head).astype(bf16)
            near = jnp.where(lanes == 1, held[owner], held[owner + 2])
            out_ref[owner, PW + 1] = jnp.where(lanes == 0, held[owner + 1], near).astype(bf16)


def combine(targets, weights, got):
    return pl.pallas_call(
        combine_kernel,
        out_shape=jax.ShapeDtypeStruct((128, TILES_OUT, SLICE, BLOCK), bf16),
        grid_spec=pltpu.PrefetchScalarGridSpec(
            num_scalar_prefetch=2,
            grid=(1,),
            in_specs=[
                whole(GROUP, 33, SLICE, BLOCK),
                whole(1, GROUP * 32),
                whole(1, GROUP * 32),
            ],
            out_specs=whole(128, TILES_OUT, SLICE, BLOCK),
            scratch_shapes=[pltpu.VMEM((130 * PW * SLICE, BLOCK), f32)] * 2
            + [pltpu.VMEM((130, SLICE, BLOCK), f32)],
        ),
        compiler_params=pltpu.CompilerParams(vmem_limit_bytes=24 * MIB),
        name="combine",
    )(targets, weights, got, targets.reshape(1, -1), weights.reshape(1, -1))


def summed(got_ref, g, j):
    total = got_ref[member(0, g), j].astype(f32)
    for group in range(1, 8):
        total = total + got_ref[member(group, g), j].astype(f32)
    return total


WIDE = BLOCK + 2 * HALO


def starlet_kernel(
    level_ref, edge_ref, got_ref,
    sky_ref, answer_ref, wide, cells,
):
    parts = summed(got_ref, 0, PW + 1)
    inverse = 1.0 / (1.0 + (parts + pltpu.roll(parts, PW, 0)))
    own, before, after = (
        [jnp.broadcast_to(inverse[j : j + 1, i : i + 1], (1, BLOCK)) for j in range(PW)]
        for i in range(3)
    )
    for g in range(GROUP):
        halo = summed(got_ref, g, PW)
        for j in range(PW):
            cols = slice(j * BLOCK, (j + 1) * BLOCK)
            cells[j, every(g), :] = summed(got_ref, g, j) * own[j]
            wide[pl.ds(g, 1), cols] = halo[j : j + 1] * before[j]
            wide[pl.ds(HALO + BLOCK + g, 1), cols] = halo[PW + j : PW + j + 1] * after[j]
    for j in range(PW):
        wide[pl.ds(HALO, BLOCK), j * BLOCK : (j + 1) * BLOCK] = cells[j]
    rows = lax.broadcasted_iota(jnp.int32, (WIDE, 1), 0)
    cols = lax.broadcasted_iota(jnp.int32, (1, SIDE), 1)
    above = (rows < HALO).astype(f32)
    under = (rows >= HALO + BLOCK).astype(f32)
    inside = 1.0 - above * edge_ref[0] - under * edge_ref[1]
    tile_of = cols // BLOCK
    lims = []
    for r in range(3):
        lim = jnp.zeros((1, SIDE), f32)
        for j in range(PW):
            lim = jnp.where(tile_of == j, level_ref[r * PW + j], lim)
        lims.append(lim)
    middle = (1.0 - above) - under
    lim = above * lims[0] + middle * lims[1] + under * lims[2]
    fine, coarse = fine_tau * lim, coarse_tau * lim

    def smooth(x, d):
        def up(y, n):
            return pltpu.roll(y, n % WIDE, 0)

        x = 0.375 * x + 0.25 * (up(x, d) + up(x, -d)) + 0.0625 * (up(x, 2 * d) + up(x, -2 * d))

        def side(y, n):
            keep = cols >= n if n > 0 else cols < SIDE + n
            return jnp.where(keep, pltpu.roll(y, n % SIDE, 1), 0.0)

        return (
            0.375 * x
            + 0.25 * (side(x, d) + side(x, -d))
            + 0.0625 * (side(x, 2 * d) + side(x, -2 * d))
        )

    def shrink(detail, limit):
        return detail - jnp.clip(detail, -limit, limit)

    x = wide[...]
    for _ in range(SWEEPS):
        x = x * inside
        one = smooth(x, 1) * inside
        two = smooth(one, 2)
        x = two + shrink(x - one, fine) + shrink(one - two, coarse)
    sky = x[HALO : HALO + BLOCK]
    sky_ref[...] = sky
    for j in range(PW):
        cells[j] = sky[:, j * BLOCK : (j + 1) * BLOCK]
        for g in range(GROUP):
            part = cells[j, every(g), :].astype(bf16)
            for group in range(8):
                answer_ref[member(group, g), j] = part


def starlet(levels, edges, partial):
    return pl.pallas_call(
        starlet_kernel,
        out_shape=(
            jax.ShapeDtypeStruct((BLOCK, SIDE), f32),
            jax.ShapeDtypeStruct((128, PW, SLICE, BLOCK), bf16),
        ),
        grid_spec=pltpu.PrefetchScalarGridSpec(
            num_scalar_prefetch=2,
            grid=(1,),
            in_specs=[whole(128, TILES_OUT, SLICE, BLOCK)],
            out_specs=[whole(BLOCK, SIDE), whole(128, PW, SLICE, BLOCK)],
            scratch_shapes=[
                pltpu.VMEM((WIDE, SIDE), f32),
                pltpu.VMEM((PW, BLOCK, BLOCK), f32),
            ],
        ),
        compiler_params=pltpu.CompilerParams(vmem_limit_bytes=16 * MIB),
        name="starlet",
    )(levels, edges, partial)


def pick_kernel(target_ref, all_ref, out_ref):
    @pl.loop(0, GROUP)
    def _(source):
        for block in range(32):
            out_ref[source, block] = all_ref[target_ref[source * 32 + block]]


def pick(targets, templates):
    return pl.pallas_call(
        pick_kernel,
        out_shape=jax.ShapeDtypeStruct((GROUP, 32, SLICE, BLOCK), bf16),
        grid_spec=pltpu.PrefetchScalarGridSpec(
            num_scalar_prefetch=1,
            grid=(1,),
            in_specs=[whole(128 * PW, SLICE, BLOCK)],
            out_specs=whole(GROUP, 32, SLICE, BLOCK),
        ),
        compiler_params=pltpu.CompilerParams(vmem_limit_bytes=16 * MIB),
        name="pick",
    )(targets, templates.reshape(128 * PW, SLICE, BLOCK))


def difference_kernel(shifted_ref, template_ref, out_ref, cells):
    for q in range(TILES):
        cols = slice(q * BLOCK, (q + 1) * BLOCK)
        for g in range(GROUP):
            cells[q, every(g), :] = template_ref[g, q].astype(f32)
        out_ref[0, :, cols] = shifted_ref[0, :, cols] - cells[q]


def difference(shifted, returned):
    rows = pl.BlockSpec((1, BLOCK, SIDE), lambda e, p: (e, p, 0))
    return pl.pallas_call(
        difference_kernel,
        out_shape=jax.ShapeDtypeStruct((2, SIDE, SIDE), f32),
        grid=(2, TILES),
        in_specs=[
            rows,
            pl.BlockSpec((GROUP, TILES, SLICE, BLOCK), lambda e, p: (0, e * TILES + p, 0, 0)),
        ],
        out_specs=rows,
        scratch_shapes=[pltpu.VMEM((TILES, BLOCK, BLOCK), f32)],
        compiler_params=pltpu.CompilerParams(vmem_limit_bytes=16 * MIB),
        name="difference",
    )(shifted, returned)


def shards(
    cutouts, vert_taps, horiz_taps, field_coeffs, exposure_weight,
    dest_owner, dest_column, shift_index, threshold_level,
):
    shifted, slices = conv_send(
        dest_owner.reshape(2, 16), dest_column, shift_index, exposure_weight,
        cutouts, vert_taps, horiz_taps, field_coeffs,
    )
    got = lax.all_to_all(slices, NEAR, split_axis=0, concat_axis=0, tiled=True)
    notes = got[:, 32, :3, :32].astype(f32)
    targets = (notes[:, 0] * PW + notes[:, 1]).astype(jnp.int32).reshape(GROUP * 32)
    weights = notes[:, 2].reshape(GROUP * 32)
    sums = combine(targets, weights, got)
    partial = lax.all_to_all(sums, AXES, split_axis=0, concat_axis=0, tiled=True)
    count = lax.axis_size(AXES)
    here = lax.axis_index(AXES)
    levels = threshold_level.astype(f32)
    level_rows = jnp.pad(levels, ((1, 1), (0, 0)))
    near = lax.dynamic_slice(level_rows, (here, 0), (3, PW)).reshape(3 * PW)
    edges = jnp.stack([here == 0, here == count - 1]).astype(f32)
    sky, answers = starlet(near, edges, partial)
    templates = lax.all_to_all(answers, AXES, split_axis=0, concat_axis=0, tiled=True)
    picked = pick(targets, templates)
    returned = lax.all_to_all(picked, NEAR, split_axis=0, concat_axis=0, tiled=True)
    return sky, difference(shifted, returned)


def solution(mesh):
    split = jax.sharding.Mesh(mesh.devices.reshape((2,) * 7), AXES)
    placed = (
        P(AXES, None, None),
        P(AXES, None, None),
        P(AXES, None, None),
        P(AXES, None, None),
        P(AXES),
        P(AXES, None, None),
        P(AXES, None),
        P(AXES, None),
        P(),
    )
    return jax.shard_map(
        shards,
        mesh=split,
        in_specs=placed,
        out_specs=(P(AXES, None), P(AXES, None, None)),
        check_vma=False,
    )
```

```python
import jax
import jax.numpy as jnp
from jax import lax
from jax.experimental import pallas as pl
from jax.experimental.pallas import tpu as pltpu
from jax.sharding import PartitionSpec as P

BLOCK = 128
PW = 4
SWEEPS = 2
SIDE = 512
TILES = 4
KERNELS = 16
TAPS = 21
MARGIN = 10
TOP = 16
HALO = 16
TAIL = 32
HALF = BLOCK // 2
WIDE_K = KERNELS * BLOCK
MAIN_K = KERNELS * HALF
TAIL_K = KERNELS * TAIL
PAD_ROWS = SIDE + 2 * TOP
PAD_COLS = SIDE + BLOCK
WIN_ROWS = BLOCK + TAIL
GROUP = 16
SLICE = BLOCK // GROUP
MIB = 1 << 20
AXES = ("z1", "z0", "y1", "y0", "x1", "x0", "c")
NEAR = ("z0", "y0", "x0", "c")
TILES_OUT = PW + 2

fine_tau = 0.04
coarse_tau = 0.02
f32 = jnp.float32
bf16 = jnp.bfloat16


def member(group, g):
    far = (group >> 2 & 1, group >> 1 & 1, group & 1)
    near = (g >> 3 & 1, g >> 2 & 1, g >> 1 & 1, g & 1)
    bits = (far[0], near[0], far[1], near[1], far[2], near[2], near[3])
    return sum(bit << (6 - i) for i, bit in enumerate(bits))


def every(g):
    return pl.ds(g, SLICE, stride=GROUP)


def lane_of(shape):
    return lax.broadcasted_iota(jnp.int32, shape, len(shape) - 1)


def row_of(shape):
    return lax.broadcasted_iota(jnp.int32, shape, 0)


def placed_taps(taps, first, step):
    shape = (TAPS, BLOCK)
    lanes = (first + step * row_of(shape)) & (BLOCK - 1)
    onto = (lane_of(shape) == lanes).astype(bf16)
    return jnp.dot(taps.astype(bf16), onto, preferred_element_type=f32)


def sloped(rows, k):
    row = jnp.broadcast_to(rows[k : k + 1], (8, BLOCK))
    return pltpu.roll(row, 0, 1, stride=1, stride_axis=0)


def conv_kernel(
    owner_ref, column_ref, shift_ref, weight_ref,
    cut_ref, vert_ref, horiz_ref, coeff_ref,
    shifted_ref, send_ref,
    padded, win, band, base_main, base_tail, cmain, ctail, ab_main, ab_tail, smeared,
    carry, cells,
):
    e = pl.program_id(0)
    step = pl.program_id(1)
    p = TILES - 1 - step
    tile = (8, BLOCK)

    @pl.when((e == 0) & (step == 0))
    def _():
        lanes = lane_of((1, BLOCK))
        owners = jnp.zeros((1, BLOCK), f32)
        columns = jnp.zeros((1, BLOCK), f32)
        for b in range(32):
            owners = jnp.where(lanes == b, owner_ref[b // 16, b % 16].astype(f32), owners)
            columns = jnp.where(lanes == b, column_ref[b // 16, b % 16].astype(f32), columns)
        weights = jnp.where(lanes < 16, weight_ref[0], weight_ref[1])
        rows = row_of(tile)
        note = jnp.where(rows == 0, owners, jnp.where(rows == 1, columns, weights))
        note = note.astype(bf16)
        for g in range(GROUP):
            send_ref[g, 32] = note
        padded[pl.ds(0, TOP), :] = jnp.zeros((TOP, PAD_COLS), bf16)
        padded[pl.ds(TOP + SIDE, TOP), :] = jnp.zeros((TOP, PAD_COLS), bf16)
        band[pl.ds(WIN_ROWS, 256 - WIN_ROWS), :] = jnp.zeros((256 - WIN_ROWS, WIDE_K), bf16)

    @pl.when(step == 0)
    def _():
        image = cut_ref[0]
        wide = jnp.concatenate([image, jnp.zeros((SIDE, BLOCK), f32)], axis=1)
        padded[pl.ds(TOP, SIDE), :] = pltpu.roll(wide, MARGIN, 1).astype(bf16)
        rows_h = placed_taps(horiz_ref[0], BLOCK, -1)
        rows_v = placed_taps(vert_ref[0], TOP - MARGIN, 1)
        lanes, rows = lane_of(tile), row_of(tile)
        for k in range(KERNELS):
            cols = slice(k * BLOCK, (k + 1) * BLOCK)
            slope = sloped(rows_h, k)
            tiles = []
            for i in range(WIN_ROWS // 8):
                part = pltpu.roll(slope, 8 * i % BLOCK, 1) if 8 * i % BLOCK else slope
                if i < 3 or i >= 16:
                    lag = 8 * i + rows - lanes
                    part = jnp.where((lag >= 0) & (lag < TAPS), part, 0.0)
                tiles.append(part)
            band[pl.ds(0, WIN_ROWS), cols] = jnp.concatenate(tiles, axis=0).astype(bf16)
            slope = sloped(rows_v, k)
            pair, quad = k % 2, k % 4
            main_cols = slice(k // 2 * BLOCK, (k // 2 + 1) * BLOCK)
            tail_cols = slice(k // 4 * BLOCK, (k // 4 + 1) * BLOCK)
            for i in range(HALF // 8):
                here = slice(8 * i, 8 * i + 8)
                spot = (8 * i + HALF * pair) % BLOCK
                part = pltpu.roll(slope, spot, 1) if spot else slope
                if pair:
                    part = jnp.where(lanes < HALF, base_main[here, main_cols], part)
                base_main[here, main_cols] = part
                spot = (8 * i + TAIL * quad - HALF) % BLOCK
                part = pltpu.roll(slope, spot, 1) if spot else slope
                if quad:
                    part = jnp.where(lanes < TAIL * quad, base_tail[here, tail_cols], part)
                base_tail[here, tail_cols] = part
            coeff = jnp.broadcast_to(coeff_ref[0][:, k : k + 1], (4, BLOCK))
            spots = lane_of((4, BLOCK))
            held = jnp.where(spots < HALF, cmain[:, main_cols], coeff) if pair else coeff
            cmain[:, main_cols] = held
            held = jnp.where(spots < TAIL * quad, ctail[:, tail_cols], coeff) if quad else coeff
            ctail[:, tail_cols] = held
        for q in range(TILES):
            win[q * PAD_ROWS : (q + 1) * PAD_ROWS, :] = padded[:, q * BLOCK : q * BLOCK + 256]
        for pair in range(KERNELS // 2):
            part = jnp.dot(
                win[...], band[:, pair * 256 : (pair + 1) * 256], preferred_element_type=f32
            ).astype(bf16)
            for q in range(TILES):
                for inner in range(2):
                    smeared[pair * 2 + inner, :, q * BLOCK : (q + 1) * BLOCK] = part[
                        q * PAD_ROWS : (q + 1) * PAD_ROWS, inner * BLOCK : (inner + 1) * BLOCK
                    ]
        carry[...] = jnp.zeros_like(carry)

    cols = lane_of((1, SIDE))
    v = (cols.astype(f32) + 0.5) / SIDE - 0.5
    halves = []
    for half in range(2):
        start = pl.multiple_of(p * BLOCK + half * HALF, HALF)
        u = ((row_of((HALF, 1)) + start).astype(f32) + 0.5) / SIDE - 0.5
        for out, base, coeff in ((ab_main, base_main, cmain), (ab_tail, base_tail, ctail)):
            c0, c1 = coeff[pl.ds(0, 1), :], coeff[pl.ds(1, 1), :]
            c2, c3 = coeff[pl.ds(2, 1), :], coeff[pl.ds(3, 1), :]
            out[half, pl.ds(0, HALF), :] = (base[...] * (c0 + u * c1)).astype(bf16)
            out[half, pl.ds(HALF, HALF), :] = (base[...] * (c2 + u * c3)).astype(bf16)
        main = smeared[:, pl.ds(start, HALF), :].reshape(MAIN_K, SIDE)
        tail = smeared[:, pl.ds(start + HALF, TAIL), :].reshape(TAIL_K, SIDE)
        both = jnp.dot(ab_main[half], main, preferred_element_type=f32)
        both = both + jnp.dot(ab_tail[half], tail, preferred_element_type=f32)
        halves.append(both[:HALF] + v * both[HALF:])
    image = jnp.concatenate(halves, axis=0)

    tile_of = cols // BLOCK
    fx = jnp.zeros((1, SIDE), f32)
    fy = jnp.zeros((1, SIDE), f32)
    for q in range(TILES):
        shift = shift_ref[e, p * TILES + q]
        fx = jnp.where(tile_of == q, ((shift & 3).astype(f32) + 0.5) * 0.25, fx)
        fy = jnp.where(tile_of == q, ((shift >> 2).astype(f32) + 0.5) * 0.25, fy)
    inside = cols < SIDE - 1

    def along(x):
        return (1.0 - fx) * x + fx * jnp.where(inside, pltpu.roll(x, SIDE - 1, 1), 0.0)

    mixed = along(image)
    below_row = along(carry[...])[:1]
    last = row_of((BLOCK, 1)) == BLOCK - 1
    below = jnp.where(last, below_row, pltpu.roll(mixed, BLOCK - 1, 0))
    result = (1.0 - fy) * mixed + fy * below
    carry[...] = image[:8]
    shifted_ref[0] = result
    first_block = e * 16 + p * TILES
    for q in range(TILES):
        cells[q] = result[:, q * BLOCK : (q + 1) * BLOCK]
        for g in range(GROUP):
            send_ref[g, first_block + q] = cells[q, every(g), :].astype(bf16)


def conv_send(owners, columns, shifts, weight, cutouts, vert, horiz, coeffs):
    def by_exposure(*shape):
        return pl.BlockSpec((1,) + shape, lambda e, s, *_: (e,) + (0,) * len(shape))

    return pl.pallas_call(
        conv_kernel,
        out_shape=(
            pltpu.HBM((2, SIDE, SIDE), f32),
            jax.ShapeDtypeStruct((GROUP, 33, SLICE, BLOCK), bf16),
        ),
        grid_spec=pltpu.PrefetchScalarGridSpec(
            num_scalar_prefetch=4,
            grid=(2, TILES),
            in_specs=[
                by_exposure(SIDE, SIDE),
                by_exposure(KERNELS, TAPS),
                by_exposure(KERNELS, TAPS),
                by_exposure(4, KERNELS),
            ],
            out_specs=[
                pl.BlockSpec((1, BLOCK, SIDE), lambda e, s, *_: (e, TILES - 1 - s, 0)),
                pl.BlockSpec((GROUP, 33, SLICE, BLOCK), lambda e, s, *_: (0, 0, 0, 0)),
            ],
            scratch_shapes=[
                pltpu.VMEM((PAD_ROWS, PAD_COLS), bf16),
                pltpu.VMEM((TILES * PAD_ROWS, 256), bf16),
                pltpu.VMEM((256, WIDE_K), bf16),
                pltpu.VMEM((HALF, MAIN_K), f32),
                pltpu.VMEM((HALF, TAIL_K), f32),
                pltpu.VMEM((4, MAIN_K), f32),
                pltpu.VMEM((4, TAIL_K), f32),
                pltpu.VMEM((2, BLOCK, MAIN_K), bf16),
                pltpu.VMEM((2, BLOCK, TAIL_K), bf16),
                pltpu.VMEM((KERNELS, PAD_ROWS, SIDE), bf16),
                pltpu.VMEM((8, SIDE), f32),
                pltpu.VMEM((TILES, BLOCK, BLOCK), f32),
            ],
        ),
        compiler_params=pltpu.CompilerParams(vmem_limit_bytes=48 * MIB),
        name="conv_send",
    )(*(
        pltpu.with_memory_space_constraint(x, pltpu.HBM)
        for x in (owners, columns, shifts, weight, cutouts, vert, horiz, coeffs)
    ))


def whole(*shape):
    return pl.BlockSpec(shape, lambda i, *_: (0,) * len(shape))


def combine_kernel(
    target_ref, w_ref, got_ref, targets_ref, weights_ref, out_ref, even, odd, held
):
    even[...] = jnp.zeros_like(even)
    odd[...] = jnp.zeros_like(odd)
    tile = (SLICE, BLOCK)
    held[0] = jnp.zeros(tile, f32)
    held[129] = jnp.zeros(tile, f32)

    @pl.loop(0, GROUP)
    def _(source):
        for block in range(32):
            index = source * 32 + block
            acc = (even, odd)[block % 2]
            rows = pl.ds(pl.multiple_of((target_ref[index] + PW) * SLICE, SLICE), SLICE)
            acc[rows, :] = acc[rows, :] + w_ref[index] * got_ref[source, block].astype(f32)

    shape = (SLICE, GROUP * 32)
    targets = jnp.broadcast_to(targets_ref[...], shape)
    weights = jnp.broadcast_to(weights_ref[...], shape)
    column = row_of(shape) & 3
    upper = row_of(tile) < PW
    lanes = lane_of(tile)

    @pl.loop(0, 128 // 8)
    def _(turn):
        for i in range(8):
            owner = turn * 8 + i
            hit = jnp.where(targets == owner * PW + column, weights, 0.0)
            total = jnp.broadcast_to(jnp.sum(hit, axis=1, keepdims=True), tile)
            high = total.astype(bf16).astype(f32)
            held[owner + 1] = jnp.where(upper, high, total - high)

    @pl.loop(0, 128 // 8)
    def _(turn):
        for i in range(8):
            owner = turn * 8 + i
            base = pl.multiple_of((owner + 1) * PW * SLICE, PW * SLICE)
            for j in range(PW):
                rows = pl.ds(base + j * SLICE, SLICE)
                out_ref[owner, j] = (even[rows, :] + odd[rows, :]).astype(bf16)
            feet = pl.ds(base - PW * SLICE + SLICE - 1, 2 * PW, stride=SLICE)
            heads = pl.ds(base, 2 * PW, stride=SLICE)
            foot = even[feet, :] + odd[feet, :]
            head = even[heads, :] + odd[heads, :]
            out_ref[owner, PW] = jnp.where(upper, foot, head).astype(bf16)
            near = jnp.where(lanes == 1, held[owner], held[owner + 2])
            out_ref[owner, PW + 1] = jnp.where(lanes == 0, held[owner + 1], near).astype(bf16)


def combine(targets, weights, got):
    return pl.pallas_call(
        combine_kernel,
        out_shape=jax.ShapeDtypeStruct((128, TILES_OUT, SLICE, BLOCK), bf16),
        grid_spec=pltpu.PrefetchScalarGridSpec(
            num_scalar_prefetch=2,
            grid=(1,),
            in_specs=[
                whole(GROUP, 33, SLICE, BLOCK),
                whole(1, GROUP * 32),
                whole(1, GROUP * 32),
            ],
            out_specs=whole(128, TILES_OUT, SLICE, BLOCK),
            scratch_shapes=[pltpu.VMEM((130 * PW * SLICE, BLOCK), f32)] * 2
            + [pltpu.VMEM((130, SLICE, BLOCK), f32)],
        ),
        compiler_params=pltpu.CompilerParams(vmem_limit_bytes=24 * MIB),
        name="combine",
    )(targets, weights, got, targets.reshape(1, -1), weights.reshape(1, -1))


def summed(got_ref, g, j):
    total = got_ref[member(0, g), j].astype(f32)
    for group in range(1, 8):
        total = total + got_ref[member(group, g), j].astype(f32)
    return total


WIDE = BLOCK + 2 * HALO


def starlet_kernel(
    level_ref, edge_ref, got_ref,
    sky_ref, answer_ref, wide, cells,
):
    parts = summed(got_ref, 0, PW + 1)
    inverse = 1.0 / (1.0 + (parts + pltpu.roll(parts, PW, 0)))
    own, before, after = (
        [jnp.broadcast_to(inverse[j : j + 1, i : i + 1], (1, BLOCK)) for j in range(PW)]
        for i in range(3)
    )
    for g in range(GROUP):
        halo = summed(got_ref, g, PW)
        for j in range(PW):
            cols = slice(j * BLOCK, (j + 1) * BLOCK)
            cells[j, every(g), :] = summed(got_ref, g, j) * own[j]
            wide[pl.ds(g, 1), cols] = halo[j : j + 1] * before[j]
            wide[pl.ds(HALO + BLOCK + g, 1), cols] = halo[PW + j : PW + j + 1] * after[j]
    for j in range(PW):
        wide[pl.ds(HALO, BLOCK), j * BLOCK : (j + 1) * BLOCK] = cells[j]
    rows = lax.broadcasted_iota(jnp.int32, (WIDE, 1), 0)
    cols = lax.broadcasted_iota(jnp.int32, (1, SIDE), 1)
    above = (rows < HALO).astype(f32)
    under = (rows >= HALO + BLOCK).astype(f32)
    inside = 1.0 - above * edge_ref[0] - under * edge_ref[1]
    tile_of = cols // BLOCK
    lims = []
    for r in range(3):
        lim = jnp.zeros((1, SIDE), f32)
        for j in range(PW):
            lim = jnp.where(tile_of == j, level_ref[r * PW + j], lim)
        lims.append(lim)
    middle = (1.0 - above) - under
    lim = above * lims[0] + middle * lims[1] + under * lims[2]
    fine, coarse = fine_tau * lim, coarse_tau * lim

    def smooth(x, d):
        def up(y, n):
            return pltpu.roll(y, n % WIDE, 0)

        x = 0.375 * x + 0.25 * (up(x, d) + up(x, -d)) + 0.0625 * (up(x, 2 * d) + up(x, -2 * d))

        def side(y, n):
            keep = cols >= n if n > 0 else cols < SIDE + n
            return jnp.where(keep, pltpu.roll(y, n % SIDE, 1), 0.0)

        return (
            0.375 * x
            + 0.25 * (side(x, d) + side(x, -d))
            + 0.0625 * (side(x, 2 * d) + side(x, -2 * d))
        )

    def shrink(detail, limit):
        return detail - jnp.clip(detail, -limit, limit)

    x = wide[...]
    for _ in range(SWEEPS):
        x = x * inside
        one = smooth(x, 1) * inside
        two = smooth(one, 2)
        x = two + shrink(x - one, fine) + shrink(one - two, coarse)
    sky = x[HALO : HALO + BLOCK]
    sky_ref[...] = sky
    for j in range(PW):
        cells[j] = sky[:, j * BLOCK : (j + 1) * BLOCK]
        for g in range(GROUP):
            part = cells[j, every(g), :].astype(bf16)
            for group in range(8):
                answer_ref[member(group, g), j] = part


def starlet(levels, edges, partial):
    return pl.pallas_call(
        starlet_kernel,
        out_shape=(
            jax.ShapeDtypeStruct((BLOCK, SIDE), f32),
            jax.ShapeDtypeStruct((128, PW, SLICE, BLOCK), bf16),
        ),
        grid_spec=pltpu.PrefetchScalarGridSpec(
            num_scalar_prefetch=2,
            grid=(1,),
            in_specs=[whole(128, TILES_OUT, SLICE, BLOCK)],
            out_specs=[whole(BLOCK, SIDE), whole(128, PW, SLICE, BLOCK)],
            scratch_shapes=[
                pltpu.VMEM((WIDE, SIDE), f32),
                pltpu.VMEM((PW, BLOCK, BLOCK), f32),
            ],
        ),
        compiler_params=pltpu.CompilerParams(vmem_limit_bytes=16 * MIB),
        name="starlet",
    )(levels, edges, partial)


def pick_kernel(target_ref, all_ref, out_ref):
    @pl.loop(0, GROUP)
    def _(source):
        for block in range(32):
            out_ref[source, block] = all_ref[target_ref[source * 32 + block]]


def pick(targets, templates):
    return pl.pallas_call(
        pick_kernel,
        out_shape=jax.ShapeDtypeStruct((GROUP, 32, SLICE, BLOCK), bf16),
        grid_spec=pltpu.PrefetchScalarGridSpec(
            num_scalar_prefetch=1,
            grid=(1,),
            in_specs=[whole(128 * PW, SLICE, BLOCK)],
            out_specs=whole(GROUP, 32, SLICE, BLOCK),
        ),
        compiler_params=pltpu.CompilerParams(vmem_limit_bytes=16 * MIB),
        name="pick",
    )(targets, templates.reshape(128 * PW, SLICE, BLOCK))


def difference_kernel(shifted_ref, template_ref, out_ref, cells):
    for q in range(TILES):
        cols = slice(q * BLOCK, (q + 1) * BLOCK)
        for g in range(GROUP):
            cells[q, every(g), :] = template_ref[g, q].astype(f32)
        out_ref[0, :, cols] = shifted_ref[0, :, cols] - cells[q]


def difference(shifted, returned):
    rows = pl.BlockSpec((1, BLOCK, SIDE), lambda e, p: (e, p, 0))
    return pl.pallas_call(
        difference_kernel,
        out_shape=jax.ShapeDtypeStruct((2, SIDE, SIDE), f32),
        grid=(2, TILES),
        in_specs=[
            rows,
            pl.BlockSpec((GROUP, TILES, SLICE, BLOCK), lambda e, p: (0, e * TILES + p, 0, 0)),
        ],
        out_specs=rows,
        scratch_shapes=[pltpu.VMEM((TILES, BLOCK, BLOCK), f32)],
        compiler_params=pltpu.CompilerParams(vmem_limit_bytes=16 * MIB),
        name="difference",
    )(shifted, returned)


def shards(
    cutouts, vert_taps, horiz_taps, field_coeffs, exposure_weight,
    dest_owner, dest_column, shift_index, threshold_level,
):
    shifted, slices = conv_send(
        dest_owner.reshape(2, 16), dest_column, shift_index, exposure_weight,
        cutouts, vert_taps, horiz_taps, field_coeffs,
    )
    got = lax.all_to_all(slices, NEAR, split_axis=0, concat_axis=0, tiled=True)
    notes = got[:, 32, :3, :32].astype(f32)
    targets = (notes[:, 0] * PW + notes[:, 1]).astype(jnp.int32).reshape(GROUP * 32)
    weights = notes[:, 2].reshape(GROUP * 32)
    sums = combine(targets, weights, got)
    partial = lax.all_to_all(sums, AXES, split_axis=0, concat_axis=0, tiled=True)
    count = lax.axis_size(AXES)
    here = lax.axis_index(AXES)
    levels = threshold_level.astype(f32)
    level_rows = jnp.pad(levels, ((1, 1), (0, 0)))
    near = lax.dynamic_slice(level_rows, (here, 0), (3, PW)).reshape(3 * PW)
    edges = jnp.stack([here == 0, here == count - 1]).astype(f32)
    sky, answers = starlet(near, edges, partial)
    templates = lax.all_to_all(answers, AXES, split_axis=0, concat_axis=0, tiled=True)
    picked = pick(targets, templates)
    returned = lax.all_to_all(picked, NEAR, split_axis=0, concat_axis=0, tiled=True)
    return sky, difference(shifted, returned)


def solution(mesh):
    split = jax.sharding.Mesh(mesh.devices.reshape((2,) * 7), AXES)
    placed = (
        P(AXES, None, None),
        P(AXES, None, None),
        P(AXES, None, None),
        P(AXES, None, None),
        P(AXES),
        P(AXES, None, None),
        P(AXES, None),
        P(AXES, None),
        P(),
    )
    return jax.shard_map(
        shards,
        mesh=split,
        in_specs=placed,
        out_specs=(P(AXES, None), P(AXES, None, None)),
        check_vma=False,
    )
```

```python
import jax
import jax.numpy as jnp
from jax import lax
from jax.experimental import pallas as pl
from jax.experimental.pallas import tpu as pltpu
from jax.sharding import PartitionSpec as P

BLOCK = 128
PW = 4
SWEEPS = 2
SIDE = 512
TILES = 4
KERNELS = 16
TAPS = 21
MARGIN = 10
TOP = 16
HALO = 16
TAIL = 32
HALF = BLOCK // 2
WIDE_K = KERNELS * BLOCK
MAIN_K = KERNELS * HALF
TAIL_K = KERNELS * TAIL
PAD_ROWS = SIDE + 2 * TOP
PAD_COLS = SIDE + BLOCK
WIN_ROWS = BLOCK + TAIL
GROUP = 32
GROUPS = 4
SLICE = BLOCK // GROUP
MIB = 1 << 20
AXES = ("z1", "z0", "y1", "y0", "x1", "x0", "c")
NEAR = ("z0", "y0", "x1", "x0", "c")
TILES_OUT = PW + 2

fine_tau = 0.04
coarse_tau = 0.02
f32 = jnp.float32
bf16 = jnp.bfloat16


def member(group, g):
    near = (g >> 4 & 1, g >> 3 & 1, g & 7)
    return (group >> 1 & 1) << 6 | near[0] << 5 | (group & 1) << 4 | near[1] << 3 | near[2]


def every(g):
    return pl.ds(g, SLICE, stride=GROUP)


def lane_of(shape):
    return lax.broadcasted_iota(jnp.int32, shape, len(shape) - 1)


def row_of(shape):
    return lax.broadcasted_iota(jnp.int32, shape, 0)


def placed_taps(taps, first, step):
    shape = (TAPS, BLOCK)
    lanes = (first + step * row_of(shape)) & (BLOCK - 1)
    onto = (lane_of(shape) == lanes).astype(bf16)
    return jnp.dot(taps.astype(bf16), onto, preferred_element_type=f32)


def sloped(rows, k):
    row = jnp.broadcast_to(rows[k : k + 1], (8, BLOCK))
    return pltpu.roll(row, 0, 1, stride=1, stride_axis=0)


def conv_kernel(
    owner_ref, column_ref, shift_ref, weight_ref,
    cut_ref, vert_ref, horiz_ref, coeff_ref,
    shifted_ref, send_ref,
    padded, win, band, base_main, base_tail, cmain, ctail, ab_main, ab_tail, smeared,
    carry, cells,
):
    e = pl.program_id(0)
    step = pl.program_id(1)
    p = TILES - 1 - step
    tile = (8, BLOCK)

    @pl.when((e == 0) & (step == 0))
    def _():
        lanes = lane_of((1, BLOCK))
        owners = jnp.zeros((1, BLOCK), f32)
        columns = jnp.zeros((1, BLOCK), f32)
        for b in range(32):
            owners = jnp.where(lanes == b, owner_ref[b // 16, b % 16].astype(f32), owners)
            columns = jnp.where(lanes == b, column_ref[b // 16, b % 16].astype(f32), columns)
        weights = jnp.where(lanes < 16, weight_ref[0], weight_ref[1])
        rows = row_of((SLICE, BLOCK))
        note = jnp.where(rows == 0, owners, jnp.where(rows == 1, columns, weights))
        note = note.astype(bf16)
        for g in range(GROUP):
            send_ref[g, 32] = note
        padded[pl.ds(0, TOP), :] = jnp.zeros((TOP, PAD_COLS), bf16)
        padded[pl.ds(TOP + SIDE, TOP), :] = jnp.zeros((TOP, PAD_COLS), bf16)
        band[pl.ds(WIN_ROWS, 256 - WIN_ROWS), :] = jnp.zeros((256 - WIN_ROWS, WIDE_K), bf16)

    @pl.when(step == 0)
    def _():
        image = cut_ref[0]
        wide = jnp.concatenate([image, jnp.zeros((SIDE, BLOCK), f32)], axis=1)
        padded[pl.ds(TOP, SIDE), :] = pltpu.roll(wide, MARGIN, 1).astype(bf16)
        rows_h = placed_taps(horiz_ref[0], BLOCK, -1)
        rows_v = placed_taps(vert_ref[0], TOP - MARGIN, 1)
        lanes, rows = lane_of(tile), row_of(tile)
        for k in range(KERNELS):
            cols = slice(k * BLOCK, (k + 1) * BLOCK)
            slope = sloped(rows_h, k)
            tiles = []
            for i in range(WIN_ROWS // 8):
                part = pltpu.roll(slope, 8 * i % BLOCK, 1) if 8 * i % BLOCK else slope
                if i < 3 or i >= 16:
                    lag = 8 * i + rows - lanes
                    part = jnp.where((lag >= 0) & (lag < TAPS), part, 0.0)
                tiles.append(part)
            band[pl.ds(0, WIN_ROWS), cols] = jnp.concatenate(tiles, axis=0).astype(bf16)
            slope = sloped(rows_v, k)
            pair, quad = k % 2, k % 4
            main_cols = slice(k // 2 * BLOCK, (k // 2 + 1) * BLOCK)
            tail_cols = slice(k // 4 * BLOCK, (k // 4 + 1) * BLOCK)
            for i in range(HALF // 8):
                here = slice(8 * i, 8 * i + 8)
                spot = (8 * i + HALF * pair) % BLOCK
                part = pltpu.roll(slope, spot, 1) if spot else slope
                if pair:
                    part = jnp.where(lanes < HALF, base_main[here, main_cols], part)
                base_main[here, main_cols] = part
                spot = (8 * i + TAIL * quad - HALF) % BLOCK
                part = pltpu.roll(slope, spot, 1) if spot else slope
                if quad:
                    part = jnp.where(lanes < TAIL * quad, base_tail[here, tail_cols], part)
                base_tail[here, tail_cols] = part
            coeff = jnp.broadcast_to(coeff_ref[0][:, k : k + 1], (4, BLOCK))
            spots = lane_of((4, BLOCK))
            held = jnp.where(spots < HALF, cmain[:, main_cols], coeff) if pair else coeff
            cmain[:, main_cols] = held
            held = jnp.where(spots < TAIL * quad, ctail[:, tail_cols], coeff) if quad else coeff
            ctail[:, tail_cols] = held
        for q in range(TILES):
            win[q * PAD_ROWS : (q + 1) * PAD_ROWS, :] = padded[:, q * BLOCK : q * BLOCK + 256]
        for pair in range(KERNELS // 2):
            part = jnp.dot(
                win[...], band[:, pair * 256 : (pair + 1) * 256], preferred_element_type=f32
            ).astype(bf16)
            for q in range(TILES):
                for inner in range(2):
                    smeared[pair * 2 + inner, :, q * BLOCK : (q + 1) * BLOCK] = part[
                        q * PAD_ROWS : (q + 1) * PAD_ROWS, inner * BLOCK : (inner + 1) * BLOCK
                    ]
        carry[...] = jnp.zeros_like(carry)

    cols = lane_of((1, SIDE))
    v = (cols.astype(f32) + 0.5) / SIDE - 0.5
    halves = []
    for half in range(2):
        start = pl.multiple_of(p * BLOCK + half * HALF, HALF)
        u = ((row_of((HALF, 1)) + start).astype(f32) + 0.5) / SIDE - 0.5
        for out, base, coeff in ((ab_main, base_main, cmain), (ab_tail, base_tail, ctail)):
            c0, c1 = coeff[pl.ds(0, 1), :], coeff[pl.ds(1, 1), :]
            c2, c3 = coeff[pl.ds(2, 1), :], coeff[pl.ds(3, 1), :]
            out[half, pl.ds(0, HALF), :] = (base[...] * (c0 + u * c1)).astype(bf16)
            out[half, pl.ds(HALF, HALF), :] = (base[...] * (c2 + u * c3)).astype(bf16)
        main = smeared[:, pl.ds(start, HALF), :].reshape(MAIN_K, SIDE)
        tail = smeared[:, pl.ds(start + HALF, TAIL), :].reshape(TAIL_K, SIDE)
        both = jnp.dot(ab_main[half], main, preferred_element_type=f32)
        both = both + jnp.dot(ab_tail[half], tail, preferred_element_type=f32)
        halves.append(both[:HALF] + v * both[HALF:])
    image = jnp.concatenate(halves, axis=0)

    tile_of = cols // BLOCK
    fx = jnp.zeros((1, SIDE), f32)
    fy = jnp.zeros((1, SIDE), f32)
    for q in range(TILES):
        shift = shift_ref[e, p * TILES + q]
        fx = jnp.where(tile_of == q, ((shift & 3).astype(f32) + 0.5) * 0.25, fx)
        fy = jnp.where(tile_of == q, ((shift >> 2).astype(f32) + 0.5) * 0.25, fy)
    inside = cols < SIDE - 1

    def along(x):
        return (1.0 - fx) * x + fx * jnp.where(inside, pltpu.roll(x, SIDE - 1, 1), 0.0)

    mixed = along(image)
    below_row = along(carry[...])[:1]
    last = row_of((BLOCK, 1)) == BLOCK - 1
    below = jnp.where(last, below_row, pltpu.roll(mixed, BLOCK - 1, 0))
    result = (1.0 - fy) * mixed + fy * below
    carry[...] = image[:8]
    shifted_ref[0] = result
    first_block = e * 16 + p * TILES
    for q in range(TILES):
        cells[q] = result[:, q * BLOCK : (q + 1) * BLOCK]
        for g in range(GROUP):
            send_ref[g, first_block + q] = cells[q, every(g), :].astype(bf16)


def conv_send(owners, columns, shifts, weight, cutouts, vert, horiz, coeffs):
    def by_exposure(*shape):
        return pl.BlockSpec((1,) + shape, lambda e, s, *_: (e,) + (0,) * len(shape))

    return pl.pallas_call(
        conv_kernel,
        out_shape=(
            pltpu.HBM((2, SIDE, SIDE), f32),
            jax.ShapeDtypeStruct((GROUP, 33, SLICE, BLOCK), bf16),
        ),
        grid_spec=pltpu.PrefetchScalarGridSpec(
            num_scalar_prefetch=4,
            grid=(2, TILES),
            in_specs=[
                by_exposure(SIDE, SIDE),
                by_exposure(KERNELS, TAPS),
                by_exposure(KERNELS, TAPS),
                by_exposure(4, KERNELS),
            ],
            out_specs=[
                pl.BlockSpec((1, BLOCK, SIDE), lambda e, s, *_: (e, TILES - 1 - s, 0)),
                pl.BlockSpec((GROUP, 33, SLICE, BLOCK), lambda e, s, *_: (0, 0, 0, 0)),
            ],
            scratch_shapes=[
                pltpu.VMEM((PAD_ROWS, PAD_COLS), bf16),
                pltpu.VMEM((TILES * PAD_ROWS, 256), bf16),
                pltpu.VMEM((256, WIDE_K), bf16),
                pltpu.VMEM((HALF, MAIN_K), f32),
                pltpu.VMEM((HALF, TAIL_K), f32),
                pltpu.VMEM((4, MAIN_K), f32),
                pltpu.VMEM((4, TAIL_K), f32),
                pltpu.VMEM((2, BLOCK, MAIN_K), bf16),
                pltpu.VMEM((2, BLOCK, TAIL_K), bf16),
                pltpu.VMEM((KERNELS, PAD_ROWS, SIDE), bf16),
                pltpu.VMEM((8, SIDE), f32),
                pltpu.VMEM((TILES, BLOCK, BLOCK), f32),
            ],
        ),
        compiler_params=pltpu.CompilerParams(vmem_limit_bytes=48 * MIB),
        name="conv_send",
    )(*(
        pltpu.with_memory_space_constraint(x, pltpu.HBM)
        for x in (owners, columns, shifts, weight, cutouts, vert, horiz, coeffs)
    ))


def whole(*shape):
    return pl.BlockSpec(shape, lambda i, *_: (0,) * len(shape))


def combine_kernel(
    target_ref, w_ref, side_ref, got_ref, targets_ref, weights_ref, out_ref, even, odd, held
):
    even[...] = jnp.zeros_like(even)
    odd[...] = jnp.zeros_like(odd)
    tile = (SLICE, BLOCK)
    held[0] = jnp.zeros(tile, f32)
    held[129] = jnp.zeros(tile, f32)

    @pl.loop(0, GROUP)
    def _(source):
        for block in range(32):
            index = source * 32 + block
            acc, spot = (even, odd)[block % 2], target_ref[index] + PW
            acc[spot] = acc[spot] + w_ref[index] * got_ref[source, block].astype(f32)

    shape = (SLICE, GROUP * 32)
    targets = jnp.broadcast_to(targets_ref[...], shape) - row_of(shape)
    weights = jnp.broadcast_to(weights_ref[...], shape)
    lanes = lane_of(tile)
    kind = jnp.where(lanes < 3, lanes, lanes - 3)
    feet = side_ref[0] == 1

    @pl.loop(0, 128 // 8)
    def _(turn):
        for i in range(8):
            owner = turn * 8 + i
            hit = jnp.where(targets == owner * PW, weights, 0.0)
            held[owner + 1] = jnp.broadcast_to(jnp.sum(hit, axis=1, keepdims=True), tile)

    @pl.loop(0, 128 // 8)
    def _(turn):
        for i in range(8):
            owner = turn * 8 + i
            for j in range(PW):
                spot = (owner + 1) * PW + j
                out_ref[owner, j] = (even[spot] + odd[spot]).astype(bf16)
            beside = pl.ds(owner * PW + jnp.where(feet, 0, 2 * PW), PW)
            foot = even[beside, SLICE - 1, :] + odd[beside, SLICE - 1, :]
            head = even[beside, 0, :] + odd[beside, 0, :]
            out_ref[owner, PW] = jnp.where(feet, foot, head).astype(bf16)
            near = jnp.where(kind == 1, held[owner], held[owner + 2])
            total = jnp.where(kind == 0, held[owner + 1], near)
            high = total.astype(bf16).astype(f32)
            out_ref[owner, PW + 1] = jnp.where(lanes < 3, high, total - high).astype(bf16)


def combine(targets, weights, side, got):
    return pl.pallas_call(
        combine_kernel,
        out_shape=jax.ShapeDtypeStruct((128, TILES_OUT, SLICE, BLOCK), bf16),
        grid_spec=pltpu.PrefetchScalarGridSpec(
            num_scalar_prefetch=3,
            grid=(1,),
            in_specs=[
                whole(GROUP, 33, SLICE, BLOCK),
                whole(1, GROUP * 32),
                whole(1, GROUP * 32),
            ],
            out_specs=whole(128, TILES_OUT, SLICE, BLOCK),
            scratch_shapes=[pltpu.VMEM((130 * PW, SLICE, BLOCK), f32)] * 2
            + [pltpu.VMEM((130, SLICE, BLOCK), f32)],
        ),
        compiler_params=pltpu.CompilerParams(vmem_limit_bytes=24 * MIB),
        name="combine",
    )(targets, weights, side, got, targets.reshape(1, -1), weights.reshape(1, -1))


def summed(got_ref, g, j):
    total = got_ref[member(0, g), j].astype(f32)
    for group in range(1, GROUPS):
        total = total + got_ref[member(group, g), j].astype(f32)
    return total


WIDE = BLOCK + 2 * HALO


def starlet_kernel(
    level_ref, edge_ref, got_ref,
    sky_ref, answer_ref, wide, cells,
):
    parts = summed(got_ref, 0, PW + 1)
    inverse = 1.0 / (1.0 + (parts + pltpu.roll(parts, BLOCK - 3, 1)))
    own, before, after = (
        [jnp.broadcast_to(inverse[j : j + 1, i : i + 1], (1, BLOCK)) for j in range(PW)]
        for i in range(3)
    )
    for g in range(GROUP):
        halo = summed(got_ref, g, PW)
        for j in range(PW):
            cols = slice(j * BLOCK, (j + 1) * BLOCK)
            cells[j, every(g), :] = summed(got_ref, g, j) * own[j]
            if g < HALO:
                wide[pl.ds(HALO + BLOCK + g, 1), cols] = halo[j : j + 1] * after[j]
            else:
                wide[pl.ds(g - HALO, 1), cols] = halo[j : j + 1] * before[j]
    for j in range(PW):
        wide[pl.ds(HALO, BLOCK), j * BLOCK : (j + 1) * BLOCK] = cells[j]
    rows = lax.broadcasted_iota(jnp.int32, (WIDE, 1), 0)
    cols = lax.broadcasted_iota(jnp.int32, (1, SIDE), 1)
    above = (rows < HALO).astype(f32)
    under = (rows >= HALO + BLOCK).astype(f32)
    inside = 1.0 - above * edge_ref[0] - under * edge_ref[1]
    tile_of = cols // BLOCK
    lims = []
    for r in range(3):
        lim = jnp.zeros((1, SIDE), f32)
        for j in range(PW):
            lim = jnp.where(tile_of == j, level_ref[r * PW + j], lim)
        lims.append(lim)
    middle = (1.0 - above) - under
    lim = above * lims[0] + middle * lims[1] + under * lims[2]
    fine, coarse = fine_tau * lim, coarse_tau * lim

    def smooth(x, d):
        def up(y, n):
            return pltpu.roll(y, n % WIDE, 0)

        x = 0.375 * x + 0.25 * (up(x, d) + up(x, -d)) + 0.0625 * (up(x, 2 * d) + up(x, -2 * d))

        def side(y, n):
            keep = cols >= n if n > 0 else cols < SIDE + n
            return jnp.where(keep, pltpu.roll(y, n % SIDE, 1), 0.0)

        return (
            0.375 * x
            + 0.25 * (side(x, d) + side(x, -d))
            + 0.0625 * (side(x, 2 * d) + side(x, -2 * d))
        )

    def shrink(detail, limit):
        return detail - jnp.clip(detail, -limit, limit)

    x = wide[...]
    for _ in range(SWEEPS):
        x = x * inside
        one = smooth(x, 1) * inside
        two = smooth(one, 2)
        x = two + shrink(x - one, fine) + shrink(one - two, coarse)
    sky = x[HALO : HALO + BLOCK]
    sky_ref[...] = sky
    for j in range(PW):
        cells[j] = sky[:, j * BLOCK : (j + 1) * BLOCK]
        for g in range(GROUP):
            part = cells[j, every(g), :].astype(bf16)
            for group in range(GROUPS):
                answer_ref[member(group, g), j] = part


def starlet(levels, edges, partial):
    return pl.pallas_call(
        starlet_kernel,
        out_shape=(
            jax.ShapeDtypeStruct((BLOCK, SIDE), f32),
            jax.ShapeDtypeStruct((128, PW, SLICE, BLOCK), bf16),
        ),
        grid_spec=pltpu.PrefetchScalarGridSpec(
            num_scalar_prefetch=2,
            grid=(1,),
            in_specs=[whole(128, TILES_OUT, SLICE, BLOCK)],
            out_specs=[whole(BLOCK, SIDE), whole(128, PW, SLICE, BLOCK)],
            scratch_shapes=[
                pltpu.VMEM((WIDE, SIDE), f32),
                pltpu.VMEM((PW, BLOCK, BLOCK), f32),
            ],
        ),
        compiler_params=pltpu.CompilerParams(vmem_limit_bytes=16 * MIB),
        name="starlet",
    )(levels, edges, partial)


def pick_kernel(target_ref, all_ref, out_ref):
    @pl.loop(0, GROUP)
    def _(source):
        for block in range(32):
            out_ref[source, block] = all_ref[target_ref[source * 32 + block]]


def pick(targets, templates):
    return pl.pallas_call(
        pick_kernel,
        out_shape=jax.ShapeDtypeStruct((GROUP, 32, SLICE, BLOCK), bf16),
        grid_spec=pltpu.PrefetchScalarGridSpec(
            num_scalar_prefetch=1,
            grid=(1,),
            in_specs=[whole(128 * PW, SLICE, BLOCK)],
            out_specs=whole(GROUP, 32, SLICE, BLOCK),
        ),
        compiler_params=pltpu.CompilerParams(vmem_limit_bytes=16 * MIB),
        name="pick",
    )(targets, templates.reshape(128 * PW, SLICE, BLOCK))


def difference_kernel(shifted_ref, template_ref, out_ref, cells):
    for q in range(TILES):
        cols = slice(q * BLOCK, (q + 1) * BLOCK)
        for g in range(GROUP):
            cells[q, every(g), :] = template_ref[g, q].astype(f32)
        out_ref[0, :, cols] = shifted_ref[0, :, cols] - cells[q]


def difference(shifted, returned):
    rows = pl.BlockSpec((1, BLOCK, SIDE), lambda e, p: (e, p, 0))
    return pl.pallas_call(
        difference_kernel,
        out_shape=jax.ShapeDtypeStruct((2, SIDE, SIDE), f32),
        grid=(2, TILES),
        in_specs=[
            rows,
            pl.BlockSpec((GROUP, TILES, SLICE, BLOCK), lambda e, p: (0, e * TILES + p, 0, 0)),
        ],
        out_specs=rows,
        scratch_shapes=[pltpu.VMEM((TILES, BLOCK, BLOCK), f32)],
        compiler_params=pltpu.CompilerParams(vmem_limit_bytes=16 * MIB),
        name="difference",
    )(shifted, returned)


def shards(
    cutouts, vert_taps, horiz_taps, field_coeffs, exposure_weight,
    dest_owner, dest_column, shift_index, threshold_level,
):
    shifted, slices = conv_send(
        dest_owner.reshape(2, 16), dest_column, shift_index, exposure_weight,
        cutouts, vert_taps, horiz_taps, field_coeffs,
    )
    got = lax.all_to_all(slices, NEAR, split_axis=0, concat_axis=0, tiled=True)
    notes = got[:, 32, :3, :32].astype(f32)
    targets = (notes[:, 0] * PW + notes[:, 1]).astype(jnp.int32).reshape(GROUP * 32)
    weights = notes[:, 2].reshape(GROUP * 32)
    side = lax.axis_index("z0").reshape(1)
    sums = combine(targets, weights, side, got)
    partial = lax.all_to_all(sums, AXES, split_axis=0, concat_axis=0, tiled=True)
    count = lax.axis_size(AXES)
    here = lax.axis_index(AXES)
    levels = threshold_level.astype(f32)
    level_rows = jnp.pad(levels, ((1, 1), (0, 0)))
    near = lax.dynamic_slice(level_rows, (here, 0), (3, PW)).reshape(3 * PW)
    edges = jnp.stack([here == 0, here == count - 1]).astype(f32)
    sky, answers = starlet(near, edges, partial)
    templates = lax.all_to_all(answers, AXES, split_axis=0, concat_axis=0, tiled=True)
    picked = pick(targets, templates)
    returned = lax.all_to_all(picked, NEAR, split_axis=0, concat_axis=0, tiled=True)
    return sky, difference(shifted, returned)


def solution(mesh):
    split = jax.sharding.Mesh(mesh.devices.reshape((2,) * 7), AXES)
    placed = (
        P(AXES, None, None),
        P(AXES, None, None),
        P(AXES, None, None),
        P(AXES, None, None),
        P(AXES),
        P(AXES, None, None),
        P(AXES, None),
        P(AXES, None),
        P(),
    )
    return jax.shard_map(
        shards,
        mesh=split,
        in_specs=placed,
        out_specs=(P(AXES, None), P(AXES, None, None)),
        check_vma=False,
    )
```

```python
import jax
import jax.numpy as jnp
from jax import lax
from jax.experimental import pallas as pl
from jax.experimental.pallas import tpu as pltpu
from jax.sharding import PartitionSpec as P

BLOCK = 128
PW = 4
SWEEPS = 2
SIDE = 512
TILES = 4
KERNELS = 16
TAPS = 21
MARGIN = 10
TOP = 16
HALO = 16
TAIL = 32
HALF = BLOCK // 2
WIDE_K = KERNELS * BLOCK
MAIN_K = KERNELS * HALF
TAIL_K = KERNELS * TAIL
PAD_ROWS = SIDE + 2 * TOP
PAD_COLS = SIDE + BLOCK
WIN_ROWS = BLOCK + TAIL
GROUP = 32
GROUPS = 4
SLICE = BLOCK // GROUP
MIB = 1 << 20
AXES = ("z1", "z0", "y1", "y0", "x1", "x0", "c")
NEAR = ("z0", "y0", "x1", "x0", "c")
TILES_OUT = PW + 2

fine_tau = 0.04
coarse_tau = 0.02
f32 = jnp.float32
bf16 = jnp.bfloat16


def member(group, g):
    near = (g >> 4 & 1, g >> 3 & 1, g & 7)
    return (group >> 1 & 1) << 6 | near[0] << 5 | (group & 1) << 4 | near[1] << 3 | near[2]


def every(g):
    return pl.ds(g, SLICE, stride=GROUP)


def lane_of(shape):
    return lax.broadcasted_iota(jnp.int32, shape, len(shape) - 1)


def row_of(shape):
    return lax.broadcasted_iota(jnp.int32, shape, 0)


def placed_taps(taps, first, step):
    shape = (TAPS, BLOCK)
    lanes = (first + step * row_of(shape)) & (BLOCK - 1)
    onto = (lane_of(shape) == lanes).astype(bf16)
    return jnp.dot(taps.astype(bf16), onto, preferred_element_type=f32)


def sloped(rows, k):
    row = jnp.broadcast_to(rows[k : k + 1], (8, BLOCK))
    return pltpu.roll(row, 0, 1, stride=1, stride_axis=0)


def conv_kernel(
    owner_ref, column_ref, shift_ref, weight_ref,
    cut_ref, vert_ref, horiz_ref, coeff_ref,
    shifted_ref, send_ref,
    padded, win, band, base_main, base_tail, cmain, ctail, ab_main, ab_tail, smeared,
    carry, cells,
):
    e = pl.program_id(0)
    step = pl.program_id(1)
    p = TILES - 1 - step
    tile = (8, BLOCK)

    @pl.when((e == 0) & (step == 0))
    def _():
        lanes = lane_of((1, BLOCK))
        owners = jnp.zeros((1, BLOCK), f32)
        columns = jnp.zeros((1, BLOCK), f32)
        for b in range(32):
            owners = jnp.where(lanes == b, owner_ref[b // 16, b % 16].astype(f32), owners)
            columns = jnp.where(lanes == b, column_ref[b // 16, b % 16].astype(f32), columns)
        weights = jnp.where(lanes < 16, weight_ref[0], weight_ref[1])
        rows = row_of((SLICE, BLOCK))
        note = jnp.where(rows == 0, owners, jnp.where(rows == 1, columns, weights))
        note = note.astype(bf16)
        for g in range(GROUP):
            send_ref[g, 32] = note
        padded[pl.ds(0, TOP), :] = jnp.zeros((TOP, PAD_COLS), bf16)
        padded[pl.ds(TOP + SIDE, TOP), :] = jnp.zeros((TOP, PAD_COLS), bf16)
        band[pl.ds(WIN_ROWS, 256 - WIN_ROWS), :] = jnp.zeros((256 - WIN_ROWS, WIDE_K), bf16)

    @pl.when(step == 0)
    def _():
        image = cut_ref[0]
        wide = jnp.concatenate([image, jnp.zeros((SIDE, BLOCK), f32)], axis=1)
        padded[pl.ds(TOP, SIDE), :] = pltpu.roll(wide, MARGIN, 1).astype(bf16)
        rows_h = placed_taps(horiz_ref[0], BLOCK, -1)
        rows_v = placed_taps(vert_ref[0], TOP - MARGIN, 1)
        lanes, rows = lane_of(tile), row_of(tile)
        for k in range(KERNELS):
            cols = slice(k * BLOCK, (k + 1) * BLOCK)
            slope = sloped(rows_h, k)
            tiles = []
            for i in range(WIN_ROWS // 8):
                part = pltpu.roll(slope, 8 * i % BLOCK, 1) if 8 * i % BLOCK else slope
                if i < 3 or i >= 16:
                    lag = 8 * i + rows - lanes
                    part = jnp.where((lag >= 0) & (lag < TAPS), part, 0.0)
                tiles.append(part)
            band[pl.ds(0, WIN_ROWS), cols] = jnp.concatenate(tiles, axis=0).astype(bf16)
            slope = sloped(rows_v, k)
            pair, quad = k % 2, k % 4
            main_cols = slice(k // 2 * BLOCK, (k // 2 + 1) * BLOCK)
            tail_cols = slice(k // 4 * BLOCK, (k // 4 + 1) * BLOCK)
            for i in range(HALF // 8):
                here = slice(8 * i, 8 * i + 8)
                spot = (8 * i + HALF * pair) % BLOCK
                part = pltpu.roll(slope, spot, 1) if spot else slope
                if pair:
                    part = jnp.where(lanes < HALF, base_main[here, main_cols], part)
                base_main[here, main_cols] = part
                spot = (8 * i + TAIL * quad - HALF) % BLOCK
                part = pltpu.roll(slope, spot, 1) if spot else slope
                if quad:
                    part = jnp.where(lanes < TAIL * quad, base_tail[here, tail_cols], part)
                base_tail[here, tail_cols] = part
            coeff = jnp.broadcast_to(coeff_ref[0][:, k : k + 1], (4, BLOCK))
            spots = lane_of((4, BLOCK))
            held = jnp.where(spots < HALF, cmain[:, main_cols], coeff) if pair else coeff
            cmain[:, main_cols] = held
            held = jnp.where(spots < TAIL * quad, ctail[:, tail_cols], coeff) if quad else coeff
            ctail[:, tail_cols] = held
        for q in range(TILES):
            win[q * PAD_ROWS : (q + 1) * PAD_ROWS, :] = padded[:, q * BLOCK : q * BLOCK + 256]
        for pair in range(KERNELS // 2):
            part = jnp.dot(
                win[...], band[:, pair * 256 : (pair + 1) * 256], preferred_element_type=f32
            ).astype(bf16)
            for q in range(TILES):
                for inner in range(2):
                    smeared[pair * 2 + inner, :, q * BLOCK : (q + 1) * BLOCK] = part[
                        q * PAD_ROWS : (q + 1) * PAD_ROWS, inner * BLOCK : (inner + 1) * BLOCK
                    ]
        carry[...] = jnp.zeros_like(carry)

    cols = lane_of((1, SIDE))
    v = (cols.astype(f32) + 0.5) / SIDE - 0.5
    halves = []
    for half in range(2):
        start = pl.multiple_of(p * BLOCK + half * HALF, HALF)
        u = ((row_of((HALF, 1)) + start).astype(f32) + 0.5) / SIDE - 0.5
        for out, base, coeff in ((ab_main, base_main, cmain), (ab_tail, base_tail, ctail)):
            c0, c1 = coeff[pl.ds(0, 1), :], coeff[pl.ds(1, 1), :]
            c2, c3 = coeff[pl.ds(2, 1), :], coeff[pl.ds(3, 1), :]
            out[half, pl.ds(0, HALF), :] = (base[...] * (c0 + u * c1)).astype(bf16)
            out[half, pl.ds(HALF, HALF), :] = (base[...] * (c2 + u * c3)).astype(bf16)
        main = smeared[:, pl.ds(start, HALF), :].reshape(MAIN_K, SIDE)
        tail = smeared[:, pl.ds(start + HALF, TAIL), :].reshape(TAIL_K, SIDE)
        both = jnp.dot(ab_main[half], main, preferred_element_type=f32)
        both = both + jnp.dot(ab_tail[half], tail, preferred_element_type=f32)
        halves.append(both[:HALF] + v * both[HALF:])
    image = jnp.concatenate(halves, axis=0)

    tile_of = cols // BLOCK
    fx = jnp.zeros((1, SIDE), f32)
    fy = jnp.zeros((1, SIDE), f32)
    for q in range(TILES):
        shift = shift_ref[e, p * TILES + q]
        fx = jnp.where(tile_of == q, ((shift & 3).astype(f32) + 0.5) * 0.25, fx)
        fy = jnp.where(tile_of == q, ((shift >> 2).astype(f32) + 0.5) * 0.25, fy)
    inside = cols < SIDE - 1

    def along(x):
        return (1.0 - fx) * x + fx * jnp.where(inside, pltpu.roll(x, SIDE - 1, 1), 0.0)

    mixed = along(image)
    below_row = along(carry[...])[:1]
    last = row_of((BLOCK, 1)) == BLOCK - 1
    below = jnp.where(last, below_row, pltpu.roll(mixed, BLOCK - 1, 0))
    result = (1.0 - fy) * mixed + fy * below
    carry[...] = image[:8]
    shifted_ref[0] = result
    first_block = e * 16 + p * TILES
    for q in range(TILES):
        cells[q] = result[:, q * BLOCK : (q + 1) * BLOCK]
        for g in range(GROUP):
            send_ref[g, first_block + q] = cells[q, every(g), :].astype(bf16)


def conv_send(owners, columns, shifts, weight, cutouts, vert, horiz, coeffs):
    def by_exposure(*shape):
        return pl.BlockSpec((1,) + shape, lambda e, s, *_: (e,) + (0,) * len(shape))

    return pl.pallas_call(
        conv_kernel,
        out_shape=(
            pltpu.HBM((2, SIDE, SIDE), f32),
            jax.ShapeDtypeStruct((GROUP, 33, SLICE, BLOCK), bf16),
        ),
        grid_spec=pltpu.PrefetchScalarGridSpec(
            num_scalar_prefetch=4,
            grid=(2, TILES),
            in_specs=[
                by_exposure(SIDE, SIDE),
                by_exposure(KERNELS, TAPS),
                by_exposure(KERNELS, TAPS),
                by_exposure(4, KERNELS),
            ],
            out_specs=[
                pl.BlockSpec((1, BLOCK, SIDE), lambda e, s, *_: (e, TILES - 1 - s, 0)),
                pl.BlockSpec((GROUP, 33, SLICE, BLOCK), lambda e, s, *_: (0, 0, 0, 0)),
            ],
            scratch_shapes=[
                pltpu.VMEM((PAD_ROWS, PAD_COLS), bf16),
                pltpu.VMEM((TILES * PAD_ROWS, 256), bf16),
                pltpu.VMEM((256, WIDE_K), bf16),
                pltpu.VMEM((HALF, MAIN_K), f32),
                pltpu.VMEM((HALF, TAIL_K), f32),
                pltpu.VMEM((4, MAIN_K), f32),
                pltpu.VMEM((4, TAIL_K), f32),
                pltpu.VMEM((2, BLOCK, MAIN_K), bf16),
                pltpu.VMEM((2, BLOCK, TAIL_K), bf16),
                pltpu.VMEM((KERNELS, PAD_ROWS, SIDE), bf16),
                pltpu.VMEM((8, SIDE), f32),
                pltpu.VMEM((TILES, BLOCK, BLOCK), f32),
            ],
        ),
        compiler_params=pltpu.CompilerParams(vmem_limit_bytes=48 * MIB),
        name="conv_send",
    )(*(
        pltpu.with_memory_space_constraint(x, pltpu.HBM)
        for x in (owners, columns, shifts, weight, cutouts, vert, horiz, coeffs)
    ))


def whole(*shape):
    return pl.BlockSpec(shape, lambda i, *_: (0,) * len(shape))


def combine_kernel(
    side_ref, got_ref, out_ref, target_ref, even, odd, weights, target_s, weight_s, sems
):
    lanes = lane_of((SLICE, BLOCK))
    owner_rows = row_of((BLOCK, BLOCK)).astype(f32)
    column_rows = row_of((8, BLOCK)).astype(f32)
    totals = jnp.zeros((8, BLOCK), f32)
    for r in range(8):
        note = got_ref[4 * r, 32].astype(f32)
        for i in range(1, 4):
            moved = pltpu.roll(got_ref[4 * r + i, 32].astype(f32), 32 * i, 1)
            note = jnp.where(lanes < 32 * i, note, moved)
        owner, column, weight = note[0:1], note[1:2], note[2:3]
        target_ref[pl.ds(r, 1), :] = (owner * PW + column).astype(jnp.int32)
        weights[pl.ds(r, 1), :] = weight
        onto = (owner_rows == owner).astype(bf16)
        placed = jnp.where(column_rows == column, weight, 0.0).astype(bf16)
        totals = totals + lax.dot_general(
            placed, onto, (((1,), (1,)), ((), ())), preferred_element_type=f32
        )
    copies = (
        pltpu.make_async_copy(target_ref, target_s, sems.at[0]),
        pltpu.make_async_copy(weights, weight_s, sems.at[1]),
    )
    for copy in copies:
        copy.start()
    even[...] = jnp.zeros_like(even)
    odd[...] = jnp.zeros_like(odd)
    for copy in copies:
        copy.wait()
    inner = tuple(acc.at[pl.ds(PW, 128 * PW)] for acc in (even, odd))

    @pl.loop(0, GROUP)
    def _(source):
        line, first = source >> 2, (source & 3) * 32
        for block in range(32):
            acc, spot = inner[block % 2], target_s[line, first + block]
            w = weight_s[line, first + block]
            acc[spot] = acc[spot] + w * got_ref[source, block].astype(f32)

    feet = side_ref[0] == 1
    high = totals.astype(bf16).astype(f32)
    table = jnp.where(feet, totals - high, high)[:SLICE].astype(bf16)

    @pl.loop(0, 128 // 8)
    def _(turn):
        for i in range(8):
            owner = turn * 8 + i
            for j in range(PW):
                spot = (owner + 1) * PW + j
                out_ref[owner, j] = (even[spot] + odd[spot]).astype(bf16)
            beside = pl.ds(owner * PW + jnp.where(feet, 0, 2 * PW), PW)
            foot = even[beside, SLICE - 1, :] + odd[beside, SLICE - 1, :]
            head = even[beside, 0, :] + odd[beside, 0, :]
            out_ref[owner, PW] = jnp.where(feet, foot, head).astype(bf16)
            out_ref[owner, PW + 1] = table


def combine(side, got):
    return pl.pallas_call(
        combine_kernel,
        out_shape=(
            jax.ShapeDtypeStruct((128, TILES_OUT, SLICE, BLOCK), bf16),
            jax.ShapeDtypeStruct((8, BLOCK), jnp.int32),
        ),
        grid_spec=pltpu.PrefetchScalarGridSpec(
            num_scalar_prefetch=1,
            grid=(1,),
            in_specs=[whole(GROUP, 33, SLICE, BLOCK)],
            out_specs=[whole(128, TILES_OUT, SLICE, BLOCK), whole(8, BLOCK)],
            scratch_shapes=[pltpu.VMEM((130 * PW, SLICE, BLOCK), f32)] * 2
            + [
                pltpu.VMEM((8, BLOCK), f32),
                pltpu.SMEM((8, BLOCK), jnp.int32),
                pltpu.SMEM((8, BLOCK), f32),
                pltpu.SemaphoreType.DMA((2,)),
            ],
        ),
        compiler_params=pltpu.CompilerParams(vmem_limit_bytes=24 * MIB),
        name="combine",
    )(side, got)


def summed(got_ref, g, j):
    total = got_ref[member(0, g), j].astype(f32)
    for group in range(1, GROUPS):
        total = total + got_ref[member(group, g), j].astype(f32)
    return total


WIDE = BLOCK + 2 * HALO


def starlet_kernel(
    level_ref, edge_ref, here_ref, got_ref,
    sky_ref, answer_ref, wide, cells,
):
    totals = summed(got_ref, 0, PW + 1) + summed(got_ref, GROUP // 2, PW + 1)
    inverse = pltpu.roll(1.0 / (1.0 + totals), BLOCK - here_ref[0], 1)
    own, before, after = (
        [jnp.broadcast_to(inverse[j : j + 1, i : i + 1], (1, BLOCK)) for j in range(PW)]
        for i in (0, BLOCK - 1, 1)
    )
    for g in range(GROUP):
        halo = summed(got_ref, g, PW)
        for j in range(PW):
            cols = slice(j * BLOCK, (j + 1) * BLOCK)
            cells[j, every(g), :] = summed(got_ref, g, j) * own[j]
            if g < HALO:
                wide[pl.ds(HALO + BLOCK + g, 1), cols] = halo[j : j + 1] * after[j]
            else:
                wide[pl.ds(g - HALO, 1), cols] = halo[j : j + 1] * before[j]
    for j in range(PW):
        wide[pl.ds(HALO, BLOCK), j * BLOCK : (j + 1) * BLOCK] = cells[j]
    rows = lax.broadcasted_iota(jnp.int32, (WIDE, 1), 0)
    cols = lax.broadcasted_iota(jnp.int32, (1, SIDE), 1)
    above = (rows < HALO).astype(f32)
    under = (rows >= HALO + BLOCK).astype(f32)
    inside = 1.0 - above * edge_ref[0] - under * edge_ref[1]
    tile_of = cols // BLOCK
    lims = []
    for r in range(3):
        lim = jnp.zeros((1, SIDE), f32)
        for j in range(PW):
            lim = jnp.where(tile_of == j, level_ref[r * PW + j], lim)
        lims.append(lim)
    middle = (1.0 - above) - under
    lim = above * lims[0] + middle * lims[1] + under * lims[2]
    fine, coarse = fine_tau * lim, coarse_tau * lim

    def smooth(x, d):
        def up(y, n):
            return pltpu.roll(y, n % WIDE, 0)

        x = 0.375 * x + 0.25 * (up(x, d) + up(x, -d)) + 0.0625 * (up(x, 2 * d) + up(x, -2 * d))

        def side(y, n):
            keep = cols >= n if n > 0 else cols < SIDE + n
            return jnp.where(keep, pltpu.roll(y, n % SIDE, 1), 0.0)

        return (
            0.375 * x
            + 0.25 * (side(x, d) + side(x, -d))
            + 0.0625 * (side(x, 2 * d) + side(x, -2 * d))
        )

    def shrink(detail, limit):
        return detail - jnp.clip(detail, -limit, limit)

    x = wide[...]
    for _ in range(SWEEPS):
        x = x * inside
        one = smooth(x, 1) * inside
        two = smooth(one, 2)
        x = two + shrink(x - one, fine) + shrink(one - two, coarse)
    sky = x[HALO : HALO + BLOCK]
    sky_ref[...] = sky
    for j in range(PW):
        cells[j] = sky[:, j * BLOCK : (j + 1) * BLOCK]
        for g in range(GROUP):
            part = cells[j, every(g), :].astype(bf16)
            for group in range(GROUPS):
                answer_ref[member(group, g), j] = part


def starlet(levels, edges, here, partial):
    return pl.pallas_call(
        starlet_kernel,
        out_shape=(
            jax.ShapeDtypeStruct((BLOCK, SIDE), f32),
            jax.ShapeDtypeStruct((128, PW, SLICE, BLOCK), bf16),
        ),
        grid_spec=pltpu.PrefetchScalarGridSpec(
            num_scalar_prefetch=3,
            grid=(1,),
            in_specs=[whole(128, TILES_OUT, SLICE, BLOCK)],
            out_specs=[whole(BLOCK, SIDE), whole(128, PW, SLICE, BLOCK)],
            scratch_shapes=[
                pltpu.VMEM((WIDE, SIDE), f32),
                pltpu.VMEM((PW, BLOCK, BLOCK), f32),
            ],
        ),
        compiler_params=pltpu.CompilerParams(vmem_limit_bytes=16 * MIB),
        name="starlet",
    )(levels, edges, here, partial)


def pick_kernel(target_ref, all_ref, out_ref):
    @pl.loop(0, GROUP)
    def _(source):
        for block in range(32):
            out_ref[source, block] = all_ref[target_ref[source >> 2, (source & 3) * 32 + block]]


def pick(targets, templates):
    return pl.pallas_call(
        pick_kernel,
        out_shape=jax.ShapeDtypeStruct((GROUP, 32, SLICE, BLOCK), bf16),
        grid_spec=pltpu.PrefetchScalarGridSpec(
            num_scalar_prefetch=1,
            grid=(1,),
            in_specs=[whole(128 * PW, SLICE, BLOCK)],
            out_specs=whole(GROUP, 32, SLICE, BLOCK),
        ),
        compiler_params=pltpu.CompilerParams(vmem_limit_bytes=16 * MIB),
        name="pick",
    )(targets, templates.reshape(128 * PW, SLICE, BLOCK))


def difference_kernel(shifted_ref, template_ref, out_ref, cells):
    for q in range(TILES):
        cols = slice(q * BLOCK, (q + 1) * BLOCK)
        for g in range(GROUP):
            cells[q, every(g), :] = template_ref[g, q].astype(f32)
        out_ref[0, :, cols] = shifted_ref[0, :, cols] - cells[q]


def difference(shifted, returned):
    rows = pl.BlockSpec((1, BLOCK, SIDE), lambda e, p: (e, p, 0))
    return pl.pallas_call(
        difference_kernel,
        out_shape=jax.ShapeDtypeStruct((2, SIDE, SIDE), f32),
        grid=(2, TILES),
        in_specs=[
            rows,
            pl.BlockSpec((GROUP, TILES, SLICE, BLOCK), lambda e, p: (0, e * TILES + p, 0, 0)),
        ],
        out_specs=rows,
        scratch_shapes=[pltpu.VMEM((TILES, BLOCK, BLOCK), f32)],
        compiler_params=pltpu.CompilerParams(vmem_limit_bytes=16 * MIB),
        name="difference",
    )(shifted, returned)


def shards(
    cutouts, vert_taps, horiz_taps, field_coeffs, exposure_weight,
    dest_owner, dest_column, shift_index, threshold_level,
):
    shifted, slices = conv_send(
        dest_owner.reshape(2, 16), dest_column, shift_index, exposure_weight,
        cutouts, vert_taps, horiz_taps, field_coeffs,
    )
    got = lax.all_to_all(slices, NEAR, split_axis=0, concat_axis=0, tiled=True)
    side = lax.axis_index("z0").reshape(1)
    sums, targets = combine(side, got)
    partial = lax.all_to_all(sums, AXES, split_axis=0, concat_axis=0, tiled=True)
    count = lax.axis_size(AXES)
    here = lax.axis_index(AXES)
    levels = threshold_level.astype(f32)
    level_rows = jnp.pad(levels, ((1, 1), (0, 0)))
    near = lax.dynamic_slice(level_rows, (here, 0), (3, PW)).reshape(3 * PW)
    edges = jnp.stack([here == 0, here == count - 1]).astype(f32)
    sky, answers = starlet(near, edges, here.reshape(1), partial)
    templates = lax.all_to_all(answers, AXES, split_axis=0, concat_axis=0, tiled=True)
    picked = pick(targets, templates)
    returned = lax.all_to_all(picked, NEAR, split_axis=0, concat_axis=0, tiled=True)
    return sky, difference(shifted, returned)


def solution(mesh):
    split = jax.sharding.Mesh(mesh.devices.reshape((2,) * 7), AXES)
    placed = (
        P(AXES, None, None),
        P(AXES, None, None),
        P(AXES, None, None),
        P(AXES, None, None),
        P(AXES),
        P(AXES, None, None),
        P(AXES, None),
        P(AXES, None),
        P(),
    )
    return jax.shard_map(
        shards,
        mesh=split,
        in_specs=placed,
        out_specs=(P(AXES, None), P(AXES, None, None)),
        check_vma=False,
    )
```

```python
import jax
import jax.numpy as jnp
from jax import lax
from jax.experimental import pallas as pl
from jax.experimental.pallas import tpu as pltpu
from jax.sharding import PartitionSpec as P

BLOCK = 128
PW = 4
SWEEPS = 2
SIDE = 512
TILES = 4
KERNELS = 16
TAPS = 21
MARGIN = 10
TOP = 16
HALO = 16
TAIL = 32
HALF = BLOCK // 2
WIDE_K = KERNELS * BLOCK
MAIN_K = KERNELS * HALF
TAIL_K = KERNELS * TAIL
PAD_ROWS = SIDE + 2 * TOP
PAD_COLS = SIDE + BLOCK
WIN_ROWS = BLOCK + TAIL
GROUP = 32
GROUPS = 4
SLICE = BLOCK // GROUP
MIB = 1 << 20
AXES = ("z1", "z0", "y1", "y0", "x1", "x0", "c")
NEAR = ("z0", "y0", "x1", "x0", "c")
TILES_OUT = PW + 2

fine_tau = 0.04
coarse_tau = 0.02
f32 = jnp.float32
bf16 = jnp.bfloat16


def member(group, g):
    near = (g >> 4 & 1, g >> 3 & 1, g & 7)
    return (group >> 1 & 1) << 6 | near[0] << 5 | (group & 1) << 4 | near[1] << 3 | near[2]


def every(g):
    return pl.ds(g, SLICE, stride=GROUP)


def lane_of(shape):
    return lax.broadcasted_iota(jnp.int32, shape, len(shape) - 1)


def row_of(shape):
    return lax.broadcasted_iota(jnp.int32, shape, 0)


def placed_taps(taps, first, step):
    shape = (TAPS, BLOCK)
    lanes = (first + step * row_of(shape)) & (BLOCK - 1)
    onto = (lane_of(shape) == lanes).astype(bf16)
    return jnp.dot(taps.astype(bf16), onto, preferred_element_type=f32)


def sloped(rows, k):
    row = jnp.broadcast_to(rows[k : k + 1], (8, BLOCK))
    return pltpu.roll(row, 0, 1, stride=1, stride_axis=0)


def conv_kernel(
    owner_ref, column_ref, shift_ref, weight_ref,
    cut_ref, vert_ref, horiz_ref, coeff_ref,
    shifted_ref, send_ref,
    padded, win, band, base_main, base_tail, cmain, ctail, ab_main, ab_tail, smeared,
    carry, cells,
):
    e = pl.program_id(0)
    step = pl.program_id(1)
    p = TILES - 1 - step
    tile = (8, BLOCK)

    @pl.when((e == 0) & (step == 0))
    def _():
        lanes = lane_of((1, BLOCK))
        owners = jnp.zeros((1, BLOCK), f32)
        columns = jnp.zeros((1, BLOCK), f32)
        for b in range(32):
            owners = jnp.where(lanes == b, owner_ref[b // 16, b % 16].astype(f32), owners)
            columns = jnp.where(lanes == b, column_ref[b // 16, b % 16].astype(f32), columns)
        weights = jnp.where(lanes < 16, weight_ref[0], weight_ref[1])
        rows = row_of((SLICE, BLOCK))
        note = jnp.where(rows == 0, owners, jnp.where(rows == 1, columns, weights))
        note = note.astype(bf16)
        for g in range(GROUP):
            send_ref[g, 32] = note
        padded[pl.ds(0, TOP), :] = jnp.zeros((TOP, PAD_COLS), bf16)
        padded[pl.ds(TOP + SIDE, TOP), :] = jnp.zeros((TOP, PAD_COLS), bf16)
        band[pl.ds(WIN_ROWS, 256 - WIN_ROWS), :] = jnp.zeros((256 - WIN_ROWS, WIDE_K), bf16)

    @pl.when(step == 0)
    def _():
        image = cut_ref[0]
        wide = jnp.concatenate([image, jnp.zeros((SIDE, BLOCK), f32)], axis=1)
        padded[pl.ds(TOP, SIDE), :] = pltpu.roll(wide, MARGIN, 1).astype(bf16)
        rows_h = placed_taps(horiz_ref[0], BLOCK, -1)
        rows_v = placed_taps(vert_ref[0], TOP - MARGIN, 1)
        lanes, rows = lane_of(tile), row_of(tile)
        for k in range(KERNELS):
            cols = slice(k * BLOCK, (k + 1) * BLOCK)
            slope = sloped(rows_h, k)
            tiles = []
            for i in range(WIN_ROWS // 8):
                part = pltpu.roll(slope, 8 * i % BLOCK, 1) if 8 * i % BLOCK else slope
                if i < 3 or i >= 16:
                    lag = 8 * i + rows - lanes
                    part = jnp.where((lag >= 0) & (lag < TAPS), part, 0.0)
                tiles.append(part)
            band[pl.ds(0, WIN_ROWS), cols] = jnp.concatenate(tiles, axis=0).astype(bf16)
            slope = sloped(rows_v, k)
            pair, quad = k % 2, k % 4
            main_cols = slice(k // 2 * BLOCK, (k // 2 + 1) * BLOCK)
            tail_cols = slice(k // 4 * BLOCK, (k // 4 + 1) * BLOCK)
            for i in range(HALF // 8):
                here = slice(8 * i, 8 * i + 8)
                spot = (8 * i + HALF * pair) % BLOCK
                part = pltpu.roll(slope, spot, 1) if spot else slope
                if pair:
                    part = jnp.where(lanes < HALF, base_main[here, main_cols], part)
                base_main[here, main_cols] = part
                spot = (8 * i + TAIL * quad - HALF) % BLOCK
                part = pltpu.roll(slope, spot, 1) if spot else slope
                if quad:
                    part = jnp.where(lanes < TAIL * quad, base_tail[here, tail_cols], part)
                base_tail[here, tail_cols] = part
            coeff = jnp.broadcast_to(coeff_ref[0][:, k : k + 1], (4, BLOCK))
            spots = lane_of((4, BLOCK))
            held = jnp.where(spots < HALF, cmain[:, main_cols], coeff) if pair else coeff
            cmain[:, main_cols] = held
            held = jnp.where(spots < TAIL * quad, ctail[:, tail_cols], coeff) if quad else coeff
            ctail[:, tail_cols] = held
        for q in range(TILES):
            win[q * PAD_ROWS : (q + 1) * PAD_ROWS, :] = padded[:, q * BLOCK : q * BLOCK + 256]
        for pair in range(KERNELS // 2):
            part = jnp.dot(
                win[...], band[:, pair * 256 : (pair + 1) * 256], preferred_element_type=f32
            ).astype(bf16)
            for q in range(TILES):
                for inner in range(2):
                    smeared[pair * 2 + inner, :, q * BLOCK : (q + 1) * BLOCK] = part[
                        q * PAD_ROWS : (q + 1) * PAD_ROWS, inner * BLOCK : (inner + 1) * BLOCK
                    ]
        carry[...] = jnp.zeros_like(carry)

    cols = lane_of((1, SIDE))
    v = (cols.astype(f32) + 0.5) / SIDE - 0.5
    halves = []
    for half in range(2):
        start = pl.multiple_of(p * BLOCK + half * HALF, HALF)
        u = ((row_of((HALF, 1)) + start).astype(f32) + 0.5) / SIDE - 0.5
        for out, base, coeff in ((ab_main, base_main, cmain), (ab_tail, base_tail, ctail)):
            c0, c1 = coeff[pl.ds(0, 1), :], coeff[pl.ds(1, 1), :]
            c2, c3 = coeff[pl.ds(2, 1), :], coeff[pl.ds(3, 1), :]
            out[half, pl.ds(0, HALF), :] = (base[...] * (c0 + u * c1)).astype(bf16)
            out[half, pl.ds(HALF, HALF), :] = (base[...] * (c2 + u * c3)).astype(bf16)
        main = smeared[:, pl.ds(start, HALF), :].reshape(MAIN_K, SIDE)
        tail = smeared[:, pl.ds(start + HALF, TAIL), :].reshape(TAIL_K, SIDE)
        both = jnp.dot(ab_main[half], main, preferred_element_type=f32)
        both = both + jnp.dot(ab_tail[half], tail, preferred_element_type=f32)
        halves.append(both[:HALF] + v * both[HALF:])
    image = jnp.concatenate(halves, axis=0)

    tile_of = cols // BLOCK
    fx = jnp.zeros((1, SIDE), f32)
    fy = jnp.zeros((1, SIDE), f32)
    for q in range(TILES):
        shift = shift_ref[e, p * TILES + q]
        fx = jnp.where(tile_of == q, ((shift & 3).astype(f32) + 0.5) * 0.25, fx)
        fy = jnp.where(tile_of == q, ((shift >> 2).astype(f32) + 0.5) * 0.25, fy)
    inside = cols < SIDE - 1

    def along(x):
        return (1.0 - fx) * x + fx * jnp.where(inside, pltpu.roll(x, SIDE - 1, 1), 0.0)

    mixed = along(image)
    below_row = along(carry[...])[:1]
    last = row_of((BLOCK, 1)) == BLOCK - 1
    below = jnp.where(last, below_row, pltpu.roll(mixed, BLOCK - 1, 0))
    result = (1.0 - fy) * mixed + fy * below
    carry[...] = image[:8]
    shifted_ref[0] = result
    first_block = e * 16 + p * TILES
    for q in range(TILES):
        cells[q] = result[:, q * BLOCK : (q + 1) * BLOCK]
        for g in range(GROUP):
            send_ref[g, first_block + q] = cells[q, every(g), :].astype(bf16)


def conv_send(owners, columns, shifts, weight, cutouts, vert, horiz, coeffs):
    def by_exposure(*shape):
        return pl.BlockSpec((1,) + shape, lambda e, s, *_: (e,) + (0,) * len(shape))

    return pl.pallas_call(
        conv_kernel,
        out_shape=(
            pltpu.HBM((2, SIDE, SIDE), f32),
            jax.ShapeDtypeStruct((GROUP, 33, SLICE, BLOCK), bf16),
        ),
        grid_spec=pltpu.PrefetchScalarGridSpec(
            num_scalar_prefetch=4,
            grid=(2, TILES),
            in_specs=[
                by_exposure(SIDE, SIDE),
                by_exposure(KERNELS, TAPS),
                by_exposure(KERNELS, TAPS),
                by_exposure(4, KERNELS),
            ],
            out_specs=[
                pl.BlockSpec((1, BLOCK, SIDE), lambda e, s, *_: (e, TILES - 1 - s, 0)),
                pl.BlockSpec((GROUP, 33, SLICE, BLOCK), lambda e, s, *_: (0, 0, 0, 0)),
            ],
            scratch_shapes=[
                pltpu.VMEM((PAD_ROWS, PAD_COLS), bf16),
                pltpu.VMEM((TILES * PAD_ROWS, 256), bf16),
                pltpu.VMEM((256, WIDE_K), bf16),
                pltpu.VMEM((HALF, MAIN_K), f32),
                pltpu.VMEM((HALF, TAIL_K), f32),
                pltpu.VMEM((4, MAIN_K), f32),
                pltpu.VMEM((4, TAIL_K), f32),
                pltpu.VMEM((2, BLOCK, MAIN_K), bf16),
                pltpu.VMEM((2, BLOCK, TAIL_K), bf16),
                pltpu.VMEM((KERNELS, PAD_ROWS, SIDE), bf16),
                pltpu.VMEM((8, SIDE), f32),
                pltpu.VMEM((TILES, BLOCK, BLOCK), f32),
            ],
        ),
        compiler_params=pltpu.CompilerParams(vmem_limit_bytes=48 * MIB),
        name="conv_send",
    )(*(
        pltpu.with_memory_space_constraint(x, pltpu.HBM)
        for x in (owners, columns, shifts, weight, cutouts, vert, horiz, coeffs)
    ))


def whole(*shape):
    return pl.BlockSpec(shape, lambda i, *_: (0,) * len(shape))


def combine_kernel(
    side_ref, got_ref, out_ref, target_ref, even, odd, weights, target_s, weight_s, sems
):
    lanes = lane_of((SLICE, BLOCK))
    owner_rows = row_of((BLOCK, BLOCK)).astype(f32)
    column_rows = row_of((8, BLOCK)).astype(f32)
    totals = jnp.zeros((8, BLOCK), f32)
    for r in range(8):
        note = got_ref[4 * r, 32].astype(f32)
        for i in range(1, 4):
            moved = pltpu.roll(got_ref[4 * r + i, 32].astype(f32), 32 * i, 1)
            note = jnp.where(lanes < 32 * i, note, moved)
        owner, column, weight = note[0:1], note[1:2], note[2:3]
        target_ref[pl.ds(r, 1), :] = (owner * PW + column).astype(jnp.int32)
        weights[pl.ds(r, 1), :] = weight
        onto = (owner_rows == owner).astype(bf16)
        placed = jnp.where(column_rows == column, weight, 0.0).astype(bf16)
        totals = totals + lax.dot_general(
            placed, onto, (((1,), (1,)), ((), ())), preferred_element_type=f32
        )
    copies = (
        pltpu.make_async_copy(target_ref, target_s, sems.at[0]),
        pltpu.make_async_copy(weights, weight_s, sems.at[1]),
    )
    for copy in copies:
        copy.start()
    even[...] = jnp.zeros_like(even)
    odd[...] = jnp.zeros_like(odd)
    for copy in copies:
        copy.wait()
    inner = tuple(acc.at[pl.ds(PW, 128 * PW)] for acc in (even, odd))

    @pl.loop(0, 8)
    def _(line):
        for i in range(BLOCK):
            acc, spot, w = inner[i % 2], target_s[line, i], weight_s[line, i]
            block = got_ref[line * 4 + i // 32, i % 32]
            acc[spot] = acc[spot] + w * block.astype(f32)

    feet = side_ref[0] == 1
    high = totals.astype(bf16).astype(f32)
    table = jnp.where(feet, totals - high, high)[:SLICE].astype(bf16)

    @pl.loop(0, 128 // 8)
    def _(turn):
        for i in range(8):
            owner = turn * 8 + i
            for j in range(PW):
                spot = (owner + 1) * PW + j
                out_ref[owner, j] = (even[spot] + odd[spot]).astype(bf16)
            beside = pl.ds(owner * PW + jnp.where(feet, 0, 2 * PW), PW)
            foot = even[beside, SLICE - 1, :] + odd[beside, SLICE - 1, :]
            head = even[beside, 0, :] + odd[beside, 0, :]
            out_ref[owner, PW] = jnp.where(feet, foot, head).astype(bf16)
            out_ref[owner, PW + 1] = table


def combine(side, got):
    return pl.pallas_call(
        combine_kernel,
        out_shape=(
            jax.ShapeDtypeStruct((128, TILES_OUT, SLICE, BLOCK), bf16),
            jax.ShapeDtypeStruct((8, BLOCK), jnp.int32),
        ),
        grid_spec=pltpu.PrefetchScalarGridSpec(
            num_scalar_prefetch=1,
            grid=(1,),
            in_specs=[whole(GROUP, 33, SLICE, BLOCK)],
            out_specs=[whole(128, TILES_OUT, SLICE, BLOCK), whole(8, BLOCK)],
            scratch_shapes=[pltpu.VMEM((130 * PW, SLICE, BLOCK), f32)] * 2
            + [
                pltpu.VMEM((8, BLOCK), f32),
                pltpu.SMEM((8, BLOCK), jnp.int32),
                pltpu.SMEM((8, BLOCK), f32),
                pltpu.SemaphoreType.DMA((2,)),
            ],
        ),
        compiler_params=pltpu.CompilerParams(vmem_limit_bytes=24 * MIB),
        name="combine",
    )(side, got)


def summed(got_ref, g, j):
    total = got_ref[member(0, g), j].astype(f32)
    for group in range(1, GROUPS):
        total = total + got_ref[member(group, g), j].astype(f32)
    return total


WIDE = BLOCK + 2 * HALO


def starlet_kernel(
    level_ref, edge_ref, here_ref, got_ref,
    sky_ref, answer_ref, wide, cells,
):
    totals = summed(got_ref, 0, PW + 1) + summed(got_ref, GROUP // 2, PW + 1)
    inverse = pltpu.roll(1.0 / (1.0 + totals), BLOCK - here_ref[0], 1)
    own, before, after = (
        [jnp.broadcast_to(inverse[j : j + 1, i : i + 1], (1, BLOCK)) for j in range(PW)]
        for i in (0, BLOCK - 1, 1)
    )
    for g in range(GROUP):
        halo = summed(got_ref, g, PW)
        for j in range(PW):
            cols = slice(j * BLOCK, (j + 1) * BLOCK)
            cells[j, every(g), :] = summed(got_ref, g, j) * own[j]
            if g < HALO:
                wide[pl.ds(HALO + BLOCK + g, 1), cols] = halo[j : j + 1] * after[j]
            else:
                wide[pl.ds(g - HALO, 1), cols] = halo[j : j + 1] * before[j]
    for j in range(PW):
        wide[pl.ds(HALO, BLOCK), j * BLOCK : (j + 1) * BLOCK] = cells[j]
    rows = lax.broadcasted_iota(jnp.int32, (WIDE, 1), 0)
    cols = lax.broadcasted_iota(jnp.int32, (1, SIDE), 1)
    above = (rows < HALO).astype(f32)
    under = (rows >= HALO + BLOCK).astype(f32)
    inside = 1.0 - above * edge_ref[0] - under * edge_ref[1]
    tile_of = cols // BLOCK
    lims = []
    for r in range(3):
        lim = jnp.zeros((1, SIDE), f32)
        for j in range(PW):
            lim = jnp.where(tile_of == j, level_ref[r * PW + j], lim)
        lims.append(lim)
    middle = (1.0 - above) - under
    lim = above * lims[0] + middle * lims[1] + under * lims[2]
    fine, coarse = fine_tau * lim, coarse_tau * lim

    def smooth(x, d):
        def up(y, n):
            return pltpu.roll(y, n % WIDE, 0)

        x = 0.375 * x + 0.25 * (up(x, d) + up(x, -d)) + 0.0625 * (up(x, 2 * d) + up(x, -2 * d))

        def side(y, n):
            keep = cols >= n if n > 0 else cols < SIDE + n
            return jnp.where(keep, pltpu.roll(y, n % SIDE, 1), 0.0)

        return (
            0.375 * x
            + 0.25 * (side(x, d) + side(x, -d))
            + 0.0625 * (side(x, 2 * d) + side(x, -2 * d))
        )

    def shrink(detail, limit):
        return detail - jnp.clip(detail, -limit, limit)

    x = wide[...]
    for _ in range(SWEEPS):
        x = x * inside
        one = smooth(x, 1) * inside
        two = smooth(one, 2)
        x = two + shrink(x - one, fine) + shrink(one - two, coarse)
    sky = x[HALO : HALO + BLOCK]
    sky_ref[...] = sky
    for j in range(PW):
        cells[j] = sky[:, j * BLOCK : (j + 1) * BLOCK]
        for g in range(GROUP):
            part = cells[j, every(g), :].astype(bf16)
            for group in range(GROUPS):
                answer_ref[member(group, g), j] = part


def starlet(levels, edges, here, partial):
    return pl.pallas_call(
        starlet_kernel,
        out_shape=(
            jax.ShapeDtypeStruct((BLOCK, SIDE), f32),
            jax.ShapeDtypeStruct((128, PW, SLICE, BLOCK), bf16),
        ),
        grid_spec=pltpu.PrefetchScalarGridSpec(
            num_scalar_prefetch=3,
            grid=(1,),
            in_specs=[whole(128, TILES_OUT, SLICE, BLOCK)],
            out_specs=[whole(BLOCK, SIDE), whole(128, PW, SLICE, BLOCK)],
            scratch_shapes=[
                pltpu.VMEM((WIDE, SIDE), f32),
                pltpu.VMEM((PW, BLOCK, BLOCK), f32),
            ],
        ),
        compiler_params=pltpu.CompilerParams(vmem_limit_bytes=16 * MIB),
        name="starlet",
    )(levels, edges, here, partial)


def pick_kernel(target_ref, all_ref, out_ref):
    @pl.loop(0, 8)
    def _(line):
        for i in range(BLOCK):
            out_ref[line * 4 + i // 32, i % 32] = all_ref[target_ref[line, i]]


def pick(targets, templates):
    return pl.pallas_call(
        pick_kernel,
        out_shape=jax.ShapeDtypeStruct((GROUP, 32, SLICE, BLOCK), bf16),
        grid_spec=pltpu.PrefetchScalarGridSpec(
            num_scalar_prefetch=1,
            grid=(1,),
            in_specs=[whole(128 * PW, SLICE, BLOCK)],
            out_specs=whole(GROUP, 32, SLICE, BLOCK),
        ),
        compiler_params=pltpu.CompilerParams(vmem_limit_bytes=16 * MIB),
        name="pick",
    )(targets, templates.reshape(128 * PW, SLICE, BLOCK))


def difference_kernel(shifted_ref, template_ref, out_ref, cells):
    for block in range(2 * TILES):
        tile, q = block // TILES, block % TILES
        rows, cols = slice(tile * BLOCK, (tile + 1) * BLOCK), slice(q * BLOCK, (q + 1) * BLOCK)
        for g in range(GROUP):
            cells[block, every(g), :] = template_ref[g, block].astype(f32)
        out_ref[0, rows, cols] = shifted_ref[0, rows, cols] - cells[block]


def difference(shifted, returned):
    rows = pl.BlockSpec((1, 2 * BLOCK, SIDE), lambda e, p: (e, p, 0))
    return pl.pallas_call(
        difference_kernel,
        out_shape=jax.ShapeDtypeStruct((2, SIDE, SIDE), f32),
        grid=(2, 2),
        in_specs=[
            rows,
            pl.BlockSpec((GROUP, 2 * TILES, SLICE, BLOCK), lambda e, p: (0, e * 2 + p, 0, 0)),
        ],
        out_specs=rows,
        scratch_shapes=[pltpu.VMEM((2 * TILES, BLOCK, BLOCK), f32)],
        compiler_params=pltpu.CompilerParams(vmem_limit_bytes=16 * MIB),
        name="difference",
    )(shifted, returned)


def shards(
    cutouts, vert_taps, horiz_taps, field_coeffs, exposure_weight,
    dest_owner, dest_column, shift_index, threshold_level,
):
    shifted, slices = conv_send(
        dest_owner.reshape(2, 16), dest_column, shift_index, exposure_weight,
        cutouts, vert_taps, horiz_taps, field_coeffs,
    )
    got = lax.all_to_all(slices, NEAR, split_axis=0, concat_axis=0, tiled=True)
    side = lax.axis_index("z0").reshape(1)
    sums, targets = combine(side, got)
    partial = lax.all_to_all(sums, AXES, split_axis=0, concat_axis=0, tiled=True)
    count = lax.axis_size(AXES)
    here = lax.axis_index(AXES)
    levels = threshold_level.astype(f32)
    level_rows = jnp.pad(levels, ((1, 1), (0, 0)))
    near = lax.dynamic_slice(level_rows, (here, 0), (3, PW)).reshape(3 * PW)
    edges = jnp.stack([here == 0, here == count - 1]).astype(f32)
    sky, answers = starlet(near, edges, here.reshape(1), partial)
    templates = lax.all_to_all(answers, AXES, split_axis=0, concat_axis=0, tiled=True)
    picked = pick(targets, templates)
    returned = lax.all_to_all(picked, NEAR, split_axis=0, concat_axis=0, tiled=True)
    return sky, difference(shifted, returned)


def solution(mesh):
    split = jax.sharding.Mesh(mesh.devices.reshape((2,) * 7), AXES)
    placed = (
        P(AXES, None, None),
        P(AXES, None, None),
        P(AXES, None, None),
        P(AXES, None, None),
        P(AXES),
        P(AXES, None, None),
        P(AXES, None),
        P(AXES, None),
        P(),
    )
    return jax.shard_map(
        shards,
        mesh=split,
        in_specs=placed,
        out_specs=(P(AXES, None), P(AXES, None, None)),
        check_vma=False,
    )
```

```python
import jax
import jax.numpy as jnp
from jax import lax
from jax.experimental import pallas as pl
from jax.experimental.pallas import tpu as pltpu
from jax.sharding import PartitionSpec as P

BLOCK = 128
PW = 4
SWEEPS = 2
SIDE = 512
TILES = 4
KERNELS = 16
TAPS = 21
MARGIN = 10
TOP = 16
HALO = 16
TAIL = 32
HALF = BLOCK // 2
WIDE_K = KERNELS * BLOCK
MAIN_K = KERNELS * HALF
TAIL_K = KERNELS * TAIL
PAD_ROWS = SIDE + 2 * TOP
PAD_COLS = SIDE + BLOCK
WIN_ROWS = BLOCK + TAIL
GROUP = 32
GROUPS = 4
SLICE = BLOCK // GROUP
MIB = 1 << 20
AXES = ("z1", "z0", "y1", "y0", "x1", "x0", "c")
NEAR = ("z0", "y0", "x1", "x0", "c")
TILES_OUT = PW + 1
REACH = 12

fine_tau = 0.04
coarse_tau = 0.02
f32 = jnp.float32
bf16 = jnp.bfloat16


def member(group, g):
    near = (g >> 4 & 1, g >> 3 & 1, g & 7)
    return (group >> 1 & 1) << 6 | near[0] << 5 | (group & 1) << 4 | near[1] << 3 | near[2]


def every(g):
    return pl.ds(g, SLICE, stride=GROUP)


def lane_of(shape):
    return lax.broadcasted_iota(jnp.int32, shape, len(shape) - 1)


def row_of(shape):
    return lax.broadcasted_iota(jnp.int32, shape, 0)


def placed_taps(taps, first, step):
    shape = (TAPS, BLOCK)
    lanes = (first + step * row_of(shape)) & (BLOCK - 1)
    onto = (lane_of(shape) == lanes).astype(bf16)
    return jnp.dot(taps.astype(bf16), onto, preferred_element_type=f32)


def sloped(rows, k):
    row = jnp.broadcast_to(rows[k : k + 1], (8, BLOCK))
    return pltpu.roll(row, 0, 1, stride=1, stride_axis=0)


def conv_kernel(
    owner_ref, column_ref, shift_ref, weight_ref,
    cut_ref, vert_ref, horiz_ref, coeff_ref,
    shifted_ref, send_ref,
    padded, win, band, base_main, base_tail, cmain, ctail, ab_main, ab_tail, smeared,
    carry, cells,
):
    e = pl.program_id(0)
    step = pl.program_id(1)
    p = TILES - 1 - step
    tile = (8, BLOCK)

    @pl.when((e == 0) & (step == 0))
    def _():
        lanes = lane_of((1, BLOCK))
        owners = jnp.zeros((1, BLOCK), f32)
        columns = jnp.zeros((1, BLOCK), f32)
        for b in range(32):
            owners = jnp.where(lanes == b, owner_ref[b // 16, b % 16].astype(f32), owners)
            columns = jnp.where(lanes == b, column_ref[b // 16, b % 16].astype(f32), columns)
        weights = jnp.where(lanes < 16, weight_ref[0], weight_ref[1])
        rows = row_of((SLICE, BLOCK))
        note = jnp.where(rows == 0, owners, jnp.where(rows == 1, columns, weights))
        note = note.astype(bf16)
        for g in range(GROUP):
            send_ref[g, 32] = note
        padded[pl.ds(0, TOP), :] = jnp.zeros((TOP, PAD_COLS), bf16)
        padded[pl.ds(TOP + SIDE, TOP), :] = jnp.zeros((TOP, PAD_COLS), bf16)
        band[pl.ds(WIN_ROWS, 256 - WIN_ROWS), :] = jnp.zeros((256 - WIN_ROWS, WIDE_K), bf16)

    @pl.when(step == 0)
    def _():
        image = cut_ref[0]
        wide = jnp.concatenate([image, jnp.zeros((SIDE, BLOCK), f32)], axis=1)
        padded[pl.ds(TOP, SIDE), :] = pltpu.roll(wide, MARGIN, 1).astype(bf16)
        rows_h = placed_taps(horiz_ref[0], BLOCK, -1)
        rows_v = placed_taps(vert_ref[0], TOP - MARGIN, 1)
        lanes, rows = lane_of(tile), row_of(tile)
        for k in range(KERNELS):
            cols = slice(k * BLOCK, (k + 1) * BLOCK)
            slope = sloped(rows_h, k)
            tiles = []
            for i in range(WIN_ROWS // 8):
                part = pltpu.roll(slope, 8 * i % BLOCK, 1) if 8 * i % BLOCK else slope
                if i < 3 or i >= 16:
                    lag = 8 * i + rows - lanes
                    part = jnp.where((lag >= 0) & (lag < TAPS), part, 0.0)
                tiles.append(part)
            band[pl.ds(0, WIN_ROWS), cols] = jnp.concatenate(tiles, axis=0).astype(bf16)
            slope = sloped(rows_v, k)
            pair, quad = k % 2, k % 4
            main_cols = slice(k // 2 * BLOCK, (k // 2 + 1) * BLOCK)
            tail_cols = slice(k // 4 * BLOCK, (k // 4 + 1) * BLOCK)
            for i in range(HALF // 8):
                here = slice(8 * i, 8 * i + 8)
                spot = (8 * i + HALF * pair) % BLOCK
                part = pltpu.roll(slope, spot, 1) if spot else slope
                if pair:
                    part = jnp.where(lanes < HALF, base_main[here, main_cols], part)
                base_main[here, main_cols] = part
                spot = (8 * i + TAIL * quad - HALF) % BLOCK
                part = pltpu.roll(slope, spot, 1) if spot else slope
                if quad:
                    part = jnp.where(lanes < TAIL * quad, base_tail[here, tail_cols], part)
                base_tail[here, tail_cols] = part
            coeff = jnp.broadcast_to(coeff_ref[0][:, k : k + 1], (4, BLOCK))
            spots = lane_of((4, BLOCK))
            held = jnp.where(spots < HALF, cmain[:, main_cols], coeff) if pair else coeff
            cmain[:, main_cols] = held
            held = jnp.where(spots < TAIL * quad, ctail[:, tail_cols], coeff) if quad else coeff
            ctail[:, tail_cols] = held
        for q in range(TILES):
            win[q * PAD_ROWS : (q + 1) * PAD_ROWS, :] = padded[:, q * BLOCK : q * BLOCK + 256]
        for pair in range(KERNELS // 2):
            part = jnp.dot(
                win[...], band[:, pair * 256 : (pair + 1) * 256], preferred_element_type=f32
            ).astype(bf16)
            for q in range(TILES):
                for inner in range(2):
                    smeared[pair * 2 + inner, :, q * BLOCK : (q + 1) * BLOCK] = part[
                        q * PAD_ROWS : (q + 1) * PAD_ROWS, inner * BLOCK : (inner + 1) * BLOCK
                    ]
        carry[...] = jnp.zeros_like(carry)

    cols = lane_of((1, SIDE))
    v = (cols.astype(f32) + 0.5) / SIDE - 0.5
    halves = []
    for half in range(2):
        start = pl.multiple_of(p * BLOCK + half * HALF, HALF)
        u = ((row_of((HALF, 1)) + start).astype(f32) + 0.5) / SIDE - 0.5
        for out, base, coeff in ((ab_main, base_main, cmain), (ab_tail, base_tail, ctail)):
            c0, c1 = coeff[pl.ds(0, 1), :], coeff[pl.ds(1, 1), :]
            c2, c3 = coeff[pl.ds(2, 1), :], coeff[pl.ds(3, 1), :]
            out[half, pl.ds(0, HALF), :] = (base[...] * (c0 + u * c1)).astype(bf16)
            out[half, pl.ds(HALF, HALF), :] = (base[...] * (c2 + u * c3)).astype(bf16)
        main = smeared[:, pl.ds(start, HALF), :].reshape(MAIN_K, SIDE)
        tail = smeared[:, pl.ds(start + HALF, TAIL), :].reshape(TAIL_K, SIDE)
        both = jnp.dot(ab_main[half], main, preferred_element_type=f32)
        both = both + jnp.dot(ab_tail[half], tail, preferred_element_type=f32)
        halves.append(both[:HALF] + v * both[HALF:])
    image = jnp.concatenate(halves, axis=0)

    tile_of = cols // BLOCK
    fx = jnp.zeros((1, SIDE), f32)
    fy = jnp.zeros((1, SIDE), f32)
    for q in range(TILES):
        shift = shift_ref[e, p * TILES + q]
        fx = jnp.where(tile_of == q, ((shift & 3).astype(f32) + 0.5) * 0.25, fx)
        fy = jnp.where(tile_of == q, ((shift >> 2).astype(f32) + 0.5) * 0.25, fy)
    inside = cols < SIDE - 1

    def along(x):
        return (1.0 - fx) * x + fx * jnp.where(inside, pltpu.roll(x, SIDE - 1, 1), 0.0)

    mixed = along(image)
    below_row = along(carry[...])[:1]
    last = row_of((BLOCK, 1)) == BLOCK - 1
    below = jnp.where(last, below_row, pltpu.roll(mixed, BLOCK - 1, 0))
    result = (1.0 - fy) * mixed + fy * below
    carry[...] = image[:8]
    shifted_ref[0] = result
    first_block = e * 16 + p * TILES
    for q in range(TILES):
        cells[q] = result[:, q * BLOCK : (q + 1) * BLOCK]
        for g in range(GROUP):
            send_ref[g, first_block + q] = cells[q, every(g), :].astype(bf16)


def conv_send(owners, columns, shifts, weight, cutouts, vert, horiz, coeffs):
    def by_exposure(*shape):
        return pl.BlockSpec((1,) + shape, lambda e, s, *_: (e,) + (0,) * len(shape))

    return pl.pallas_call(
        conv_kernel,
        out_shape=(
            pltpu.HBM((2, SIDE, SIDE), f32),
            jax.ShapeDtypeStruct((GROUP, 33, SLICE, BLOCK), bf16),
        ),
        grid_spec=pltpu.PrefetchScalarGridSpec(
            num_scalar_prefetch=4,
            grid=(2, TILES),
            in_specs=[
                by_exposure(SIDE, SIDE),
                by_exposure(KERNELS, TAPS),
                by_exposure(KERNELS, TAPS),
                by_exposure(4, KERNELS),
            ],
            out_specs=[
                pl.BlockSpec((1, BLOCK, SIDE), lambda e, s, *_: (e, TILES - 1 - s, 0)),
                pl.BlockSpec((GROUP, 33, SLICE, BLOCK), lambda e, s, *_: (0, 0, 0, 0)),
            ],
            scratch_shapes=[
                pltpu.VMEM((PAD_ROWS, PAD_COLS), bf16),
                pltpu.VMEM((TILES * PAD_ROWS, 256), bf16),
                pltpu.VMEM((256, WIDE_K), bf16),
                pltpu.VMEM((HALF, MAIN_K), f32),
                pltpu.VMEM((HALF, TAIL_K), f32),
                pltpu.VMEM((4, MAIN_K), f32),
                pltpu.VMEM((4, TAIL_K), f32),
                pltpu.VMEM((2, BLOCK, MAIN_K), bf16),
                pltpu.VMEM((2, BLOCK, TAIL_K), bf16),
                pltpu.VMEM((KERNELS, PAD_ROWS, SIDE), bf16),
                pltpu.VMEM((8, SIDE), f32),
                pltpu.VMEM((TILES, BLOCK, BLOCK), f32),
            ],
        ),
        compiler_params=pltpu.CompilerParams(vmem_limit_bytes=48 * MIB),
        name="conv_send",
    )(*(
        pltpu.with_memory_space_constraint(x, pltpu.HBM)
        for x in (owners, columns, shifts, weight, cutouts, vert, horiz, coeffs)
    ))


def whole(*shape):
    return pl.BlockSpec(shape, lambda i, *_: (0,) * len(shape))


def combine_kernel(
    side_ref, got_ref, out_ref, target_ref, even, odd, weights, target_s, weight_s, sems
):
    lanes = lane_of((SLICE, BLOCK))
    owner_rows = row_of((BLOCK, BLOCK)).astype(f32)
    column_rows = row_of((8, BLOCK)).astype(f32)
    totals = jnp.zeros((8, BLOCK), f32)
    for r in range(8):
        note = got_ref[4 * r, 32].astype(f32)
        for i in range(1, 4):
            moved = pltpu.roll(got_ref[4 * r + i, 32].astype(f32), 32 * i, 1)
            note = jnp.where(lanes < 32 * i, note, moved)
        owner, column, weight = note[0:1], note[1:2], note[2:3]
        target_ref[pl.ds(r, 1), :] = (owner * PW + column).astype(jnp.int32)
        weights[pl.ds(r, 1), :] = weight
        onto = (owner_rows == owner).astype(bf16)
        placed = jnp.where(column_rows == column, weight, 0.0).astype(bf16)
        totals = totals + lax.dot_general(
            placed, onto, (((1,), (1,)), ((), ())), preferred_element_type=f32
        )
    copies = (
        pltpu.make_async_copy(target_ref, target_s, sems.at[0]),
        pltpu.make_async_copy(weights, weight_s, sems.at[1]),
    )
    for copy in copies:
        copy.start()
    even[...] = jnp.zeros_like(even)
    odd[...] = jnp.zeros_like(odd)
    for copy in copies:
        copy.wait()
    inner = tuple(acc.at[pl.ds(PW, 128 * PW)] for acc in (even, odd))

    @pl.loop(0, 8)
    def _(line):
        for i in range(BLOCK):
            acc, spot, w = inner[i % 2], target_s[line, i], weight_s[line, i]
            block = got_ref[line * 4 + i // 32, i % 32]
            acc[spot] = acc[spot] + w * block.astype(f32)

    feet = side_ref[0] >= HALO
    carries_table = (side_ref[0] >= REACH) & (side_ref[0] < GROUP - REACH)
    high = totals.astype(bf16).astype(f32)
    table = jnp.where(feet, totals - high, high)[:SLICE]

    @pl.loop(0, 128 // 8)
    def _(turn):
        for i in range(8):
            owner = turn * 8 + i
            for j in range(PW):
                spot = (owner + 1) * PW + j
                out_ref[owner, j] = (even[spot] + odd[spot]).astype(bf16)
            beside = pl.ds(owner * PW + jnp.where(feet, 0, 2 * PW), PW)
            foot = even[beside, SLICE - 1, :] + odd[beside, SLICE - 1, :]
            head = even[beside, 0, :] + odd[beside, 0, :]
            halo = jnp.where(feet, foot, head)
            out_ref[owner, PW] = jnp.where(carries_table, table, halo).astype(bf16)


def combine(side, got):
    return pl.pallas_call(
        combine_kernel,
        out_shape=(
            jax.ShapeDtypeStruct((128, TILES_OUT, SLICE, BLOCK), bf16),
            jax.ShapeDtypeStruct((8, BLOCK), jnp.int32),
        ),
        grid_spec=pltpu.PrefetchScalarGridSpec(
            num_scalar_prefetch=1,
            grid=(1,),
            in_specs=[whole(GROUP, 33, SLICE, BLOCK)],
            out_specs=[whole(128, TILES_OUT, SLICE, BLOCK), whole(8, BLOCK)],
            scratch_shapes=[pltpu.VMEM((130 * PW, SLICE, BLOCK), f32)] * 2
            + [
                pltpu.VMEM((8, BLOCK), f32),
                pltpu.SMEM((8, BLOCK), jnp.int32),
                pltpu.SMEM((8, BLOCK), f32),
                pltpu.SemaphoreType.DMA((2,)),
            ],
        ),
        compiler_params=pltpu.CompilerParams(vmem_limit_bytes=24 * MIB),
        name="combine",
    )(side, got)


def summed(got_ref, g, j):
    total = got_ref[member(0, g), j].astype(f32)
    for group in range(1, GROUPS):
        total = total + got_ref[member(group, g), j].astype(f32)
    return total


WIDE = BLOCK + 2 * HALO


def starlet_kernel(
    level_ref, edge_ref, here_ref, got_ref,
    sky_ref, answer_ref, wide, cells,
):
    totals = summed(got_ref, REACH, PW) + summed(got_ref, GROUP // 2, PW)
    wide[pl.ds(0, 8), :] = jnp.zeros((8, SIDE), f32)
    wide[pl.ds(WIDE - 8, 8), :] = jnp.zeros((8, SIDE), f32)
    inverse = pltpu.roll(1.0 / (1.0 + totals), BLOCK - here_ref[0], 1)
    own, before, after = (
        [jnp.broadcast_to(inverse[j : j + 1, i : i + 1], (1, BLOCK)) for j in range(PW)]
        for i in (0, BLOCK - 1, 1)
    )
    for g in range(GROUP):
        halo = summed(got_ref, g, PW)
        for j in range(PW):
            cols = slice(j * BLOCK, (j + 1) * BLOCK)
            cells[j, every(g), :] = summed(got_ref, g, j) * own[j]
            if g < REACH:
                wide[pl.ds(HALO + BLOCK + g, 1), cols] = halo[j : j + 1] * after[j]
            elif g >= GROUP - REACH:
                wide[pl.ds(g - HALO, 1), cols] = halo[j : j + 1] * before[j]
    for j in range(PW):
        wide[pl.ds(HALO, BLOCK), j * BLOCK : (j + 1) * BLOCK] = cells[j]
    rows = lax.broadcasted_iota(jnp.int32, (WIDE, 1), 0)
    cols = lax.broadcasted_iota(jnp.int32, (1, SIDE), 1)
    above = (rows < HALO).astype(f32)
    under = (rows >= HALO + BLOCK).astype(f32)
    inside = 1.0 - above * edge_ref[0] - under * edge_ref[1]
    tile_of = cols // BLOCK
    lims = []
    for r in range(3):
        lim = jnp.zeros((1, SIDE), f32)
        for j in range(PW):
            lim = jnp.where(tile_of == j, level_ref[r * PW + j], lim)
        lims.append(lim)
    middle = (1.0 - above) - under
    lim = above * lims[0] + middle * lims[1] + under * lims[2]
    fine, coarse = fine_tau * lim, coarse_tau * lim

    def smooth(x, d):
        def up(y, n):
            return pltpu.roll(y, n % WIDE, 0)

        x = 0.375 * x + 0.25 * (up(x, d) + up(x, -d)) + 0.0625 * (up(x, 2 * d) + up(x, -2 * d))

        def side(y, n):
            keep = cols >= n if n > 0 else cols < SIDE + n
            return jnp.where(keep, pltpu.roll(y, n % SIDE, 1), 0.0)

        return (
            0.375 * x
            + 0.25 * (side(x, d) + side(x, -d))
            + 0.0625 * (side(x, 2 * d) + side(x, -2 * d))
        )

    def shrink(detail, limit):
        return detail - jnp.clip(detail, -limit, limit)

    x = wide[...]
    for _ in range(SWEEPS):
        x = x * inside
        one = smooth(x, 1) * inside
        two = smooth(one, 2)
        x = two + shrink(x - one, fine) + shrink(one - two, coarse)
    sky = x[HALO : HALO + BLOCK]
    sky_ref[...] = sky
    for j in range(PW):
        cells[j] = sky[:, j * BLOCK : (j + 1) * BLOCK]
        for g in range(GROUP):
            part = cells[j, every(g), :].astype(bf16)
            for group in range(GROUPS):
                answer_ref[member(group, g), j] = part


def starlet(levels, edges, here, partial):
    return pl.pallas_call(
        starlet_kernel,
        out_shape=(
            jax.ShapeDtypeStruct((BLOCK, SIDE), f32),
            jax.ShapeDtypeStruct((128, PW, SLICE, BLOCK), bf16),
        ),
        grid_spec=pltpu.PrefetchScalarGridSpec(
            num_scalar_prefetch=3,
            grid=(1,),
            in_specs=[whole(128, TILES_OUT, SLICE, BLOCK)],
            out_specs=[whole(BLOCK, SIDE), whole(128, PW, SLICE, BLOCK)],
            scratch_shapes=[
                pltpu.VMEM((WIDE, SIDE), f32),
                pltpu.VMEM((PW, BLOCK, BLOCK), f32),
            ],
        ),
        compiler_params=pltpu.CompilerParams(vmem_limit_bytes=16 * MIB),
        name="starlet",
    )(levels, edges, here, partial)


def pick_kernel(target_ref, all_ref, out_ref):
    @pl.loop(0, 8)
    def _(line):
        for i in range(BLOCK):
            out_ref[line * 4 + i // 32, i % 32] = all_ref[target_ref[line, i]]


def pick(targets, templates):
    return pl.pallas_call(
        pick_kernel,
        out_shape=jax.ShapeDtypeStruct((GROUP, 32, SLICE, BLOCK), bf16),
        grid_spec=pltpu.PrefetchScalarGridSpec(
            num_scalar_prefetch=1,
            grid=(1,),
            in_specs=[whole(128 * PW, SLICE, BLOCK)],
            out_specs=whole(GROUP, 32, SLICE, BLOCK),
        ),
        compiler_params=pltpu.CompilerParams(vmem_limit_bytes=16 * MIB),
        name="pick",
    )(targets, templates.reshape(128 * PW, SLICE, BLOCK))


def difference_kernel(shifted_ref, template_ref, out_ref, cells):
    for block in range(2 * TILES):
        tile, q = block // TILES, block % TILES
        rows, cols = slice(tile * BLOCK, (tile + 1) * BLOCK), slice(q * BLOCK, (q + 1) * BLOCK)
        for g in range(GROUP):
            cells[block, every(g), :] = template_ref[g, block].astype(f32)
        out_ref[0, rows, cols] = shifted_ref[0, rows, cols] - cells[block]


def difference(shifted, returned):
    rows = pl.BlockSpec((1, 2 * BLOCK, SIDE), lambda e, p: (e, p, 0))
    return pl.pallas_call(
        difference_kernel,
        out_shape=jax.ShapeDtypeStruct((2, SIDE, SIDE), f32),
        grid=(2, 2),
        in_specs=[
            rows,
            pl.BlockSpec((GROUP, 2 * TILES, SLICE, BLOCK), lambda e, p: (0, e * 2 + p, 0, 0)),
        ],
        out_specs=rows,
        scratch_shapes=[pltpu.VMEM((2 * TILES, BLOCK, BLOCK), f32)],
        compiler_params=pltpu.CompilerParams(vmem_limit_bytes=16 * MIB),
        name="difference",
    )(shifted, returned)


def shards(
    cutouts, vert_taps, horiz_taps, field_coeffs, exposure_weight,
    dest_owner, dest_column, shift_index, threshold_level,
):
    shifted, slices = conv_send(
        dest_owner.reshape(2, 16), dest_column, shift_index, exposure_weight,
        cutouts, vert_taps, horiz_taps, field_coeffs,
    )
    got = lax.all_to_all(slices, NEAR, split_axis=0, concat_axis=0, tiled=True)
    side = lax.axis_index(NEAR).reshape(1)
    sums, targets = combine(side, got)
    partial = lax.all_to_all(sums, AXES, split_axis=0, concat_axis=0, tiled=True)
    count = lax.axis_size(AXES)
    here = lax.axis_index(AXES)
    levels = threshold_level.astype(f32)
    level_rows = jnp.pad(levels, ((1, 1), (0, 0)))
    near = lax.dynamic_slice(level_rows, (here, 0), (3, PW)).reshape(3 * PW)
    edges = jnp.stack([here == 0, here == count - 1]).astype(f32)
    sky, answers = starlet(near, edges, here.reshape(1), partial)
    templates = lax.all_to_all(answers, AXES, split_axis=0, concat_axis=0, tiled=True)
    picked = pick(targets, templates)
    returned = lax.all_to_all(picked, NEAR, split_axis=0, concat_axis=0, tiled=True)
    return sky, difference(shifted, returned)


def solution(mesh):
    split = jax.sharding.Mesh(mesh.devices.reshape((2,) * 7), AXES)
    placed = (
        P(AXES, None, None),
        P(AXES, None, None),
        P(AXES, None, None),
        P(AXES, None, None),
        P(AXES),
        P(AXES, None, None),
        P(AXES, None),
        P(AXES, None),
        P(),
    )
    return jax.shard_map(
        shards,
        mesh=split,
        in_specs=placed,
        out_specs=(P(AXES, None), P(AXES, None, None)),
        check_vma=False,
    )
```

```python
import jax
import jax.numpy as jnp
from jax import lax
from jax.experimental import pallas as pl
from jax.experimental.pallas import tpu as pltpu
from jax.sharding import PartitionSpec as P

BLOCK = 128
PW = 4
SWEEPS = 2
SIDE = 512
TILES = 4
KERNELS = 16
TAPS = 21
MARGIN = 10
TOP = 16
HALO = 16
TAIL = 32
HALF = BLOCK // 2
WIDE_K = KERNELS * BLOCK
MAIN_K = KERNELS * HALF
TAIL_K = KERNELS * TAIL
PAD_ROWS = SIDE + 2 * TOP
PAD_COLS = SIDE + BLOCK
WIN_ROWS = BLOCK + TAIL
GROUP = 32
GROUPS = 4
SLICE = BLOCK // GROUP
MIB = 1 << 20
AXES = ("z1", "z0", "y1", "y0", "x1", "x0", "c")
NEAR = ("z0", "y0", "x1", "x0", "c")
TILES_OUT = PW + 1
REACH = 12

fine_tau = 0.04
coarse_tau = 0.02
f32 = jnp.float32
bf16 = jnp.bfloat16


def member(group, g):
    near = (g >> 4 & 1, g >> 3 & 1, g & 7)
    return (group >> 1 & 1) << 6 | near[0] << 5 | (group & 1) << 4 | near[1] << 3 | near[2]


def every(g):
    return pl.ds(g, SLICE, stride=GROUP)


def lane_of(shape):
    return lax.broadcasted_iota(jnp.int32, shape, len(shape) - 1)


def row_of(shape):
    return lax.broadcasted_iota(jnp.int32, shape, 0)


def placed_taps(taps, first, step):
    shape = (TAPS, BLOCK)
    lanes = (first + step * row_of(shape)) & (BLOCK - 1)
    onto = (lane_of(shape) == lanes).astype(bf16)
    return jnp.dot(taps.astype(bf16), onto, preferred_element_type=f32)


def sloped(rows, k):
    row = jnp.broadcast_to(rows[k : k + 1], (8, BLOCK))
    return pltpu.roll(row, 0, 1, stride=1, stride_axis=0)


def conv_kernel(
    owner_ref, column_ref, shift_ref, weight_ref,
    cut_ref, vert_ref, horiz_ref, coeff_ref,
    shifted_ref, send_ref,
    padded, win, band, base_main, base_tail, cmain, ctail, ab_main, ab_tail, smeared,
    carry, cells,
):
    e = pl.program_id(0)
    step = pl.program_id(1)
    p = TILES - 1 - step
    tile = (8, BLOCK)

    @pl.when((e == 0) & (step == 0))
    def _():
        lanes = lane_of((1, BLOCK))
        owners = jnp.zeros((1, BLOCK), f32)
        columns = jnp.zeros((1, BLOCK), f32)
        for b in range(32):
            owners = jnp.where(lanes == b, owner_ref[b // 16, b % 16].astype(f32), owners)
            columns = jnp.where(lanes == b, column_ref[b // 16, b % 16].astype(f32), columns)
        weights = jnp.where(lanes < 16, weight_ref[0], weight_ref[1])
        rows = row_of((SLICE, BLOCK))
        note = jnp.where(rows == 0, owners, jnp.where(rows == 1, columns, weights))
        note = note.astype(bf16)
        for g in range(GROUP):
            send_ref[g, 32] = note
        padded[pl.ds(0, TOP), :] = jnp.zeros((TOP, PAD_COLS), bf16)
        padded[pl.ds(TOP + SIDE, TOP), :] = jnp.zeros((TOP, PAD_COLS), bf16)
        band[pl.ds(WIN_ROWS, 256 - WIN_ROWS), :] = jnp.zeros((256 - WIN_ROWS, WIDE_K), bf16)

    @pl.when(step == 0)
    def _():
        image = cut_ref[0]
        wide = jnp.concatenate([image, jnp.zeros((SIDE, BLOCK), f32)], axis=1)
        padded[pl.ds(TOP, SIDE), :] = pltpu.roll(wide, MARGIN, 1).astype(bf16)
        rows_h = placed_taps(horiz_ref[0], BLOCK, -1)
        rows_v = placed_taps(vert_ref[0], TOP - MARGIN, 1)
        lanes, rows = lane_of(tile), row_of(tile)
        for k in range(KERNELS):
            cols = slice(k * BLOCK, (k + 1) * BLOCK)
            slope = sloped(rows_h, k)
            tiles = []
            for i in range(WIN_ROWS // 8):
                part = pltpu.roll(slope, 8 * i % BLOCK, 1) if 8 * i % BLOCK else slope
                if i < 3 or i >= 16:
                    lag = 8 * i + rows - lanes
                    part = jnp.where((lag >= 0) & (lag < TAPS), part, 0.0)
                tiles.append(part)
            band[pl.ds(0, WIN_ROWS), cols] = jnp.concatenate(tiles, axis=0).astype(bf16)
            slope = sloped(rows_v, k)
            pair, quad = k % 2, k % 4
            main_cols = slice(k // 2 * BLOCK, (k // 2 + 1) * BLOCK)
            tail_cols = slice(k // 4 * BLOCK, (k // 4 + 1) * BLOCK)
            for i in range(HALF // 8):
                here = slice(8 * i, 8 * i + 8)
                spot = (8 * i + HALF * pair) % BLOCK
                part = pltpu.roll(slope, spot, 1) if spot else slope
                if pair:
                    part = jnp.where(lanes < HALF, base_main[here, main_cols], part)
                base_main[here, main_cols] = part
                spot = (8 * i + TAIL * quad - HALF) % BLOCK
                part = pltpu.roll(slope, spot, 1) if spot else slope
                if quad:
                    part = jnp.where(lanes < TAIL * quad, base_tail[here, tail_cols], part)
                base_tail[here, tail_cols] = part
            coeff = jnp.broadcast_to(coeff_ref[0][:, k : k + 1], (4, BLOCK))
            spots = lane_of((4, BLOCK))
            held = jnp.where(spots < HALF, cmain[:, main_cols], coeff) if pair else coeff
            cmain[:, main_cols] = held
            held = jnp.where(spots < TAIL * quad, ctail[:, tail_cols], coeff) if quad else coeff
            ctail[:, tail_cols] = held
        for q in range(TILES):
            win[q * PAD_ROWS : (q + 1) * PAD_ROWS, :] = padded[:, q * BLOCK : q * BLOCK + 256]
        for pair in range(KERNELS // 2):
            part = jnp.dot(
                win[...], band[:, pair * 256 : (pair + 1) * 256], preferred_element_type=f32
            ).astype(bf16)
            for q in range(TILES):
                for inner in range(2):
                    smeared[pair * 2 + inner, :, q * BLOCK : (q + 1) * BLOCK] = part[
                        q * PAD_ROWS : (q + 1) * PAD_ROWS, inner * BLOCK : (inner + 1) * BLOCK
                    ]
        carry[...] = jnp.zeros_like(carry)

    cols = lane_of((1, SIDE))
    v = (cols.astype(f32) + 0.5) / SIDE - 0.5
    halves = []
    for half in range(2):
        start = pl.multiple_of(p * BLOCK + half * HALF, HALF)
        u = ((row_of((HALF, 1)) + start).astype(f32) + 0.5) / SIDE - 0.5
        for out, base, coeff in ((ab_main, base_main, cmain), (ab_tail, base_tail, ctail)):
            c0, c1 = coeff[pl.ds(0, 1), :], coeff[pl.ds(1, 1), :]
            c2, c3 = coeff[pl.ds(2, 1), :], coeff[pl.ds(3, 1), :]
            out[half, pl.ds(0, HALF), :] = (base[...] * (c0 + u * c1)).astype(bf16)
            out[half, pl.ds(HALF, HALF), :] = (base[...] * (c2 + u * c3)).astype(bf16)
        main = smeared[:, pl.ds(start, HALF), :].reshape(MAIN_K, SIDE)
        tail = smeared[:, pl.ds(start + HALF, TAIL), :].reshape(TAIL_K, SIDE)
        both = jnp.dot(ab_main[half], main, preferred_element_type=f32)
        both = both + jnp.dot(ab_tail[half], tail, preferred_element_type=f32)
        halves.append(both[:HALF] + v * both[HALF:])
    image = jnp.concatenate(halves, axis=0)

    tile_of = cols // BLOCK
    fx = jnp.zeros((1, SIDE), f32)
    fy = jnp.zeros((1, SIDE), f32)
    for q in range(TILES):
        shift = shift_ref[e, p * TILES + q]
        fx = jnp.where(tile_of == q, ((shift & 3).astype(f32) + 0.5) * 0.25, fx)
        fy = jnp.where(tile_of == q, ((shift >> 2).astype(f32) + 0.5) * 0.25, fy)
    inside = cols < SIDE - 1

    def along(x):
        return (1.0 - fx) * x + fx * jnp.where(inside, pltpu.roll(x, SIDE - 1, 1), 0.0)

    mixed = along(image)
    below_row = along(carry[...])[:1]
    last = row_of((BLOCK, 1)) == BLOCK - 1
    below = jnp.where(last, below_row, pltpu.roll(mixed, BLOCK - 1, 0))
    result = (1.0 - fy) * mixed + fy * below
    carry[...] = image[:8]
    shifted_ref[0] = result
    first_block = e * 16 + p * TILES
    for q in range(TILES):
        cells[q] = result[:, q * BLOCK : (q + 1) * BLOCK]
        for g in range(GROUP):
            send_ref[g, first_block + q] = cells[q, every(g), :].astype(bf16)


def conv_send(owners, columns, shifts, weight, cutouts, vert, horiz, coeffs):
    def by_exposure(*shape):
        return pl.BlockSpec((1,) + shape, lambda e, s, *_: (e,) + (0,) * len(shape))

    return pl.pallas_call(
        conv_kernel,
        out_shape=(
            pltpu.HBM((2, SIDE, SIDE), f32),
            jax.ShapeDtypeStruct((GROUP, 33, SLICE, BLOCK), bf16),
        ),
        grid_spec=pltpu.PrefetchScalarGridSpec(
            num_scalar_prefetch=4,
            grid=(2, TILES),
            in_specs=[
                by_exposure(SIDE, SIDE),
                by_exposure(KERNELS, TAPS),
                by_exposure(KERNELS, TAPS),
                by_exposure(4, KERNELS),
            ],
            out_specs=[
                pl.BlockSpec((1, BLOCK, SIDE), lambda e, s, *_: (e, TILES - 1 - s, 0)),
                pl.BlockSpec((GROUP, 33, SLICE, BLOCK), lambda e, s, *_: (0, 0, 0, 0)),
            ],
            scratch_shapes=[
                pltpu.VMEM((PAD_ROWS, PAD_COLS), bf16),
                pltpu.VMEM((TILES * PAD_ROWS, 256), bf16),
                pltpu.VMEM((256, WIDE_K), bf16),
                pltpu.VMEM((HALF, MAIN_K), f32),
                pltpu.VMEM((HALF, TAIL_K), f32),
                pltpu.VMEM((4, MAIN_K), f32),
                pltpu.VMEM((4, TAIL_K), f32),
                pltpu.VMEM((2, BLOCK, MAIN_K), bf16),
                pltpu.VMEM((2, BLOCK, TAIL_K), bf16),
                pltpu.VMEM((KERNELS, PAD_ROWS, SIDE), bf16),
                pltpu.VMEM((8, SIDE), f32),
                pltpu.VMEM((TILES, BLOCK, BLOCK), f32),
            ],
        ),
        compiler_params=pltpu.CompilerParams(vmem_limit_bytes=48 * MIB),
        name="conv_send",
    )(*(
        pltpu.with_memory_space_constraint(x, pltpu.HBM)
        for x in (owners, columns, shifts, weight, cutouts, vert, horiz, coeffs)
    ))


def whole(*shape):
    return pl.BlockSpec(shape, lambda i, *_: (0,) * len(shape))


def combine_kernel(
    side_ref, got_ref, out_ref, target_ref, even, odd, weights, target_s, weight_s, sems
):
    lanes = lane_of((SLICE, BLOCK))
    owner_rows = row_of((BLOCK, BLOCK)).astype(f32)
    column_rows = row_of((8, BLOCK)).astype(f32)
    totals = jnp.zeros((8, BLOCK), f32)
    for r in range(8):
        note = got_ref[4 * r, 32].astype(f32)
        for i in range(1, 4):
            moved = pltpu.roll(got_ref[4 * r + i, 32].astype(f32), 32 * i, 1)
            note = jnp.where(lanes < 32 * i, note, moved)
        owner, column, weight = note[0:1], note[1:2], note[2:3]
        target_ref[pl.ds(r, 1), :] = (owner * PW + column).astype(jnp.int32)
        weights[pl.ds(r, 1), :] = weight
        onto = (owner_rows == owner).astype(bf16)
        placed = jnp.where(column_rows == column, weight, 0.0).astype(bf16)
        totals = totals + lax.dot_general(
            placed, onto, (((1,), (1,)), ((), ())), preferred_element_type=f32
        )
    copies = (
        pltpu.make_async_copy(target_ref, target_s, sems.at[0]),
        pltpu.make_async_copy(weights, weight_s, sems.at[1]),
    )
    for copy in copies:
        copy.start()
    even[...] = jnp.zeros_like(even)
    odd[...] = jnp.zeros_like(odd)
    for copy in copies:
        copy.wait()
    inner = tuple(acc.at[pl.ds(PW, 128 * PW)] for acc in (even, odd))

    @pl.loop(0, 8)
    def _(line):
        for i in range(BLOCK):
            acc, spot, w = inner[i % 2], target_s[line, i], weight_s[line, i]
            block = got_ref[line * 4 + i // 32, i % 32]
            acc[spot] = acc[spot] + w * block.astype(f32)

    feet = side_ref[0] >= HALO
    carries_table = (side_ref[0] >= REACH) & (side_ref[0] < GROUP - REACH)
    high = totals.astype(bf16).astype(f32)
    table = jnp.where(feet, totals - high, high)[:SLICE]

    @pl.loop(0, 128 // 8)
    def _(turn):
        for i in range(8):
            owner = turn * 8 + i
            for j in range(PW):
                spot = (owner + 1) * PW + j
                out_ref[owner, j] = (even[spot] + odd[spot]).astype(bf16)
            beside = pl.ds(owner * PW + jnp.where(feet, 0, 2 * PW), PW)
            foot = even[beside, SLICE - 1, :] + odd[beside, SLICE - 1, :]
            head = even[beside, 0, :] + odd[beside, 0, :]
            halo = jnp.where(feet, foot, head)
            out_ref[owner, PW] = jnp.where(carries_table, table, halo).astype(bf16)


def combine(side, got):
    return pl.pallas_call(
        combine_kernel,
        out_shape=(
            jax.ShapeDtypeStruct((128, TILES_OUT, SLICE, BLOCK), bf16),
            jax.ShapeDtypeStruct((8, BLOCK), jnp.int32),
        ),
        grid_spec=pltpu.PrefetchScalarGridSpec(
            num_scalar_prefetch=1,
            grid=(1,),
            in_specs=[whole(GROUP, 33, SLICE, BLOCK)],
            out_specs=[whole(128, TILES_OUT, SLICE, BLOCK), whole(8, BLOCK)],
            scratch_shapes=[pltpu.VMEM((130 * PW, SLICE, BLOCK), f32)] * 2
            + [
                pltpu.VMEM((8, BLOCK), f32),
                pltpu.SMEM((8, BLOCK), jnp.int32),
                pltpu.SMEM((8, BLOCK), f32),
                pltpu.SemaphoreType.DMA((2,)),
            ],
        ),
        compiler_params=pltpu.CompilerParams(vmem_limit_bytes=24 * MIB),
        name="combine",
    )(side, got)


def summed(got_ref, g, j):
    total = got_ref[member(0, g), j].astype(f32)
    for group in range(1, GROUPS):
        total = total + got_ref[member(group, g), j].astype(f32)
    return total


WIDE = BLOCK + 2 * HALO


def starlet_kernel(
    level_ref, here_ref, got_ref,
    sky_ref, answer_ref, wide, cells,
):
    totals = summed(got_ref, REACH, PW) + summed(got_ref, GROUP // 2, PW)
    wide[pl.ds(0, 8), :] = jnp.zeros((8, SIDE), f32)
    wide[pl.ds(WIDE - 8, 8), :] = jnp.zeros((8, SIDE), f32)
    inverse = pltpu.roll(1.0 / (1.0 + totals), BLOCK - here_ref[0], 1)
    own, before, after = (
        [jnp.broadcast_to(inverse[j : j + 1, i : i + 1], (1, BLOCK)) for j in range(PW)]
        for i in (0, BLOCK - 1, 1)
    )
    for g in range(GROUP):
        halo = summed(got_ref, g, PW)
        for j in range(PW):
            cols = slice(j * BLOCK, (j + 1) * BLOCK)
            cells[j, every(g), :] = summed(got_ref, g, j) * own[j]
            if g < REACH:
                wide[pl.ds(HALO + BLOCK + g, 1), cols] = halo[j : j + 1] * after[j]
            elif g >= GROUP - REACH:
                wide[pl.ds(g - HALO, 1), cols] = halo[j : j + 1] * before[j]
    for j in range(PW):
        wide[pl.ds(HALO, BLOCK), j * BLOCK : (j + 1) * BLOCK] = cells[j]
    rows = lax.broadcasted_iota(jnp.int32, (WIDE, 1), 0)
    cols = lax.broadcasted_iota(jnp.int32, (1, SIDE), 1)
    above = (rows < HALO).astype(f32)
    under = (rows >= HALO + BLOCK).astype(f32)
    here = here_ref[0]
    starts = jnp.where(here == 0, 1.0, 0.0)
    ends = jnp.where(here == 127, 1.0, 0.0)
    inside = 1.0 - above * starts - under * ends
    tile_of = cols // BLOCK
    lims = []
    for strip in (jnp.maximum(here - 1, 0), here, jnp.minimum(here + 1, 127)):
        lim = jnp.zeros((1, SIDE), f32)
        for j in range(PW):
            lim = jnp.where(tile_of == j, level_ref[j, strip].astype(f32), lim)
        lims.append(lim)
    middle = (1.0 - above) - under
    lim = above * lims[0] + middle * lims[1] + under * lims[2]
    fine, coarse = fine_tau * lim, coarse_tau * lim

    def smooth(x, d):
        def up(y, n):
            return pltpu.roll(y, n % WIDE, 0)

        x = 0.375 * x + 0.25 * (up(x, d) + up(x, -d)) + 0.0625 * (up(x, 2 * d) + up(x, -2 * d))

        def side(y, n):
            keep = cols >= n if n > 0 else cols < SIDE + n
            return jnp.where(keep, pltpu.roll(y, n % SIDE, 1), 0.0)

        return (
            0.375 * x
            + 0.25 * (side(x, d) + side(x, -d))
            + 0.0625 * (side(x, 2 * d) + side(x, -2 * d))
        )

    def shrink(detail, limit):
        return detail - jnp.clip(detail, -limit, limit)

    x = wide[...]
    for _ in range(SWEEPS):
        x = x * inside
        one = smooth(x, 1) * inside
        two = smooth(one, 2)
        x = two + shrink(x - one, fine) + shrink(one - two, coarse)
    sky = x[HALO : HALO + BLOCK]
    sky_ref[...] = sky
    for j in range(PW):
        cells[j] = sky[:, j * BLOCK : (j + 1) * BLOCK]
        for g in range(GROUP):
            part = cells[j, every(g), :].astype(bf16)
            for group in range(GROUPS):
                answer_ref[member(group, g), j] = part


def starlet(levels, here, partial):
    return pl.pallas_call(
        starlet_kernel,
        out_shape=(
            jax.ShapeDtypeStruct((BLOCK, SIDE), f32),
            jax.ShapeDtypeStruct((128, PW, SLICE, BLOCK), bf16),
        ),
        grid_spec=pltpu.PrefetchScalarGridSpec(
            num_scalar_prefetch=2,
            grid=(1,),
            in_specs=[whole(128, TILES_OUT, SLICE, BLOCK)],
            out_specs=[whole(BLOCK, SIDE), whole(128, PW, SLICE, BLOCK)],
            scratch_shapes=[
                pltpu.VMEM((WIDE, SIDE), f32),
                pltpu.VMEM((PW, BLOCK, BLOCK), f32),
            ],
        ),
        compiler_params=pltpu.CompilerParams(vmem_limit_bytes=16 * MIB),
        name="starlet",
    )(pltpu.with_memory_space_constraint(levels, pltpu.HBM), here, partial)


def pick_kernel(target_ref, all_ref, out_ref):
    @pl.loop(0, 8)
    def _(line):
        for i in range(BLOCK):
            out_ref[line * 4 + i // 32, i % 32] = all_ref[target_ref[line, i]]


def pick(targets, templates):
    return pl.pallas_call(
        pick_kernel,
        out_shape=jax.ShapeDtypeStruct((GROUP, 32, SLICE, BLOCK), bf16),
        grid_spec=pltpu.PrefetchScalarGridSpec(
            num_scalar_prefetch=1,
            grid=(1,),
            in_specs=[whole(128 * PW, SLICE, BLOCK)],
            out_specs=whole(GROUP, 32, SLICE, BLOCK),
        ),
        compiler_params=pltpu.CompilerParams(vmem_limit_bytes=16 * MIB),
        name="pick",
    )(targets, templates.reshape(128 * PW, SLICE, BLOCK))


def difference_kernel(shifted_ref, template_ref, out_ref, cells):
    for block in range(2 * TILES):
        tile, q = block // TILES, block % TILES
        rows, cols = slice(tile * BLOCK, (tile + 1) * BLOCK), slice(q * BLOCK, (q + 1) * BLOCK)
        for g in range(GROUP):
            cells[block, every(g), :] = template_ref[g, block].astype(f32)
        out_ref[0, rows, cols] = shifted_ref[0, rows, cols] - cells[block]


def difference(shifted, returned):
    rows = pl.BlockSpec((1, 2 * BLOCK, SIDE), lambda e, p: (e, p, 0))
    return pl.pallas_call(
        difference_kernel,
        out_shape=jax.ShapeDtypeStruct((2, SIDE, SIDE), f32),
        grid=(2, 2),
        in_specs=[
            rows,
            pl.BlockSpec((GROUP, 2 * TILES, SLICE, BLOCK), lambda e, p: (0, e * 2 + p, 0, 0)),
        ],
        out_specs=rows,
        scratch_shapes=[pltpu.VMEM((2 * TILES, BLOCK, BLOCK), f32)],
        compiler_params=pltpu.CompilerParams(vmem_limit_bytes=16 * MIB),
        name="difference",
    )(shifted, returned)


def shards(
    cutouts, vert_taps, horiz_taps, field_coeffs, exposure_weight,
    dest_owner, dest_column, shift_index, threshold_level,
):
    here = lax.axis_index(AXES).reshape(1)
    side = lax.axis_index(NEAR).reshape(1)
    shifts, here, side = lax.optimization_barrier((shift_index, here, side))
    shifted, slices = conv_send(
        dest_owner.reshape(2, 16), dest_column, shifts, exposure_weight,
        cutouts, vert_taps, horiz_taps, field_coeffs,
    )
    got = lax.all_to_all(slices, NEAR, split_axis=0, concat_axis=0, tiled=True)
    sums, targets = combine(side, got)
    partial = lax.all_to_all(sums, AXES, split_axis=0, concat_axis=0, tiled=True)
    sky, answers = starlet(threshold_level.T, here, partial)
    templates = lax.all_to_all(answers, AXES, split_axis=0, concat_axis=0, tiled=True)
    picked = pick(targets, templates)
    returned = lax.all_to_all(picked, NEAR, split_axis=0, concat_axis=0, tiled=True)
    return sky, difference(shifted, returned)


def solution(mesh):
    split = jax.sharding.Mesh(mesh.devices.reshape((2,) * 7), AXES)
    placed = (
        P(AXES, None, None),
        P(AXES, None, None),
        P(AXES, None, None),
        P(AXES, None, None),
        P(AXES),
        P(AXES, None, None),
        P(AXES, None),
        P(AXES, None),
        P(),
    )
    return jax.shard_map(
        shards,
        mesh=split,
        in_specs=placed,
        out_specs=(P(AXES, None), P(AXES, None, None)),
        check_vma=False,
    )
```
